32 devices in a mesh: row: 2 (over y), circ: 4 (over x, core), span: 4 (over z).
Axes of the slice: x: 2, y: 2, z: 4, core: 2. Of those that a mesh axis runs over, the one named last changes fastest.
Arguments:
- density: float32 [2, 32, 64, 256], P('row', 'circ', 'span'), may hold values from 0.6 to 1.6
- velocity: float32 [2, 3, 32, 64, 256], P('row', None, 'circ', 'span'), may hold values from -1.2 to 1.2
- pressure: float32 [2, 32, 64, 256], P('row', 'circ', 'span'), may hold values from 0.6 to 1.6
- blade_force: float32 [2, 3, 32, 64, 256], P('row', None, 'circ', 'span'), may hold values from -4 to 4
- offsets: int32 [2], replicated, may hold values from 0 to 31
- weights: float32 [2, 4], replicated, may hold values from 0.1 to 1
Outputs:
- state: float32 [2, 5, 32, 64, 256], P('row', None, 'circ', 'span')
- plane_flux: float32 [2, 2, 5, 32, 64], P('row', None, None, 'circ', 'span')
The draws below stay inside these ranges and needn't reach their ends.
All inputs are finite; a program needn't handle non-finite values.
Results may differ from the reference program's by a relative error of at most 0.0003.
Values sent between devices are 32-bit elements; how exact they have to be, the bound alone decides.
No kernel may reach another device: no remote copies, remote signals or barrier semaphores. Data moves between devices by JAX's collectives and lax.ppermute only.
A program may use at most 64 MiB of HBM per device.

```python
import math
import jax
import jax.numpy as jnp
from jax import lax

C_DEV = 8
NA = 256
STEPS = 2
NC = 32
NS = 64


def shard_levels(own_key, dims, shards, least, largest):
    def one(position, parts):
        heights = jax.random.uniform(jax.random.fold_in(jax.random.fold_in(own_key, 6), position), (parts,), jnp.float32, least / len(shards), largest / len(shards))
        return jnp.repeat(jnp.exp(heights), dims[position] // parts).reshape((-1,) + (1,) * (len(dims) - position - 1))

    loudness = one(*shards[0])
    for cut in shards[1:]:
        loudness = loudness * one(*cut)
    return loudness


def scatter_about(stream_key, extent, scale, most, pieces=(), kind=jnp.bfloat16):
    loudness = shard_levels(stream_key, extent, pieces, -0.22, 0.18) if pieces else 1.0
    result = jax.random.normal(stream_key, extent, jnp.float32) * scale * loudness
    return jnp.minimum(jnp.maximum(result, -most), most).astype(kind)


def setup_inputs(seed: int = 0) -> dict:
    keys = jax.random.split(jax.random.key(seed), 7)
    density = jnp.clip(jnp.exp(math.log(1.6) - 0.98082923 * jax.random.uniform(keys[0], (2, NC, NS, NA), jnp.float32) ** shard_levels(keys[0], (2, NC, NS, NA), ((0, 2), (1, 4), (2, 4)), -0.2, 0.2)), 0.6, 1.6)
    velocity = scatter_about(keys[1], (2, 3, NC, NS, NA), 0.3, 1.2, ((0, 2), (2, 4), (3, 4)), jnp.float32)
    pressure = jnp.clip(jnp.exp(math.log(1.6) - 0.98082923 * jax.random.uniform(keys[2], (2, NC, NS, NA), jnp.float32) ** shard_levels(keys[2], (2, NC, NS, NA), ((0, 2), (1, 4), (2, 4)), -0.2, 0.2)), 0.6, 1.6)
    blade_force = scatter_about(keys[3], (2, 3, NC, NS, NA), 1.0, 4.0, ((0, 2), (2, 4), (3, 4)), jnp.float32)
    offsets = jax.random.randint(keys[4], (STEPS,), 0, NC).astype(jnp.int32)
    weights = jnp.clip(jax.random.uniform(keys[5], (STEPS, 4), jnp.float32, 0.1, 1.0), 0.1, 1.0)
    return {"density": density, "velocity": velocity, "pressure": pressure, "blade_force": blade_force, "offsets": offsets, "weights": weights}


HEAT_RATIO = 1.4
TIME_STEP = 0.04

def direction_flux(cells, direction):
    density_here = cells[0]
    momentum = cells[1:4]
    energy = cells[4]
    kinetic = 0.5 * (momentum[0] * momentum[0] + momentum[1] * momentum[1] + momentum[2] * momentum[2]) / density_here
    pressure_now = (HEAT_RATIO - 1.0) * (energy - kinetic)
    normal = momentum[direction] / density_here
    components = [momentum[direction], momentum[0] * normal, momentum[1] * normal, momentum[2] * normal, (energy + pressure_now) * normal]
    components[1 + direction] = components[1 + direction] + pressure_now
    wave_speed = jnp.abs(normal) + jnp.sqrt(HEAT_RATIO * pressure_now / density_here)
    return (jnp.stack(components), wave_speed)

def face_flux(left_state, right_state, direction):
    left_flux, left_speed = direction_flux(left_state, direction)
    right_flux, right_speed = direction_flux(right_state, direction)
    top_speed = jnp.maximum(left_speed, right_speed)
    return 0.5 * (left_flux + right_flux) - 0.5 * top_speed * (right_state - left_state)

def region_step(padded, force, lower_ghost, upper_ghost):
    region = padded[:, 1:-1, 1:-1]
    circ_flux = face_flux(padded[:, :-1, 1:-1], padded[:, 1:, 1:-1], 1)
    span_flux = face_flux(padded[:, 1:-1, :-1], padded[:, 1:-1, 1:], 2)
    axial_row = jnp.concatenate([lower_ghost, region, upper_ghost], 3)
    axial_flux = face_flux(axial_row[..., :-1], axial_row[..., 1:], 0)
    divergence = axial_flux[..., 1:] - axial_flux[..., :-1] + (circ_flux[:, 1:] - circ_flux[:, :-1]) + (span_flux[:, :, 1:] - span_flux[:, :, :-1])
    source = jnp.stack([jnp.zeros_like(region[0]), region[0] * force[0], region[0] * force[1], region[0] * force[2], lax.optimization_barrier(jnp.sum(region[1:4] * force, axis=0))])
    updated = region - TIME_STEP * divergence + TIME_STEP * source
    return (updated, axial_flux[..., 0], axial_flux[..., -1])

def conserved(density_row, velocity_row, pressure_row):
    momentum = density_row[None] * velocity_row
    energy = pressure_row / (HEAT_RATIO - 1.0) + 0.5 * density_row * lax.optimization_barrier(jnp.sum(velocity_row * velocity_row, axis=0))
    return jnp.concatenate([density_row[None], momentum, energy[None]], 0)

def mirror_sign():
    return jnp.array([1.0, 1.0, 1.0, -1.0, 1.0], jnp.float32).reshape(5, 1, 1, 1)

def advance_row(cells, force, lower_ghost, upper_ghost, row_index):
    flip_sign = mirror_sign()
    wrapped = jnp.concatenate([cells[:, -1:], cells, cells[:, :1]], 1)
    padded = jnp.concatenate([wrapped[:, :, :1] * flip_sign, wrapped, wrapped[:, :, -1:] * flip_sign], 2)
    block_count = NC // C_DEV

    def one_block(block_index):
        start = (block_index * C_DEV).astype(jnp.int32)
        piece = lax.dynamic_slice_in_dim(padded, start, C_DEV + 2, 1)
        force_piece = lax.dynamic_slice_in_dim(force, start, C_DEV, 1)
        lower_piece = lax.dynamic_slice_in_dim(lower_ghost, start, C_DEV, 1)
        upper_piece = lax.dynamic_slice_in_dim(upper_ghost, start, C_DEV, 1)
        updated, first_face, last_face = region_step(piece, force_piece, lower_piece, upper_piece)
        plane = last_face if row_index == 0 else first_face
        return (updated, plane)
    blocks, planes = lax.map(one_block, jnp.arange(block_count, dtype=jnp.int32))
    updated = jnp.moveaxis(blocks, 0, 1).reshape(5, NC, NS, NA)
    plane = jnp.moveaxis(planes, 0, 1).reshape(5, NC, NS)
    return (updated, plane)

def reference(density, velocity, pressure, blade_force, offsets, weights):
    states = [conserved(density[0], velocity[0], pressure[0]), conserved(density[1], velocity[1], pressure[1])]
    tap_weights = weights / lax.optimization_barrier(jnp.sum(weights, axis=1, keepdims=True))
    inlet = jnp.array([1.0, 0.5, 0.0, 0.0, 2.625], jnp.float32).reshape(5, 1, 1, 1)
    planes = [[], []]
    for step_index in range(STEPS):
        turn = offsets[step_index].astype(jnp.int32)
        shifts = [turn, (NC - turn) % NC]
        donors = [states[1][..., 0], states[0][..., -1]]
        updated_rows = []
        for row_index in range(2):
            cells = states[row_index]
            ghost_layer = jnp.zeros_like(donors[row_index])
            for tap_index in range(4):
                ghost_layer = ghost_layer + tap_weights[step_index, tap_index] * jnp.roll(donors[row_index], -(shifts[row_index] + tap_index - 1), axis=1)
            ghost_layer = ghost_layer[..., None]
            if row_index == 0:
                lower_ghost = jnp.broadcast_to(inlet, ghost_layer.shape)
                upper_ghost = ghost_layer
            else:
                lower_ghost = ghost_layer
                upper_ghost = cells[..., -1:]
            updated, plane = advance_row(cells, blade_force[row_index], lower_ghost, upper_ghost, row_index)
            updated_rows.append(updated)
            planes[row_index].append(plane)
        states = updated_rows
    state = jnp.stack(states)
    plane_flux = jnp.stack([jnp.stack(planes[0]), jnp.stack(planes[1])])
    return (state, plane_flux)
```

```python
import functools

import jax
import jax.numpy as jnp
from jax import lax
from jax.experimental import pallas as pl
from jax.experimental.pallas import tpu as pltpu
from jax.sharding import PartitionSpec as P

GAMMA = 1.4
STEP = 0.04
INLET = (1.0, 0.5, 0.0, 0.0, 2.625)
LANES = 128
ROWS = 24


def vmem():
    return pl.BlockSpec(memory_space=pltpu.VMEM)


def smem():
    return pl.BlockSpec(memory_space=pltpu.SMEM)


def call(kernel, shapes, args, specs=None, scratch=(), aliases=None, cost=None):
    return pl.pallas_call(
        kernel,
        out_shape=[jax.ShapeDtypeStruct(s, jnp.float32) for s in shapes],
        in_specs=specs or [vmem()] * len(args),
        out_specs=[vmem()] * len(shapes),
        scratch_shapes=list(scratch),
        input_output_aliases=aliases or {},
        cost_estimate=cost,
    )(*args)


class Cell:
    def __init__(self, u):
        self.u = u
        rho, m0, m1, m2, en = u
        self.inv = 1.0 / rho
        kin = 0.5 * (m0 * m0 + m1 * m1 + m2 * m2) * self.inv
        self.p = (GAMMA - 1.0) * (en - kin)
        self.sound = jnp.sqrt(GAMMA * self.p * self.inv)

    def flux(self, d):
        m = self.u[1:4]
        vel = m[d] * self.inv
        f = [m[d], m[0] * vel, m[1] * vel, m[2] * vel, (self.u[4] + self.p) * vel]
        f[1 + d] = f[1 + d] + self.p
        return f, jnp.abs(vel) + self.sound


def face(ul, fl, sl, ur, fr, sr):
    top = jnp.maximum(sl, sr)
    return [a + b - top * (y - x) for x, a, y, b in zip(ul, fl, ur, fr)]


def updated(u, force, *spans):
    src = [None, u[0] * force[0], u[0] * force[1], u[0] * force[2]]
    src.append(u[1] * force[0] + u[2] * force[1] + u[3] * force[2])
    out = []
    for k in range(5):
        div = spans[0][0][k] - spans[0][1][k]
        for hi, lo in spans[1:]:
            div = div + (hi[k] - lo[k])
        new = u[k] - (0.5 * STEP) * div
        out.append(new if src[k] is None else new + STEP * src[k])
    return out


def conserved(rho, v, p):
    m = [rho * x for x in v]
    en = p / (GAMMA - 1.0) + 0.5 * rho * (v[0] * v[0] + v[1] * v[1] + v[2] * v[2])
    return [rho] + m + [en]


def inlet_flux():
    rho, m0, m1, m2, en = INLET
    p = (GAMMA - 1.0) * (en - 0.5 * (m0 * m0 + m1 * m1 + m2 * m2) / rho)
    vel = m0 / rho
    f = [m0, m0 * vel + p, m1 * vel, m2 * vel, (en + p) * vel]
    return f, abs(vel) + (GAMMA * p / rho) ** 0.5


def axial_faces(cell, slide, rotor):
    u = cell.u
    f, s = cell.flux(0)
    shape = u[0].shape
    lane = lax.broadcasted_iota(jnp.int32, shape, 1)
    last = shape[1] - 1
    first_lane = lane == 0
    last_lane = lane == last
    inf, ins = inlet_flux()

    def back(x, v):
        return jnp.where(first_lane, v, pltpu.roll(x, 1, 1))

    pu = [back(x, v) for x, v in zip(u, INLET)]
    pf = [pu[1]] + [back(x, v) for x, v in zip(f[1:], inf[1:])]
    lo = face(pu, pf, back(s, ins), u, f, s)
    stator_first = jnp.logical_and(first_lane, jnp.logical_not(rotor))
    lo = [jnp.where(stator_first, h, x) for h, x in zip(slide, lo)]
    hi = [
        jnp.where(last_lane, jnp.where(rotor, h, 2.0 * g), pltpu.roll(x, last, 1))
        for h, g, x in zip(slide, f, lo)
    ]
    return hi, lo


def wall_face(f, s, m, sign):
    zero = jnp.zeros_like(s)
    return [zero, zero, zero, 2.0 * (f[3] + sign * s * m), zero]


def place():
    row = lax.axis_index("row")
    circ = lax.axis_index("circ")
    span = lax.axis_index("span")
    return row, lax.rem(circ, 2) == 0, lax.rem(span, 2) == 0, span


def first_kernel(C, T, rho_ref, v_ref, p_ref, f_ref, u_ref, sa_ref, sb_ref, pa_ref, pb_ref):
    _, even_c, even_s, _ = place()
    for c in range(C):
        u = conserved(rho_ref[c], [v_ref[k, c] for k in range(3)], p_ref[c])
        for k in range(5):
            u_ref[k, c] = u[k]

    def row(k, s):
        ref = u_ref.at[k] if k < 5 else f_ref.at[k - 5]
        return ref[:, s, :]

    def send(slot, k, low, high):
        a, b = row(k, low), row(k, high)
        sa_ref[slot] = jnp.where(even_s, b, a)
        sb_ref[slot] = jnp.where(even_s, a, b)

    for k in range(5):
        send(k, k, 0, T - 1)
        send(5 + k, k, 1, T - 2)
    for k in range(3):
        send(10 + k, 5 + k, 0, T - 1)
    near = jnp.where(even_c, C - 1, 0)
    far = jnp.where(even_c, C - 2, 1)
    for ref, n, m in ((pa_ref, near, far), (pb_ref, C - 1 - near, C - 1 - far)):
        for k in range(5):
            ref[k] = u_ref[k, n]
            ref[5 + k] = u_ref[k, m]
        for k in range(3):
            ref[10 + k] = f_ref[k, n]


def thin_kernel(C, T, u_ref, f_ref, ha_ref, hb_ref, m1_ref, m2_ref, t_ref):
    row, even_c, even_s, _ = place()
    rotor = row == 0
    width = u_ref.shape[3]
    half = pl.ds(pl.multiple_of(jnp.where(rotor, width - LANES, 0), LANES), LANES)
    end = jnp.where(rotor, LANES - 1, 0)
    second = jnp.where(rotor, LANES - 2, 1)
    lane = lax.broadcasted_iota(jnp.int32, (C * T, LANES), 1)
    t = jnp.zeros((C * T, LANES), jnp.float32)

    def put(x, j, e):
        return pltpu.roll(x, lax.rem(j - e + LANES, LANES), 1)

    for k in range(5):
        x = u_ref[k, :, :, half].reshape(C * T, LANES)
        t = jnp.where(lane == k, put(x, k, end), t)
        t = jnp.where(lane == 5 + k, put(x, 5 + k, second), t)
    for k in range(3):
        t = jnp.where(lane == 10 + k, put(f_ref[k, :, :, half].reshape(C * T, LANES), 10 + k, end), t)
    t_ref[...] = t
    small = lax.broadcasted_iota(jnp.int32, (C, LANES), 1)
    for start, is_low in ((0, True), (T - 1, False)):
        where_a = even_s if not is_low else jnp.logical_not(even_s)
        rows = pl.ds(start, C, stride=T)
        x = t_ref[rows, :]
        for k in range(5):
            h = jnp.where(where_a, ha_ref[k, :, half], hb_ref[k, :, half])
            x = jnp.where(small == 13 + k, put(h, 13 + k, end), x)
        t_ref[rows, :] = x
    planes = t_ref[...].T[:ROWS]
    m1_ref[0:ROWS, :] = planes
    m2_ref[0:ROWS, :] = planes
    m2_ref[ROWS : 2 * ROWS, :] = jnp.zeros((ROWS, LANES), jnp.float32)

    def corner(ref, base, c):
        for k in range(5):
            for side in range(2):
                where_a = even_s if side == 1 else jnp.logical_not(even_s)
                x = jnp.where(where_a, ha_ref[k, pl.ds(c, 1), :], hb_ref[k, pl.ds(c, 1), :])
                for part in range(width // LANES):
                    r = base + 16 * part + 2 * k + side
                    ref[r : r + 1, :] = x[:, part * LANES : (part + 1) * LANES]
        for part in range(width // LANES):
            r = base + 16 * part
            ref[r + 10 : r + 16, :] = jnp.zeros((6, LANES), jnp.float32)

    near = jnp.where(even_c, C - 1, 0)
    corner(m1_ref, ROWS, near)
    corner(m2_ref, 2 * ROWS, C - 1 - near)


def fill_kernel(m1_ref, m2_ref, out_ref):
    out_ref[...] = m2_ref[...]
    out_ref[ROWS : 2 * ROWS, :] = m1_ref[0:ROWS, :]


def ring_kernel(m2_ref, got_ref, ring_ref):
    _, even, _, _ = place()
    mate = m2_ref[ROWS : 2 * ROWS, :]
    next_ = got_ref[0:ROWS, :]
    ring_ref[0] = m2_ref[0:ROWS, :]
    ring_ref[1] = jnp.where(even, mate, next_)
    ring_ref[2] = got_ref[ROWS : 2 * ROWS, :]
    ring_ref[3] = jnp.where(even, next_, mate)


def final_kernel(
    C, T, nc, ns,
    off_ref, wt_ref, u_ref, f_ref, ha_ref, hb_ref, pa_ref, pb_ref, m1_ref, m2_ref, own_ref, par_ref,
    out_ref, pf_ref,
    own_s, par_s, ht_s, ext_s, one_s, far_s, edge_s, rows_s,
):
    row, even_c, even_s, span = place()
    rotor = row == 0
    hub = span == 0
    casing = span == ns - 1
    width = u_ref.shape[3]
    periods = own_s.shape[0] // (nc * ROWS)
    depth = nc * periods
    sg = jnp.where(rotor, 1, -1)
    sgf = jnp.where(rotor, 1.0, -1.0)
    cycle = nc * C

    for copy in range(periods):
        own_s[copy * nc * ROWS : (copy + 1) * nc * ROWS, :] = own_ref[...]
        par_s[copy * nc * ROWS : (copy + 1) * nc * ROWS, :] = par_ref[...]
    shape = (depth, LANES)
    lane = lax.broadcasted_iota(jnp.int32, shape, 1)
    in_span = lax.rem(lane, T)

    def get(ref, j):
        return ref[pl.ds(j, depth, stride=ROWS), :]

    def ahead(x, k):
        if k == 0:
            return x
        a = pltpu.roll(x, (LANES - T * k) % LANES, 1)
        b = pltpu.roll(a, depth - 1, 0)
        return jnp.where(lane < LANES - T * k, a, b)

    def behind(x):
        a = pltpu.roll(x, T, 1)
        b = pltpu.roll(a, 1, 0)
        return jnp.where(lane >= T, a, b)

    def turned(x, cells):
        q = lax.div(cells, C)
        r = lax.rem(cells, C)
        y = pltpu.roll(x, lax.rem(depth - q, depth), 0)
        a = pltpu.roll(y, lax.rem(LANES - T * r, LANES), 1)
        b = pltpu.roll(a, depth - 1, 0)
        return jnp.where(lane < LANES - T * r, a, b)

    def taps(t):
        w = [jnp.full((1, LANES), wt_ref[t, k], jnp.float32) for k in range(4)]
        total = w[0] + w[1] + w[2] + w[3]
        return [x / total for x in w]

    def ghosts(xs, t, sign):
        w = taps(t)
        start = lax.rem(sign * off_ref[t] - 1 + 2 * cycle, cycle)
        out = []
        for x in xs:
            x = turned(x, start)
            g = w[0] * x
            for k in range(1, 4):
                g = g + w[k] * ahead(x, k)
            out.append(g)
        return out

    def slide(cell, ghost, sign):
        f, s = cell.flux(0)
        g = Cell(ghost)
        fg, s_g = g.flux(0)
        top = jnp.maximum(s, s_g) * sign
        return [a + b - top * (y - x) for x, a, y, b in zip(cell.u, f, ghost, fg)]

    def ring_step(ref, cell, h, sign):
        inner = Cell([get(ref, 5 + k) for k in range(5)])
        fi, si = inner.flux(0)
        f, s = cell.flux(0)
        top = jnp.maximum(s, si) * sign
        h1 = [a + b - top * (x - y) for x, a, y, b in zip(cell.u, f, inner.u, fi)]
        ax_hi = [sign * x for x in h]
        ax_lo = [sign * x for x in h1]
        f, s = cell.flux(1)
        lo = face([behind(x) for x in cell.u], [behind(x) for x in f], behind(s), cell.u, f, s)
        hi = [ahead(x, 1) for x in lo]
        f, s = cell.flux(2)
        edge = Cell([get(ref, 13 + k) for k in range(5)])
        fe, se = edge.flux(2)
        first = in_span == 0
        last = in_span == T - 1

        def prev(x, e):
            return jnp.where(first, e, pltpu.roll(x, 1, 1))

        slo = face([prev(x, e) for x, e in zip(cell.u, edge.u)], [prev(x, e) for x, e in zip(f, fe)], prev(s, se), cell.u, f, s)
        wall = wall_face(f, s, cell.u[3], -1.0)
        slo = [jnp.where(jnp.logical_and(first, hub), a, b) for a, b in zip(wall, slo)]
        top_face = face(cell.u, f, s, edge.u, fe, se)
        wall = wall_face(f, s, cell.u[3], 1.0)
        top_face = [jnp.where(casing, a, b) for a, b in zip(wall, top_face)]
        shi = [jnp.where(last, a, pltpu.roll(b, LANES - 1, 1)) for a, b in zip(top_face, slo)]
        force = [get(ref, 10 + k) for k in range(3)]
        return updated(cell.u, force, (ax_hi, ax_lo), (hi, lo), (shi, slo))

    own = Cell([get(own_s, k) for k in range(5)])
    par = Cell([get(par_s, k) for k in range(5)])
    g_own = ghosts(par.u, 0, sg)
    g_par = ghosts(own.u, 0, -sg)
    h_own = slide(own, g_own, sgf)
    h_par = slide(par, g_par, -sgf)
    g_edge = ghosts([get(par_s, 13 + k) for k in range(5)], 0, sg)
    h_edge = slide(Cell([get(own_s, 13 + k) for k in range(5)]), g_edge, sgf)
    own_new = ring_step(own_s, own, h_own, sgf)
    par_new = ring_step(par_s, par, h_par, -sgf)
    h_next = slide(Cell(own_new), ghosts(par_new, 1, sg), sgf)

    def eight(x):
        if depth == 8:
            return x
        return jnp.concatenate([x[0:7], x[depth - 1 : depth]], 0)

    tile = [eight(x) for x in h_own + h_edge + h_next]
    tile.append(jnp.zeros((8, LANES), jnp.float32))
    ht_s[...] = jnp.concatenate(tile, 0).T
    for t, h in ((0, h_own), (1, h_next)):
        for k in range(5):
            x = 0.5 * h[k][0:1, :]
            for c in range(C):
                pf_ref[t, k, c : c + 1, :] = x[:, c * T : (c + 1) * T]

    def left(slot, rows=slice(None)):
        return jnp.where(even_c, pb_ref[slot, rows, :], pa_ref[slot, rows, :])

    def right(slot, rows=slice(None)):
        return jnp.where(even_c, pa_ref[slot, rows, :], pb_ref[slot, rows, :])

    def low(slot):
        return jnp.where(even_s, hb_ref[slot], ha_ref[slot])

    def high(slot):
        return jnp.where(even_s, ha_ref[slot], hb_ref[slot])

    def corner(ref, base, k, side):
        parts = [ref[pl.ds(base + 16 * q + 2 * k + side, 1), :] for q in range(width // LANES)]
        return jnp.concatenate(parts, 1)

    def corners(k, side):
        a = corner(m1_ref, ROWS, k, side)
        b = corner(m2_ref, 2 * ROWS, k, side)
        return jnp.where(even_c, b, a), jnp.where(even_c, a, b)

    eight_rows = lax.broadcasted_iota(jnp.int32, (C, width), 0)

    def extend(mid, lf, rt):
        shape = (C, width)
        tail = jnp.where(eight_rows == 0, jnp.broadcast_to(rt, shape), jnp.broadcast_to(lf, shape))
        return jnp.concatenate([mid, tail], 0)

    def own_row(k, s):
        mid = u_ref[k, :, s, :]
        return extend(mid, left(k, pl.ds(s, 1)), right(k, pl.ds(s, 1)))

    for side in range(2):
        halo = low if side == 0 else high
        inner = Cell([own_row(k, 0 if side == 0 else T - 1) for k in range(5)])
        lf_rt = [corners(k, side) for k in range(5)]
        cell = Cell([extend(halo(k), *lf_rt[k]) for k in range(5)])
        outer = Cell([halo(5 + k) for k in range(5)])
        f, s = cell.flux(2)
        fi, si = inner.flux(2)
        fo, so = outer.flux(2)
        cut = lambda xs: [x[:C] for x in xs]
        if side == 0:
            near = face(cell.u, f, s, inner.u, fi, si)
            hi2, lo2 = near, face(outer.u, fo, so, cut(cell.u), cut(f), s[:C])
            wall = wall_face(fi, si, inner.u[3], -1.0)
            at_wall = hub
        else:
            near = face(inner.u, fi, si, cell.u, f, s)
            hi2, lo2 = face(cut(cell.u), cut(f), s[:C], outer.u, fo, so), near
            wall = wall_face(fi, si, inner.u[3], 1.0)
            at_wall = casing
        for k in range(5):
            edge_s[side, k] = jnp.where(at_wall, wall[k], near[k])
        f, s = cell.flux(1)
        back = lambda x: pltpu.roll(x, 1, 0)
        lo1 = face([back(x) for x in cell.u], [back(x) for x in f], back(s), cell.u, f, s)
        hi1 = [pltpu.roll(x, 2 * C - 1, 0) for x in lo1]
        mid = Cell(cut(cell.u))
        first = 0 if side == 0 else T - 1
        strip = ht_s[pl.ds(first, C, stride=T), :]
        hs = [strip[:, 40 + 8 * k : 41 + 8 * k] for k in range(5)]
        hi0, lo0 = axial_faces(mid, hs, rotor)
        force = [halo(10 + k) for k in range(3)]
        new = updated(mid.u, force, (hi0, lo0), (cut(hi1), cut(lo1)), (cut(hi2), cut(lo2)))
        for k in range(5):
            rows_s[side, k] = new[k]

    column = (T, width)
    srow = lax.broadcasted_iota(jnp.int32, column, 0)

    def column_update(cell, circ_lo, circ_hi, slide_h, edge_row, force):
        hi0, lo0 = axial_faces(cell, slide_h, rotor)
        f, s = cell.flux(2)
        back = lambda x: pltpu.roll(x, 1, 0)
        lo2 = face([back(x) for x in cell.u], [back(x) for x in f], back(s), cell.u, f, s)
        low_row = [edge_s[0, k, edge_row : edge_row + 1, :] for k in range(5)]
        top_row = [edge_s[1, k, edge_row : edge_row + 1, :] for k in range(5)]
        lo2 = [jnp.where(srow == 0, jnp.broadcast_to(e, column), x) for e, x in zip(low_row, lo2)]
        hi2 = [
            jnp.where(srow == T - 1, jnp.broadcast_to(e, column), pltpu.roll(x, T - 1, 0))
            for e, x in zip(top_row, lo2)
        ]
        return updated(cell.u, force, (hi0, lo0), (circ_hi, circ_lo), (hi2, lo2))

    def sweep(load, lo, hi, slide_of, force_of, store):
        prev = Cell(load(lo - 1))
        pf, ps = prev.flux(1)
        cell = Cell(load(lo))
        cf, cs = cell.flux(1)
        h_lo = face(prev.u, pf, ps, cell.u, cf, cs)
        for c in range(lo, hi):
            nxt = Cell(load(c + 1))
            nf, ns_ = nxt.flux(1)
            h_hi = face(cell.u, cf, cs, nxt.u, nf, ns_)
            edge_row = c if c >= 0 else 2 * C - 1
            store(c, column_update(cell, h_lo, h_hi, slide_of(c), edge_row, force_of(c)))
            cell, cf, cs, h_lo = nxt, nf, ns_, h_hi

    def load0(c):
        if c < 0:
            return [left(k + (5 if c == -2 else 0)) for k in range(5)]
        if c >= C:
            return [right(k + (5 if c == C + 1 else 0)) for k in range(5)]
        return [u_ref[k, c] for k in range(5)]

    def force0(c):
        if c < 0:
            return [left(10 + k) for k in range(3)]
        if c >= C:
            return [right(10 + k) for k in range(3)]
        return [f_ref[k, c] for k in range(3)]

    def slide0(c):
        sector = 0 if 0 <= c < C else (1 if c >= C else 7)
        r = (c % C) * T
        return [ht_s[r : r + T, 8 * k + sector : 8 * k + sector + 1] for k in range(5)]

    def store0(c, u):
        for k in range(5):
            one_s[k, c + 1] = u[k]

    sweep(load0, -1, C + 1, slide0, force0, store0)

    for side in range(2):
        s = 0 if side == 0 else T - 1
        inner = Cell([one_s[k, 1 : C + 1, s, :] for k in range(5)])
        outer = Cell([rows_s[side, k] for k in range(5)])
        fi, si = inner.flux(2)
        fo, so = outer.flux(2)
        if side == 0:
            near = face(outer.u, fo, so, inner.u, fi, si)
            wall, at_wall = wall_face(fi, si, inner.u[3], -1.0), hub
        else:
            near = face(inner.u, fi, si, outer.u, fo, so)
            wall, at_wall = wall_face(fi, si, inner.u[3], 1.0), casing
        for k in range(5):
            edge_s[side, k, 0:C, :] = jnp.where(at_wall, wall[k], near[k])

    def load1(c):
        return [one_s[k, c + 1] for k in range(5)]

    def slide1(c):
        return [ht_s[c * T : (c + 1) * T, 80 + 8 * k : 81 + 8 * k] for k in range(5)]

    def store1(c, u):
        for k in range(5):
            out_ref[k, c] = u[k]

    sweep(load1, 0, C, slide1, force0, store1)


def pairs(count, first, wrap):
    route = []
    for low in range(first, count, 2):
        high = low + 1
        if high < count or wrap:
            route += [(low, high % count), (high % count, low)]
    return route


def body(density, velocity, pressure, blade_force, offsets, weights):
    C, T, A = density.shape[1:]
    nc = lax.axis_size("circ")
    ns = lax.axis_size("span")
    area = C * T
    assert area == LANES and nc % 2 == 0 and A % LANES == 0 and C == 8
    rho, v, p, force = density[0], velocity[0], pressure[0], blade_force[0]

    u, sa, sb, pa, pb = call(
        functools.partial(first_kernel, C, T),
        [(5, C, T, A), (13, C, A), (13, C, A), (13, T, A), (13, T, A)],
        (rho, v, p, force),
    )
    ha = lax.ppermute(sa, "span", pairs(ns, 0, False))
    hb = lax.ppermute(sb, "span", pairs(ns, 1, False))
    pa = lax.ppermute(pa, "circ", pairs(nc, 0, True))
    pb = lax.ppermute(pb, "circ", pairs(nc, 1, True))

    thin = 2 * 16 * (A // LANES) // 2
    m1, m2 = call(
        functools.partial(thin_kernel, C, T),
        [(ROWS + thin, LANES), (2 * ROWS + thin, LANES)],
        (u, force, ha, hb),
        scratch=[pltpu.VMEM((area, LANES), jnp.float32)],
    )
    planes = m1[:ROWS]
    m1 = lax.ppermute(m1, "circ", pairs(nc, 0, True))
    if nc == 4:
        (m2,) = call(fill_kernel, [m2.shape], (m1, m2), aliases={1: 0})
        got = lax.ppermute(m2, "circ", pairs(nc, 1, True))
        (ring,) = call(ring_kernel, [(nc, ROWS, LANES)], (m2, got))
    else:
        got = lax.ppermute(m2, "circ", pairs(nc, 1, True))
        whole = lax.all_gather(planes, "circ")
        whole = jnp.concatenate([whole, whole], 0)
        ring = lax.dynamic_slice_in_dim(whole, lax.axis_index("circ"), nc, 0)
    partner = lax.ppermute(ring, "row", [(0, 1), (1, 0)])
    copies = max(1, 8 // nc)
    rows = nc * ROWS
    state, plane_flux = call(
        functools.partial(final_kernel, C, T, nc, ns),
        [(5, C, T, A), (2, 5, C, T)],
        (offsets, weights, u, force, ha, hb, pa, pb, m1, got, ring.reshape(rows, LANES), partner.reshape(rows, LANES)),
        specs=[smem(), smem()] + [vmem()] * 10,
        scratch=[
            pltpu.VMEM((copies * rows, LANES), jnp.float32),
            pltpu.VMEM((copies * rows, LANES), jnp.float32),
            pltpu.VMEM((LANES, LANES), jnp.float32),
            pltpu.VMEM((8, LANES), jnp.float32),
            pltpu.VMEM((5, C + 2, T, A), jnp.float32),
            pltpu.VMEM((8, LANES), jnp.float32),
            pltpu.VMEM((2, 5, 2 * C, A), jnp.float32),
            pltpu.VMEM((2, 5, C, A), jnp.float32),
        ],
    )
    return state[None], plane_flux[None]


def solution(mesh):
    placed = (
        P("row", "circ", "span", None),
        P("row", None, "circ", "span", None),
        P("row", "circ", "span", None),
        P("row", None, "circ", "span", None),
        P(),
        P(),
    )
    return jax.shard_map(
        body,
        mesh=mesh,
        in_specs=placed,
        out_specs=(P("row", None, "circ", "span", None), P("row", None, None, "circ", "span")),
        check_vma=False,
    )
```

```python
import functools

import jax
import jax.numpy as jnp
from jax import lax
from jax.experimental import pallas as pl
from jax.experimental.pallas import tpu as pltpu
from jax.sharding import PartitionSpec as P

GAMMA = 1.4
STEP = 0.04
INLET = (1.0, 0.5, 0.0, 0.0, 2.625)
LANES = 128
ROWS = 24


def vmem():
    return pl.BlockSpec(memory_space=pltpu.VMEM)


def smem():
    return pl.BlockSpec(memory_space=pltpu.SMEM)


def hbm():
    return pl.BlockSpec(memory_space=pltpu.HBM)


def call(kernel, shapes, args, specs=None, scratch=(), aliases=None, cost=None, limit=6):
    return pl.pallas_call(
        kernel,
        out_shape=[jax.ShapeDtypeStruct(s.shape, s.dtype) if hasattr(s, "dtype") else jax.ShapeDtypeStruct(s, jnp.float32) for s in shapes],
        in_specs=specs or [vmem()] * len(args),
        out_specs=[vmem()] * len(shapes),
        scratch_shapes=list(scratch),
        input_output_aliases=aliases or {},
        cost_estimate=cost,
        compiler_params=pltpu.CompilerParams(vmem_limit_bytes=limit << 20),
    )(*args)


class Cell:
    def __init__(self, u):
        self.u = u
        rho, m0, m1, m2, en = u
        self.inv = 1.0 / rho
        kin = 0.5 * (m0 * m0 + m1 * m1 + m2 * m2) * self.inv
        self.p = (GAMMA - 1.0) * (en - kin)
        self.sound = jnp.sqrt(GAMMA * self.p * self.inv)

    def flux(self, d):
        m = self.u[1:4]
        vel = m[d] * self.inv
        f = [m[d], m[0] * vel, m[1] * vel, m[2] * vel, (self.u[4] + self.p) * vel]
        f[1 + d] = f[1 + d] + self.p
        return f, jnp.abs(vel) + self.sound


def face(ul, fl, sl, ur, fr, sr):
    top = jnp.maximum(sl, sr)
    return [a + b - top * (y - x) for x, a, y, b in zip(ul, fl, ur, fr)]


def updated(u, force, *spans):
    src = [None, u[0] * force[0], u[0] * force[1], u[0] * force[2]]
    src.append(u[1] * force[0] + u[2] * force[1] + u[3] * force[2])
    out = []
    for k in range(5):
        div = spans[0][0][k] - spans[0][1][k]
        for hi, lo in spans[1:]:
            div = div + (hi[k] - lo[k])
        new = u[k] - (0.5 * STEP) * div
        out.append(new if src[k] is None else new + STEP * src[k])
    return out


def conserved(rho, v, p):
    m = [rho * x for x in v]
    en = p / (GAMMA - 1.0) + 0.5 * rho * (v[0] * v[0] + v[1] * v[1] + v[2] * v[2])
    return [rho] + m + [en]


def inlet_flux():
    rho, m0, m1, m2, en = INLET
    p = (GAMMA - 1.0) * (en - 0.5 * (m0 * m0 + m1 * m1 + m2 * m2) / rho)
    vel = m0 / rho
    f = [m0, m0 * vel + p, m1 * vel, m2 * vel, (en + p) * vel]
    return f, abs(vel) + (GAMMA * p / rho) ** 0.5


def axial_faces(cell, slide, rotor):
    u = cell.u
    f, s = cell.flux(0)
    shape = u[0].shape
    lane = lax.broadcasted_iota(jnp.int32, shape, 1)
    last = shape[1] - 1
    first_lane = lane == 0
    last_lane = lane == last
    inf, ins = inlet_flux()

    def back(x, v):
        return jnp.where(first_lane, v, pltpu.roll(x, 1, 1))

    pu = [back(x, v) for x, v in zip(u, INLET)]
    pf = [pu[1]] + [back(x, v) for x, v in zip(f[1:], inf[1:])]
    lo = face(pu, pf, back(s, ins), u, f, s)
    stator_first = jnp.logical_and(first_lane, jnp.logical_not(rotor))
    lo = [jnp.where(stator_first, h, x) for h, x in zip(slide, lo)]
    hi = [
        jnp.where(last_lane, jnp.where(rotor, h, 2.0 * g), pltpu.roll(x, last, 1))
        for h, g, x in zip(slide, f, lo)
    ]
    return hi, lo


def wall_face(f, s, m, sign):
    zero = jnp.zeros_like(s)
    return [zero, zero, zero, 2.0 * (f[3] + sign * s * m), zero]


def place():
    row = lax.axis_index("row")
    circ = lax.axis_index("circ")
    span = lax.axis_index("span")
    return row, lax.rem(circ, 2) == 0, lax.rem(span, 2) == 0, span


def first_kernel(
    C, T,
    rho_hbm, v_hbm, p_hbm, f_hbm, off_hbm, wt_hbm,
    u_ref, f_ref, off_ref, wt_ref, sa_ref, sb_ref, pa_ref, pb_ref,
    rho_ref, v_ref, p_ref, sem,
):
    copies = [
        pltpu.make_async_copy(src, dst, sem.at[i])
        for i, (src, dst) in enumerate(
            [(rho_hbm, rho_ref), (v_hbm, v_ref), (p_hbm, p_ref), (f_hbm, f_ref), (off_hbm, off_ref), (wt_hbm, wt_ref)]
        )
    ]
    for copy in copies:
        copy.start()
    _, even_c, even_s, _ = place()
    for copy in copies:
        copy.wait()
    for c in range(C):
        u = conserved(rho_ref[c], [v_ref[k, c] for k in range(3)], p_ref[c])
        for k in range(5):
            u_ref[k, c] = u[k]

    def row(k, s):
        ref = u_ref.at[k] if k < 5 else f_ref.at[k - 5]
        return ref[:, s, :]

    def send(slot, k, low, high):
        a, b = row(k, low), row(k, high)
        sa_ref[slot] = jnp.where(even_s, b, a)
        sb_ref[slot] = jnp.where(even_s, a, b)

    for k in range(5):
        send(k, k, 0, T - 1)
        send(5 + k, k, 1, T - 2)
    for k in range(3):
        send(10 + k, 5 + k, 0, T - 1)
    near = jnp.where(even_c, C - 1, 0)
    far = jnp.where(even_c, C - 2, 1)
    for ref, n, m in ((pa_ref, near, far), (pb_ref, C - 1 - near, C - 1 - far)):
        for k in range(5):
            ref[k] = u_ref[k, n]
            ref[5 + k] = u_ref[k, m]
        for k in range(3):
            ref[10 + k] = f_ref[k, n]


def thin_kernel(C, T, u_ref, f_ref, ha_ref, hb_ref, m1_ref, m2_ref, t_ref):
    row, even_c, even_s, _ = place()
    rotor = row == 0
    width = u_ref.shape[3]
    half = pl.ds(pl.multiple_of(jnp.where(rotor, width - LANES, 0), LANES), LANES)
    end = jnp.where(rotor, LANES - 1, 0)
    second = jnp.where(rotor, LANES - 2, 1)
    lane = lax.broadcasted_iota(jnp.int32, (C * T, LANES), 1)
    t = jnp.zeros((C * T, LANES), jnp.float32)

    def put(x, j, e):
        return pltpu.roll(x, lax.rem(j - e + LANES, LANES), 1)

    for k in range(5):
        x = u_ref[k, :, :, half].reshape(C * T, LANES)
        t = jnp.where(lane == k, put(x, k, end), t)
        t = jnp.where(lane == 5 + k, put(x, 5 + k, second), t)
    for k in range(3):
        t = jnp.where(lane == 10 + k, put(f_ref[k, :, :, half].reshape(C * T, LANES), 10 + k, end), t)
    t_ref[...] = t
    small = lax.broadcasted_iota(jnp.int32, (C, LANES), 1)
    for start, is_low in ((0, True), (T - 1, False)):
        where_a = even_s if not is_low else jnp.logical_not(even_s)
        rows = pl.ds(start, C, stride=T)
        x = t_ref[rows, :]
        for k in range(5):
            h = jnp.where(where_a, ha_ref[k, :, half], hb_ref[k, :, half])
            x = jnp.where(small == 13 + k, put(h, 13 + k, end), x)
        t_ref[rows, :] = x
    planes = t_ref[...].T[:ROWS]
    m1_ref[0:ROWS, :] = planes
    m2_ref[0:ROWS, :] = planes
    m2_ref[ROWS : 2 * ROWS, :] = jnp.zeros((ROWS, LANES), jnp.float32)

    def corner(ref, base, c):
        for k in range(5):
            for side in range(2):
                where_a = even_s if side == 1 else jnp.logical_not(even_s)
                x = jnp.where(where_a, ha_ref[k, pl.ds(c, 1), :], hb_ref[k, pl.ds(c, 1), :])
                for part in range(width // LANES):
                    r = base + 16 * part + 2 * k + side
                    ref[r : r + 1, :] = x[:, part * LANES : (part + 1) * LANES]
        for part in range(width // LANES):
            r = base + 16 * part
            ref[r + 10 : r + 16, :] = jnp.zeros((6, LANES), jnp.float32)

    near = jnp.where(even_c, C - 1, 0)
    corner(m1_ref, ROWS, near)
    corner(m2_ref, 2 * ROWS, C - 1 - near)


def fill_kernel(m1_ref, m2_ref, out_ref):
    out_ref[...] = m2_ref[...]
    out_ref[ROWS : 2 * ROWS, :] = m1_ref[0:ROWS, :]


def ring_kernel(m2_ref, got_ref, ring_ref):
    _, even, _, _ = place()
    mate = m2_ref[ROWS : 2 * ROWS, :]
    next_ = got_ref[0:ROWS, :]
    ring_ref[0] = m2_ref[0:ROWS, :]
    ring_ref[1] = jnp.where(even, mate, next_)
    ring_ref[2] = got_ref[ROWS : 2 * ROWS, :]
    ring_ref[3] = jnp.where(even, next_, mate)


def final_kernel(
    C, T, nc, ns,
    off_ref, wt_ref, u_ref, f_ref, ha_ref, hb_ref, pa_ref, pb_ref, m1_ref, m2_ref, own_ref, par_ref,
    out_ref, pf_ref,
    own_s, par_s, ht_s, ext_s, one_s, far_s, edge_s, rows_s,
):
    row, even_c, even_s, span = place()
    rotor = row == 0
    hub = span == 0
    casing = span == ns - 1
    width = u_ref.shape[3]
    periods = own_s.shape[0] // (nc * ROWS)
    depth = nc * periods
    sg = jnp.where(rotor, 1, -1)
    sgf = jnp.where(rotor, 1.0, -1.0)
    cycle = nc * C

    for copy in range(periods):
        own_s[copy * nc * ROWS : (copy + 1) * nc * ROWS, :] = own_ref[...]
        par_s[copy * nc * ROWS : (copy + 1) * nc * ROWS, :] = par_ref[...]
    shape = (depth, LANES)
    lane = lax.broadcasted_iota(jnp.int32, shape, 1)
    in_span = lax.rem(lane, T)

    def get(ref, j):
        return ref[pl.ds(j, depth, stride=ROWS), :]

    def ahead(x, k):
        if k == 0:
            return x
        a = pltpu.roll(x, (LANES - T * k) % LANES, 1)
        b = pltpu.roll(a, depth - 1, 0)
        return jnp.where(lane < LANES - T * k, a, b)

    def behind(x):
        a = pltpu.roll(x, T, 1)
        b = pltpu.roll(a, 1, 0)
        return jnp.where(lane >= T, a, b)

    def turned(x, cells):
        q = lax.div(cells, C)
        r = lax.rem(cells, C)
        y = pltpu.roll(x, lax.rem(depth - q, depth), 0)
        a = pltpu.roll(y, lax.rem(LANES - T * r, LANES), 1)
        b = pltpu.roll(a, depth - 1, 0)
        return jnp.where(lane < LANES - T * r, a, b)

    def taps(t):
        w = [jnp.full((1, LANES), wt_ref[t, k], jnp.float32) for k in range(4)]
        total = w[0] + w[1] + w[2] + w[3]
        return [x / total for x in w]

    def ghosts(xs, t, sign):
        w = taps(t)
        start = lax.rem(sign * off_ref[t] - 1 + 2 * cycle, cycle)
        out = []
        for x in xs:
            x = turned(x, start)
            g = w[0] * x
            for k in range(1, 4):
                g = g + w[k] * ahead(x, k)
            out.append(g)
        return out

    def slide(cell, ghost, sign):
        f, s = cell.flux(0)
        g = Cell(ghost)
        fg, s_g = g.flux(0)
        top = jnp.maximum(s, s_g) * sign
        return [a + b - top * (y - x) for x, a, y, b in zip(cell.u, f, ghost, fg)]

    def ring_step(ref, cell, h, sign):
        inner = Cell([get(ref, 5 + k) for k in range(5)])
        fi, si = inner.flux(0)
        f, s = cell.flux(0)
        top = jnp.maximum(s, si) * sign
        h1 = [a + b - top * (x - y) for x, a, y, b in zip(cell.u, f, inner.u, fi)]
        ax_hi = [sign * x for x in h]
        ax_lo = [sign * x for x in h1]
        f, s = cell.flux(1)
        lo = face([behind(x) for x in cell.u], [behind(x) for x in f], behind(s), cell.u, f, s)
        hi = [ahead(x, 1) for x in lo]
        f, s = cell.flux(2)
        edge = Cell([get(ref, 13 + k) for k in range(5)])
        fe, se = edge.flux(2)
        first = in_span == 0
        last = in_span == T - 1

        def prev(x, e):
            return jnp.where(first, e, pltpu.roll(x, 1, 1))

        slo = face([prev(x, e) for x, e in zip(cell.u, edge.u)], [prev(x, e) for x, e in zip(f, fe)], prev(s, se), cell.u, f, s)
        wall = wall_face(f, s, cell.u[3], -1.0)
        slo = [jnp.where(jnp.logical_and(first, hub), a, b) for a, b in zip(wall, slo)]
        top_face = face(cell.u, f, s, edge.u, fe, se)
        wall = wall_face(f, s, cell.u[3], 1.0)
        top_face = [jnp.where(casing, a, b) for a, b in zip(wall, top_face)]
        shi = [jnp.where(last, a, pltpu.roll(b, LANES - 1, 1)) for a, b in zip(top_face, slo)]
        force = [get(ref, 10 + k) for k in range(3)]
        return updated(cell.u, force, (ax_hi, ax_lo), (hi, lo), (shi, slo))

    own = Cell([get(own_s, k) for k in range(5)])
    par = Cell([get(par_s, k) for k in range(5)])
    g_own = ghosts(par.u, 0, sg)
    g_par = ghosts(own.u, 0, -sg)
    h_own = slide(own, g_own, sgf)
    h_par = slide(par, g_par, -sgf)
    g_edge = ghosts([get(par_s, 13 + k) for k in range(5)], 0, sg)
    h_edge = slide(Cell([get(own_s, 13 + k) for k in range(5)]), g_edge, sgf)
    own_new = ring_step(own_s, own, h_own, sgf)
    par_new = ring_step(par_s, par, h_par, -sgf)
    h_next = slide(Cell(own_new), ghosts(par_new, 1, sg), sgf)

    def eight(x):
        if depth == 8:
            return x
        return jnp.concatenate([x[0:7], x[depth - 1 : depth]], 0)

    tile = [eight(x) for x in h_own + h_edge + h_next]
    tile.append(jnp.zeros((8, LANES), jnp.float32))
    ht_s[...] = jnp.concatenate(tile, 0).T
    for t, h in ((0, h_own), (1, h_next)):
        for k in range(5):
            x = 0.5 * h[k][0:1, :]
            for c in range(C):
                pf_ref[t, k, c : c + 1, :] = x[:, c * T : (c + 1) * T]

    def left(slot, rows=slice(None)):
        return jnp.where(even_c, pb_ref[slot, rows, :], pa_ref[slot, rows, :])

    def right(slot, rows=slice(None)):
        return jnp.where(even_c, pa_ref[slot, rows, :], pb_ref[slot, rows, :])

    def low(slot):
        return jnp.where(even_s, hb_ref[slot], ha_ref[slot])

    def high(slot):
        return jnp.where(even_s, ha_ref[slot], hb_ref[slot])

    def corner(ref, base, k, side):
        parts = [ref[pl.ds(base + 16 * q + 2 * k + side, 1), :] for q in range(width // LANES)]
        return jnp.concatenate(parts, 1)

    def corners(k, side):
        a = corner(m1_ref, ROWS, k, side)
        b = corner(m2_ref, 2 * ROWS, k, side)
        return jnp.where(even_c, b, a), jnp.where(even_c, a, b)

    eight_rows = lax.broadcasted_iota(jnp.int32, (C, width), 0)

    def extend(mid, lf, rt):
        shape = (C, width)
        tail = jnp.where(eight_rows == 0, jnp.broadcast_to(rt, shape), jnp.broadcast_to(lf, shape))
        return jnp.concatenate([mid, tail], 0)

    def own_row(k, s):
        mid = u_ref[k, :, s, :]
        return extend(mid, left(k, pl.ds(s, 1)), right(k, pl.ds(s, 1)))

    for side in range(2):
        halo = low if side == 0 else high
        inner = Cell([own_row(k, 0 if side == 0 else T - 1) for k in range(5)])
        lf_rt = [corners(k, side) for k in range(5)]
        cell = Cell([extend(halo(k), *lf_rt[k]) for k in range(5)])
        outer = Cell([halo(5 + k) for k in range(5)])
        f, s = cell.flux(2)
        fi, si = inner.flux(2)
        fo, so = outer.flux(2)
        cut = lambda xs: [x[:C] for x in xs]
        if side == 0:
            near = face(cell.u, f, s, inner.u, fi, si)
            hi2, lo2 = near, face(outer.u, fo, so, cut(cell.u), cut(f), s[:C])
            wall = wall_face(fi, si, inner.u[3], -1.0)
            at_wall = hub
        else:
            near = face(inner.u, fi, si, cell.u, f, s)
            hi2, lo2 = face(cut(cell.u), cut(f), s[:C], outer.u, fo, so), near
            wall = wall_face(fi, si, inner.u[3], 1.0)
            at_wall = casing
        for k in range(5):
            edge_s[side, k] = jnp.where(at_wall, wall[k], near[k])
        f, s = cell.flux(1)
        back = lambda x: pltpu.roll(x, 1, 0)
        lo1 = face([back(x) for x in cell.u], [back(x) for x in f], back(s), cell.u, f, s)
        hi1 = [pltpu.roll(x, 2 * C - 1, 0) for x in lo1]
        mid = Cell(cut(cell.u))
        first = 0 if side == 0 else T - 1
        strip = ht_s[pl.ds(first, C, stride=T), :]
        hs = [strip[:, 40 + 8 * k : 41 + 8 * k] for k in range(5)]
        hi0, lo0 = axial_faces(mid, hs, rotor)
        force = [halo(10 + k) for k in range(3)]
        new = updated(mid.u, force, (hi0, lo0), (cut(hi1), cut(lo1)), (cut(hi2), cut(lo2)))
        for k in range(5):
            rows_s[side, k] = new[k]

    column = (T, width)
    srow = lax.broadcasted_iota(jnp.int32, column, 0)

    def column_update(cell, circ_lo, circ_hi, slide_h, edge_row, force):
        hi0, lo0 = axial_faces(cell, slide_h, rotor)
        f, s = cell.flux(2)
        back = lambda x: pltpu.roll(x, 1, 0)
        lo2 = face([back(x) for x in cell.u], [back(x) for x in f], back(s), cell.u, f, s)
        low_row = [edge_s[0, k, edge_row : edge_row + 1, :] for k in range(5)]
        top_row = [edge_s[1, k, edge_row : edge_row + 1, :] for k in range(5)]
        lo2 = [jnp.where(srow == 0, jnp.broadcast_to(e, column), x) for e, x in zip(low_row, lo2)]
        hi2 = [
            jnp.where(srow == T - 1, jnp.broadcast_to(e, column), pltpu.roll(x, T - 1, 0))
            for e, x in zip(top_row, lo2)
        ]
        return updated(cell.u, force, (hi0, lo0), (circ_hi, circ_lo), (hi2, lo2))

    def sweep(load, lo, hi, slide_of, force_of, store):
        prev = Cell(load(lo - 1))
        pf, ps = prev.flux(1)
        cell = Cell(load(lo))
        cf, cs = cell.flux(1)
        h_lo = face(prev.u, pf, ps, cell.u, cf, cs)
        for c in range(lo, hi):
            nxt = Cell(load(c + 1))
            nf, ns_ = nxt.flux(1)
            h_hi = face(cell.u, cf, cs, nxt.u, nf, ns_)
            edge_row = c if c >= 0 else 2 * C - 1
            store(c, column_update(cell, h_lo, h_hi, slide_of(c), edge_row, force_of(c)))
            cell, cf, cs, h_lo = nxt, nf, ns_, h_hi

    def load0(c):
        if c < 0:
            return [left(k + (5 if c == -2 else 0)) for k in range(5)]
        if c >= C:
            return [right(k + (5 if c == C + 1 else 0)) for k in range(5)]
        return [u_ref[k, c] for k in range(5)]

    def force0(c):
        if c < 0:
            return [left(10 + k) for k in range(3)]
        if c >= C:
            return [right(10 + k) for k in range(3)]
        return [f_ref[k, c] for k in range(3)]

    def slide0(c):
        sector = 0 if 0 <= c < C else (1 if c >= C else 7)
        r = (c % C) * T
        return [ht_s[r : r + T, 8 * k + sector : 8 * k + sector + 1] for k in range(5)]

    def store0(c, u):
        for k in range(5):
            one_s[k, c + 1] = u[k]

    sweep(load0, -1, C + 1, slide0, force0, store0)

    for side in range(2):
        s = 0 if side == 0 else T - 1
        inner = Cell([one_s[k, 1 : C + 1, s, :] for k in range(5)])
        outer = Cell([rows_s[side, k] for k in range(5)])
        fi, si = inner.flux(2)
        fo, so = outer.flux(2)
        if side == 0:
            near = face(outer.u, fo, so, inner.u, fi, si)
            wall, at_wall = wall_face(fi, si, inner.u[3], -1.0), hub
        else:
            near = face(inner.u, fi, si, outer.u, fo, so)
            wall, at_wall = wall_face(fi, si, inner.u[3], 1.0), casing
        for k in range(5):
            edge_s[side, k, 0:C, :] = jnp.where(at_wall, wall[k], near[k])

    def load1(c):
        return [one_s[k, c + 1] for k in range(5)]

    def slide1(c):
        return [ht_s[c * T : (c + 1) * T, 80 + 8 * k : 81 + 8 * k] for k in range(5)]

    def store1(c, u):
        for k in range(5):
            out_ref[k, c] = u[k]

    sweep(load1, 0, C, slide1, force0, store1)


def pairs(count, first, wrap):
    route = []
    for low in range(first, count, 2):
        high = low + 1
        if high < count or wrap:
            route += [(low, high % count), (high % count, low)]
    return route


def body(density, velocity, pressure, blade_force, offsets, weights):
    C, T, A = density.shape[1:]
    nc = lax.axis_size("circ")
    ns = lax.axis_size("span")
    area = C * T
    assert area == LANES and nc % 2 == 0 and A % LANES == 0 and C == 8
    rho, v, p, force = density[0], velocity[0], pressure[0], blade_force[0]

    u, force, off, wt, sa, sb, pa, pb = call(
        functools.partial(first_kernel, C, T),
        [(5, C, T, A), (3, C, T, A), offsets, weights, (13, C, A), (13, C, A), (13, T, A), (13, T, A)],
        [pltpu.with_memory_space_constraint(x, pltpu.HBM) for x in (rho, v, p, force, offsets, weights)],
        specs=[hbm()] * 6,
        scratch=[
            pltpu.VMEM((C, T, A), jnp.float32),
            pltpu.VMEM((3, C, T, A), jnp.float32),
            pltpu.VMEM((C, T, A), jnp.float32),
            pltpu.SemaphoreType.DMA((6,)),
        ],
    )
    ha = lax.ppermute(sa, "span", pairs(ns, 0, False))
    hb = lax.ppermute(sb, "span", pairs(ns, 1, False))
    pa = lax.ppermute(pa, "circ", pairs(nc, 0, True))
    pb = lax.ppermute(pb, "circ", pairs(nc, 1, True))

    thin = 2 * 16 * (A // LANES) // 2
    m1, m2 = call(
        functools.partial(thin_kernel, C, T),
        [(ROWS + thin, LANES), (2 * ROWS + thin, LANES)],
        (u, force, ha, hb),
        scratch=[pltpu.VMEM((area, LANES), jnp.float32)],
    )
    planes = m1[:ROWS]
    m1 = lax.ppermute(m1, "circ", pairs(nc, 0, True))
    if nc == 4:
        (m2,) = call(fill_kernel, [m2.shape], (m1, m2), aliases={1: 0})
        got = lax.ppermute(m2, "circ", pairs(nc, 1, True))
        (ring,) = call(ring_kernel, [(nc, ROWS, LANES)], (m2, got))
    else:
        got = lax.ppermute(m2, "circ", pairs(nc, 1, True))
        whole = lax.all_gather(planes, "circ")
        whole = jnp.concatenate([whole, whole], 0)
        ring = lax.dynamic_slice_in_dim(whole, lax.axis_index("circ"), nc, 0)
    partner = lax.ppermute(ring, "row", [(0, 1), (1, 0)])
    copies = max(1, 8 // nc)
    rows = nc * ROWS
    state, plane_flux = call(
        functools.partial(final_kernel, C, T, nc, ns),
        [(5, C, T, A), (2, 5, C, T)],
        (off, wt, u, force, ha, hb, pa, pb, m1, got, ring.reshape(rows, LANES), partner.reshape(rows, LANES)),
        specs=[smem(), smem()] + [vmem()] * 10,
        limit=16,
        scratch=[
            pltpu.VMEM((copies * rows, LANES), jnp.float32),
            pltpu.VMEM((copies * rows, LANES), jnp.float32),
            pltpu.VMEM((LANES, LANES), jnp.float32),
            pltpu.VMEM((8, LANES), jnp.float32),
            pltpu.VMEM((5, C + 2, T, A), jnp.float32),
            pltpu.VMEM((8, LANES), jnp.float32),
            pltpu.VMEM((2, 5, 2 * C, A), jnp.float32),
            pltpu.VMEM((2, 5, C, A), jnp.float32),
        ],
    )
    return state[None], plane_flux[None]


def solution(mesh):
    placed = (
        P("row", "circ", "span", None),
        P("row", None, "circ", "span", None),
        P("row", "circ", "span", None),
        P("row", None, "circ", "span", None),
        P(),
        P(),
    )
    return jax.shard_map(
        body,
        mesh=mesh,
        in_specs=placed,
        out_specs=(P("row", None, "circ", "span", None), P("row", None, None, "circ", "span")),
        check_vma=False,
    )
```

```python
import functools

import jax
import jax.numpy as jnp
from jax import lax
from jax.experimental import pallas as pl
from jax.experimental.pallas import tpu as pltpu
from jax.sharding import PartitionSpec as P

GAMMA = 1.4
STEP = 0.04
INLET = (1.0, 0.5, 0.0, 0.0, 2.625)
LANES = 128
ROWS = 24


def vmem():
    return pl.BlockSpec(memory_space=pltpu.VMEM)


def smem():
    return pl.BlockSpec(memory_space=pltpu.SMEM)


def hbm():
    return pl.BlockSpec(memory_space=pltpu.HBM)


def call(kernel, shapes, args, specs=None, scratch=(), aliases=None, cost=None, limit=6, outs=None):
    return pl.pallas_call(
        kernel,
        out_shape=[jax.ShapeDtypeStruct(s.shape, s.dtype) if hasattr(s, "dtype") else jax.ShapeDtypeStruct(s, jnp.float32) for s in shapes],
        in_specs=specs or [vmem()] * len(args),
        out_specs=outs or [vmem()] * len(shapes),
        scratch_shapes=list(scratch),
        input_output_aliases=aliases or {},
        cost_estimate=cost,
        compiler_params=pltpu.CompilerParams(vmem_limit_bytes=limit << 20),
    )(*args)


class Cell:
    def __init__(self, u):
        self.u = u
        rho, m0, m1, m2, en = u
        self.inv = 1.0 / rho
        kin = 0.5 * (m0 * m0 + m1 * m1 + m2 * m2) * self.inv
        self.p = (GAMMA - 1.0) * (en - kin)
        self.sound = jnp.sqrt(GAMMA * self.p * self.inv)

    def flux(self, d):
        m = self.u[1:4]
        vel = m[d] * self.inv
        f = [m[d], m[0] * vel, m[1] * vel, m[2] * vel, (self.u[4] + self.p) * vel]
        f[1 + d] = f[1 + d] + self.p
        return f, jnp.abs(vel) + self.sound


def face(ul, fl, sl, ur, fr, sr):
    top = jnp.maximum(sl, sr)
    return [a + b - top * (y - x) for x, a, y, b in zip(ul, fl, ur, fr)]


def updated(u, force, *spans):
    src = [None, u[0] * force[0], u[0] * force[1], u[0] * force[2]]
    src.append(u[1] * force[0] + u[2] * force[1] + u[3] * force[2])
    out = []
    for k in range(5):
        div = spans[0][0][k] - spans[0][1][k]
        for hi, lo in spans[1:]:
            div = div + (hi[k] - lo[k])
        new = u[k] - (0.5 * STEP) * div
        out.append(new if src[k] is None else new + STEP * src[k])
    return out


def conserved(rho, v, p):
    m = [rho * x for x in v]
    en = p / (GAMMA - 1.0) + 0.5 * rho * (v[0] * v[0] + v[1] * v[1] + v[2] * v[2])
    return [rho] + m + [en]


def inlet_flux():
    rho, m0, m1, m2, en = INLET
    p = (GAMMA - 1.0) * (en - 0.5 * (m0 * m0 + m1 * m1 + m2 * m2) / rho)
    vel = m0 / rho
    f = [m0, m0 * vel + p, m1 * vel, m2 * vel, (en + p) * vel]
    return f, abs(vel) + (GAMMA * p / rho) ** 0.5


def axial_faces(cell, slide, rotor):
    u = cell.u
    f, s = cell.flux(0)
    shape = u[0].shape
    lane = lax.broadcasted_iota(jnp.int32, shape, 1)
    last = shape[1] - 1
    first_lane = lane == 0
    last_lane = lane == last
    inf, ins = inlet_flux()

    def back(x, v):
        return jnp.where(first_lane, v, pltpu.roll(x, 1, 1))

    pu = [back(x, v) for x, v in zip(u, INLET)]
    pf = [pu[1]] + [back(x, v) for x, v in zip(f[1:], inf[1:])]
    lo = face(pu, pf, back(s, ins), u, f, s)
    stator_first = jnp.logical_and(first_lane, jnp.logical_not(rotor))
    lo = [jnp.where(stator_first, h, x) for h, x in zip(slide, lo)]
    hi = [
        jnp.where(last_lane, jnp.where(rotor, h, 2.0 * g), pltpu.roll(x, last, 1))
        for h, g, x in zip(slide, f, lo)
    ]
    return hi, lo


def wall_face(f, s, m, sign):
    zero = jnp.zeros_like(s)
    return [zero, zero, zero, 2.0 * (f[3] + sign * s * m), zero]


def place():
    row = lax.axis_index("row")
    circ = lax.axis_index("circ")
    span = lax.axis_index("span")
    return row, lax.rem(circ, 2) == 0, lax.rem(span, 2) == 0, span


def first_kernel(
    C, T,
    rho_hbm, v_hbm, p_hbm, f_hbm, off_hbm, wt_hbm,
    u_ref, f_ref, off_ref, wt_ref, sa_ref, sb_ref, pa_ref, pb_ref,
    rho_ref, v_ref, p_ref, sem,
):
    copies = [
        pltpu.make_async_copy(src, dst, sem.at[i])
        for i, (src, dst) in enumerate(
            [(rho_hbm, rho_ref), (v_hbm, v_ref), (p_hbm, p_ref), (f_hbm, f_ref), (off_hbm, off_ref), (wt_hbm, wt_ref)]
        )
    ]
    for copy in copies:
        copy.start()
    _, even_c, even_s, _ = place()
    for copy in copies:
        copy.wait()
    for c in range(C):
        u = conserved(rho_ref[c], [v_ref[k, c] for k in range(3)], p_ref[c])
        for k in range(5):
            u_ref[k, c] = u[k]

    def row(k, s):
        ref = u_ref.at[k] if k < 5 else f_ref.at[k - 5]
        return ref[:, s, :]

    def send(slot, k, low, high):
        a, b = row(k, low), row(k, high)
        sa_ref[slot] = jnp.where(even_s, b, a)
        sb_ref[slot] = jnp.where(even_s, a, b)

    for k in range(5):
        send(k, k, 0, T - 1)
        send(5 + k, k, 1, T - 2)
    for k in range(3):
        send(10 + k, 5 + k, 0, T - 1)
    near = jnp.where(even_c, C - 1, 0)
    far = jnp.where(even_c, C - 2, 1)
    for ref, n, m in ((pa_ref, near, far), (pb_ref, C - 1 - near, C - 1 - far)):
        for k in range(5):
            ref[k] = u_ref[k, n]
            ref[5 + k] = u_ref[k, m]
        for k in range(3):
            ref[10 + k] = f_ref[k, n]


def thin_kernel(C, T, u_ref, f_ref, ha_ref, hb_ref, m1_ref, m2_ref, t_ref):
    row, even_c, even_s, _ = place()
    rotor = row == 0
    width = u_ref.shape[3]
    half = pl.ds(pl.multiple_of(jnp.where(rotor, width - LANES, 0), LANES), LANES)
    end = jnp.where(rotor, LANES - 1, 0)
    second = jnp.where(rotor, LANES - 2, 1)
    lane = lax.broadcasted_iota(jnp.int32, (C * T, LANES), 1)
    t = jnp.zeros((C * T, LANES), jnp.float32)

    def put(x, j, e):
        return pltpu.roll(x, lax.rem(j - e + LANES, LANES), 1)

    for k in range(5):
        x = u_ref[k, :, :, half].reshape(C * T, LANES)
        t = jnp.where(lane == k, put(x, k, end), t)
        t = jnp.where(lane == 5 + k, put(x, 5 + k, second), t)
    for k in range(3):
        t = jnp.where(lane == 10 + k, put(f_ref[k, :, :, half].reshape(C * T, LANES), 10 + k, end), t)
    t_ref[...] = t
    small = lax.broadcasted_iota(jnp.int32, (C, LANES), 1)
    for start, is_low in ((0, True), (T - 1, False)):
        where_a = even_s if not is_low else jnp.logical_not(even_s)
        rows = pl.ds(start, C, stride=T)
        x = t_ref[rows, :]
        for k in range(5):
            h = jnp.where(where_a, ha_ref[k, :, half], hb_ref[k, :, half])
            x = jnp.where(small == 13 + k, put(h, 13 + k, end), x)
        t_ref[rows, :] = x
    planes = t_ref[...].T[:ROWS]
    m1_ref[0:ROWS, :] = planes
    m2_ref[0:ROWS, :] = planes
    m2_ref[ROWS : 2 * ROWS, :] = jnp.zeros((ROWS, LANES), jnp.float32)

    def corner(ref, base, c):
        for k in range(5):
            for side in range(2):
                where_a = even_s if side == 1 else jnp.logical_not(even_s)
                x = jnp.where(where_a, ha_ref[k, pl.ds(c, 1), :], hb_ref[k, pl.ds(c, 1), :])
                for part in range(width // LANES):
                    r = base + 16 * part + 2 * k + side
                    ref[r : r + 1, :] = x[:, part * LANES : (part + 1) * LANES]
        for part in range(width // LANES):
            r = base + 16 * part
            ref[r + 10 : r + 16, :] = jnp.zeros((6, LANES), jnp.float32)

    near = jnp.where(even_c, C - 1, 0)
    corner(m1_ref, ROWS, near)
    corner(m2_ref, 2 * ROWS, C - 1 - near)


def fill_kernel(m1_ref, m2_ref, out_ref):
    out_ref[...] = m2_ref[...]
    out_ref[ROWS : 2 * ROWS, :] = m1_ref[0:ROWS, :]


def ring_kernel(m2_ref, got_ref, after_ref, ring_ref):
    _, even, _, _ = place()
    mate = m2_ref[ROWS : 2 * ROWS, :]
    next_ = got_ref[0:ROWS, :]
    ring_ref[0] = m2_ref[0:ROWS, :]
    ring_ref[1] = jnp.where(even, mate, next_)
    ring_ref[2] = got_ref[ROWS : 2 * ROWS, :]
    ring_ref[3] = jnp.where(even, next_, mate)


class Halo:
    def __init__(self, C, ha, hb, pa, pb):
        _, self.even_c, self.even_s, _ = place()
        self.C, self.ha, self.hb, self.pa, self.pb = C, ha, hb, pa, pb

    def left(self, slot, rows=slice(None)):
        return jnp.where(self.even_c, self.pb[slot, rows, :], self.pa[slot, rows, :])

    def right(self, slot, rows=slice(None)):
        return jnp.where(self.even_c, self.pa[slot, rows, :], self.pb[slot, rows, :])

    def beyond(self, side, slot):
        where_a = self.even_s if side == 1 else jnp.logical_not(self.even_s)
        return jnp.where(where_a, self.ha[slot], self.hb[slot])


def edge_faces(side, outer, inner, at_wall):
    fo, so = outer.flux(2)
    fi, si = inner.flux(2)
    if side == 0:
        near = face(outer.u, fo, so, inner.u, fi, si)
        wall = wall_face(fi, si, inner.u[3], -1.0)
    else:
        near = face(inner.u, fi, si, outer.u, fo, so)
        wall = wall_face(fi, si, inner.u[3], 1.0)
    return [jnp.where(at_wall, w, x) for w, x in zip(wall, near)], near


def column_update(cell, circ_lo, circ_hi, axial, low_row, top_row, force):
    column = cell.u[0].shape
    T = column[0]
    srow = lax.broadcasted_iota(jnp.int32, column, 0)
    f, s = cell.flux(2)
    back = lambda x: pltpu.roll(x, 1, 0)
    lo2 = face([back(x) for x in cell.u], [back(x) for x in f], back(s), cell.u, f, s)
    lo2 = [jnp.where(srow == 0, jnp.broadcast_to(e, column), x) for e, x in zip(low_row, lo2)]
    hi2 = [
        jnp.where(srow == T - 1, jnp.broadcast_to(e, column), pltpu.roll(x, T - 1, 0))
        for e, x in zip(top_row, lo2)
    ]
    return updated(cell.u, force, axial, (circ_hi, circ_lo), (hi2, lo2))


def sweep(load, lo, hi, axial_of, edges_of, force_of, store):
    prev = Cell(load(lo - 1))
    pf, ps = prev.flux(1)
    cell = Cell(load(lo))
    cf, cs = cell.flux(1)
    h_lo = face(prev.u, pf, ps, cell.u, cf, cs)
    for c in range(lo, hi):
        nxt = Cell(load(c + 1))
        nf, ns_ = nxt.flux(1)
        h_hi = face(cell.u, cf, cs, nxt.u, nf, ns_)
        store(c, column_update(cell, h_lo, h_hi, axial_of(c, cell), *edges_of(c), force_of(c)))
        cell, cf, cs, h_lo = nxt, nf, ns_, h_hi


def walls(ns):
    span = lax.axis_index("span")
    return span == 0, span == ns - 1


def bulk_kernel(C, T, ns, u_ref, f_ref, ha_ref, hb_ref, after_ref, one_ref, edge_s):
    rotor = lax.axis_index("row") == 0
    halo = Halo(C, ha_ref, hb_ref, None, None)
    for side, wall in enumerate(walls(ns)):
        inner = Cell([u_ref[k, :, 0 if side == 0 else T - 1, :] for k in range(5)])
        outer = Cell([halo.beyond(side, k) for k in range(5)])
        edge, _ = edge_faces(side, outer, inner, wall)
        for k in range(5):
            edge_s[side, k] = edge[k]

    def axial(c, cell):
        return axial_faces(cell, [0.0] * 5, rotor)

    def edges(c):
        return [[edge_s[side, k, c : c + 1, :] for k in range(5)] for side in range(2)]

    def store(c, u):
        for k in range(5):
            one_ref[k, c] = u[k]

    sweep(lambda c: [u_ref[k, c] for k in range(5)], 1, C - 1, axial, edges, lambda c: [f_ref[k, c] for k in range(3)], store)


def half_faces(cell, beside, rotor, near, slide=None):
    f, s = cell.flux(0)
    lane = lax.broadcasted_iota(jnp.int32, s.shape, 1)
    first = lane == 0
    last = lane == LANES - 1
    inf, ins = inlet_flux()

    def back(x, v):
        return jnp.where(first, v, pltpu.roll(x, 1, 1))

    pu = [back(x, v) for x, v in zip(cell.u, INLET)]
    pf = [pu[1]] + [back(x, v) for x, v in zip(f[1:], inf[1:])]
    lo = face(pu, pf, back(s, ins), cell.u, f, s)
    fb, sb = beside.flux(0)
    sign = jnp.where(rotor, 1.0, -1.0) * (-1.0 if near else 1.0)
    top = jnp.maximum(s, sb) * sign
    mid = [a + b - top * (y - x) for x, a, y, b in zip(cell.u, f, beside.u, fb)]
    if near:
        lo = [jnp.where(first, jnp.where(rotor, m, h), x) for m, h, x in zip(mid, slide, lo)]
        hi = [jnp.where(last, jnp.where(rotor, h, m), pltpu.roll(x, LANES - 1, 1)) for m, h, x in zip(mid, slide, lo)]
    else:
        lo = [jnp.where(jnp.logical_and(first, jnp.logical_not(rotor)), m, x) for m, x in zip(mid, lo)]
        hi = [
            jnp.where(last, jnp.where(rotor, m, 2.0 * g), pltpu.roll(x, LANES - 1, 1))
            for m, g, x in zip(mid, f, lo)
        ]
    return hi, lo


def halves(width, rotor):
    near = pl.multiple_of(jnp.where(rotor, width - LANES, 0), LANES)
    return near, pl.multiple_of(width - LANES - near, LANES)


def far_kernel(
    C, T, ns,
    u_ref, f_ref, ha_ref, hb_ref, pa_ref, pb_ref, m1_ref, m2_ref, one_ref, after_ref,
    near_ref, rows_ref, beside_ref, far_ref,
    edge_s, col_s, row_s, fedge_s,
):
    rotor = lax.axis_index("row") == 0
    width = u_ref.shape[3]
    near, far = halves(width, rotor)
    halo = Halo(C, ha_ref, hb_ref, pa_ref, pb_ref)

    def corner(ref, base, k, side):
        parts = [ref[pl.ds(base + 16 * q + 2 * k + side, 1), :] for q in range(width // LANES)]
        return jnp.concatenate(parts, 1)

    def corners(k, side):
        a = corner(m1_ref, ROWS, k, side)
        b = corner(m2_ref, 2 * ROWS, k, side)
        return jnp.where(halo.even_c, b, a), jnp.where(halo.even_c, a, b)

    top_rows = lax.broadcasted_iota(jnp.int32, (C, width), 0)

    def extend(mid, lf, rt):
        shape = (C, width)
        tail = jnp.where(top_rows == 0, jnp.broadcast_to(rt, shape), jnp.broadcast_to(lf, shape))
        return jnp.concatenate([mid, tail], 0)

    cut = lambda xs: [x[:C] for x in xs]
    for side, wall in enumerate(walls(ns)):
        s0 = 0 if side == 0 else T - 1
        row = pl.ds(s0, 1)
        inner = Cell([extend(u_ref[k, :, s0, :], halo.left(k, row), halo.right(k, row)) for k in range(5)])
        cell = Cell([extend(halo.beyond(side, k), *corners(k, side)) for k in range(5)])
        outer = Cell([halo.beyond(side, 5 + k) for k in range(5)])
        edge, adjoining = edge_faces(side, cell, inner, wall)
        for k in range(5):
            edge_s[side, k] = edge[k]
        f, s = cell.flux(2)
        fo, so = outer.flux(2)
        if side == 0:
            span = cut(adjoining), face(outer.u, fo, so, cut(cell.u), cut(f), s[:C])
        else:
            span = face(cut(cell.u), cut(f), s[:C], outer.u, fo, so), cut(adjoining)
        f, s = cell.flux(1)
        back = lambda x: pltpu.roll(x, 1, 0)
        lo1 = face([back(x) for x in cell.u], [back(x) for x in f], back(s), cell.u, f, s)
        hi1 = [pltpu.roll(x, 2 * C - 1, 0) for x in lo1]
        mid = Cell(cut(cell.u))
        axial = axial_faces(mid, [0.0] * 5, rotor)
        force = [halo.beyond(side, 10 + k) for k in range(3)]
        new = updated(mid.u, force, axial, (cut(hi1), cut(lo1)), span)
        for k in range(5):
            row_s[side, k] = new[k]
            rows_ref[side, k] = row_s[side, k, :, pl.ds(near, LANES)]

    def load(c):
        if c < 0:
            return [halo.left(k + (5 if c == -2 else 0)) for k in range(5)]
        if c >= C:
            return [halo.right(k + (5 if c == C + 1 else 0)) for k in range(5)]
        return [u_ref[k, c] for k in range(5)]

    def edges(c):
        r = c if c >= 0 else 2 * C - 1
        return [[edge_s[side, k, r : r + 1, :] for k in range(5)] for side in range(2)]

    def force_of(c):
        if 0 <= c < C:
            return [f_ref[k, c] for k in range(3)]
        return [(halo.left if c < 0 else halo.right)(10 + k) for k in range(3)]

    slots = {-1: 0, 0: 1, C - 1: 2, C: 3}

    def store(c, u):
        for k in range(5):
            col_s[k, slots[c]] = u[k]

    axial = lambda c, cell: axial_faces(cell, [0.0] * 5, rotor)
    sweep(load, -1, 1, axial, edges, force_of, store)
    sweep(load, C - 1, C + 1, axial, edges, force_of, store)

    def half(k, c, start):
        lanes = pl.ds(start, LANES)
        if c in slots:
            return col_s[k, slots[c], :, lanes]
        return one_ref[k, c, :, lanes]

    def across(k, s0):
        lanes = pl.ds(far, LANES)
        mid = one_ref[k, :, s0, lanes]
        c = lax.broadcasted_iota(jnp.int32, mid.shape, 0)
        ends = [jnp.broadcast_to(col_s[k, slots[e], s0 : s0 + 1, lanes], mid.shape) for e in (0, C - 1)]
        return jnp.where(c == 0, ends[0], jnp.where(c == C - 1, ends[1], mid))

    for k in range(5):
        for c in range(-1, C + 1):
            near_ref[k, c + 1] = half(k, c, near)

    for side, wall in enumerate(walls(ns)):
        s0 = 0 if side == 0 else T - 1
        inner = Cell([across(k, s0) for k in range(5)])
        outer = Cell([row_s[side, k, :, pl.ds(far, LANES)] for k in range(5)])
        edge, _ = edge_faces(side, outer, inner, wall)
        for k in range(5):
            fedge_s[side, k] = edge[k]

    down = jnp.where(rotor, LANES - 1, 1)
    up = jnp.where(rotor, 1, LANES - 1)

    def far_axial(c, cell):
        for k in range(5):
            beside_ref[k, c] = pltpu.roll(cell.u[k], up, 1)
        beside = Cell([pltpu.roll(near_ref[k, c + 1], down, 1) for k in range(5)])
        return half_faces(cell, beside, rotor, False)

    def far_edges(c):
        return [[fedge_s[side, k, c : c + 1, :] for k in range(5)] for side in range(2)]

    def far_store(c, u):
        for k in range(5):
            far_ref[k, c] = u[k]

    sweep(
        lambda c: [half(k, c, far) for k in range(5)], 0, C, far_axial, far_edges,
        lambda c: [f_ref[k, c, :, pl.ds(far, LANES)] for k in range(3)], far_store,
    )


def last_kernel(
    C, T, nc, ns,
    off_ref, wt_ref, f_ref, own_ref, par_ref, near_ref, rows_ref, beside_ref, far_ref,
    out_hbm, pf_hbm,
    own_s, par_s, ht_s, one_s, edge_s, new_s, pf_ref, sem,
):
    row = lax.axis_index("row")
    rotor = row == 0
    hub, casing = walls(ns)
    width = f_ref.shape[3]
    near, far = halves(width, rotor)
    far_copy = pltpu.make_async_copy(far_ref, out_hbm.at[:, :, :, pl.ds(far, LANES)], sem.at[C])
    far_copy.start()
    periods = own_s.shape[0] // (nc * ROWS)
    depth = nc * periods
    sg = jnp.where(rotor, 1, -1)
    sgf = jnp.where(rotor, 1.0, -1.0)
    cycle = nc * C

    for copy in range(periods):
        own_s[copy * nc * ROWS : (copy + 1) * nc * ROWS, :] = own_ref[...]
        par_s[copy * nc * ROWS : (copy + 1) * nc * ROWS, :] = par_ref[...]
    shape = (depth, LANES)
    lane = lax.broadcasted_iota(jnp.int32, shape, 1)
    in_span = lax.rem(lane, T)

    def get(ref, j):
        return ref[pl.ds(j, depth, stride=ROWS), :]

    def ahead(x, k):
        if k == 0:
            return x
        a = pltpu.roll(x, (LANES - T * k) % LANES, 1)
        b = pltpu.roll(a, depth - 1, 0)
        return jnp.where(lane < LANES - T * k, a, b)

    def behind(x):
        a = pltpu.roll(x, T, 1)
        b = pltpu.roll(a, 1, 0)
        return jnp.where(lane >= T, a, b)

    def turned(x, cells):
        q = lax.div(cells, C)
        r = lax.rem(cells, C)
        y = pltpu.roll(x, lax.rem(depth - q, depth), 0)
        a = pltpu.roll(y, lax.rem(LANES - T * r, LANES), 1)
        b = pltpu.roll(a, depth - 1, 0)
        return jnp.where(lane < LANES - T * r, a, b)

    def taps(t):
        w = [jnp.full((1, LANES), wt_ref[t, k], jnp.float32) for k in range(4)]
        total = w[0] + w[1] + w[2] + w[3]
        return [x / total for x in w]

    def ghosts(xs, t, sign):
        w = taps(t)
        start = lax.rem(sign * off_ref[t] - 1 + 2 * cycle, cycle)
        out = []
        for x in xs:
            x = turned(x, start)
            g = w[0] * x
            for k in range(1, 4):
                g = g + w[k] * ahead(x, k)
            out.append(g)
        return out

    def slide(cell, ghost, sign):
        f, s = cell.flux(0)
        g = Cell(ghost)
        fg, s_g = g.flux(0)
        top = jnp.maximum(s, s_g) * sign
        return [a + b - top * (y - x) for x, a, y, b in zip(cell.u, f, ghost, fg)]

    def ring_step(ref, cell, h, sign):
        inner = Cell([get(ref, 5 + k) for k in range(5)])
        fi, si = inner.flux(0)
        f, s = cell.flux(0)
        top = jnp.maximum(s, si) * sign
        h1 = [a + b - top * (x - y) for x, a, y, b in zip(cell.u, f, inner.u, fi)]
        ax_hi = [sign * x for x in h]
        ax_lo = [sign * x for x in h1]
        f, s = cell.flux(1)
        lo = face([behind(x) for x in cell.u], [behind(x) for x in f], behind(s), cell.u, f, s)
        hi = [ahead(x, 1) for x in lo]
        f, s = cell.flux(2)
        edge = Cell([get(ref, 13 + k) for k in range(5)])
        fe, se = edge.flux(2)
        first = in_span == 0
        last = in_span == T - 1

        def prev(x, e):
            return jnp.where(first, e, pltpu.roll(x, 1, 1))

        slo = face([prev(x, e) for x, e in zip(cell.u, edge.u)], [prev(x, e) for x, e in zip(f, fe)], prev(s, se), cell.u, f, s)
        wall = wall_face(f, s, cell.u[3], -1.0)
        slo = [jnp.where(jnp.logical_and(first, hub), a, b) for a, b in zip(wall, slo)]
        top_face = face(cell.u, f, s, edge.u, fe, se)
        wall = wall_face(f, s, cell.u[3], 1.0)
        top_face = [jnp.where(casing, a, b) for a, b in zip(wall, top_face)]
        shi = [jnp.where(last, a, pltpu.roll(b, LANES - 1, 1)) for a, b in zip(top_face, slo)]
        force = [get(ref, 10 + k) for k in range(3)]
        return updated(cell.u, force, (ax_hi, ax_lo), (hi, lo), (shi, slo))

    own = Cell([get(own_s, k) for k in range(5)])
    par = Cell([get(par_s, k) for k in range(5)])
    g_own = ghosts(par.u, 0, sg)
    g_par = ghosts(own.u, 0, -sg)
    h_own = slide(own, g_own, sgf)
    h_par = slide(par, g_par, -sgf)
    g_edge = ghosts([get(par_s, 13 + k) for k in range(5)], 0, sg)
    h_edge = slide(Cell([get(own_s, 13 + k) for k in range(5)]), g_edge, sgf)
    own_new = ring_step(own_s, own, h_own, sgf)
    par_new = ring_step(par_s, par, h_par, -sgf)
    h_next = slide(Cell(own_new), ghosts(par_new, 1, sg), sgf)

    def eight(x):
        if depth == 8:
            return x
        return jnp.concatenate([x[0:7], x[depth - 1 : depth]], 0)

    tile = [eight(x) for x in h_own + h_edge + h_next]
    tile.append(jnp.zeros((8, LANES), jnp.float32))
    ht_s[...] = jnp.concatenate(tile, 0).T
    for t, h in ((0, h_own), (1, h_next)):
        for k in range(5):
            x = 0.5 * h[k][0:1, :]
            for c in range(C):
                pf_ref[t, k, c : c + 1, :] = x[:, c * T : (c + 1) * T]

    pf_copy = pltpu.make_async_copy(pf_ref, pf_hbm, sem.at[C + 1])
    pf_copy.start()

    lane = lax.broadcasted_iota(jnp.int32, (T, LANES), 1)
    end = lane == jnp.where(rotor, LANES - 1, 0)
    weight = (0.5 * STEP) * sgf

    def at_end(x, column):
        return pltpu.roll(x, jnp.where(rotor, LANES - 1 - column, (LANES - column) % LANES), 1)

    for c in range(-1, C + 1):
        sector = 0 if 0 <= c < C else (1 if c >= C else 7)
        r = (c % C) * T
        for k in range(5):
            h = at_end(ht_s[r : r + T, :], 8 * k + sector)
            one_s[k, c + 1] = near_ref[k, c + 1] - jnp.where(end, weight * h, 0.0)
    for side, wall in enumerate((hub, casing)):
        s0 = 0 if side == 0 else T - 1
        strip = ht_s[pl.ds(s0, C, stride=T), :]
        inner = Cell([one_s[k, 1 : C + 1, s0, :] for k in range(5)])
        outer = Cell([
            rows_ref[side, k] - jnp.where(end[:C], weight * at_end(strip, 40 + 8 * k), 0.0)
            for k in range(5)
        ])
        edge, _ = edge_faces(side, outer, inner, wall)
        for k in range(5):
            edge_s[side, k] = edge[k]

    def axial(c, cell):
        beside = Cell([beside_ref[k, c] for k in range(5)])
        h = [at_end(ht_s[c * T : (c + 1) * T, :], 80 + 8 * k) for k in range(5)]
        return half_faces(cell, beside, rotor, True, h)

    def edges(c):
        return [[edge_s[side, k, c : c + 1, :] for k in range(5)] for side in range(2)]

    def out_copy(c):
        return pltpu.make_async_copy(new_s.at[:, c], out_hbm.at[:, c, :, pl.ds(near, LANES)], sem.at[c])

    def store(c, u):
        for k in range(5):
            new_s[k, c] = u[k]
        out_copy(c).start()

    sweep(
        lambda c: [one_s[k, c + 1] for k in range(5)], 0, C, axial, edges,
        lambda c: [f_ref[k, c, :, pl.ds(near, LANES)] for k in range(3)], store,
    )
    far_copy.wait()
    pf_copy.wait()
    for c in range(C):
        out_copy(c).wait()


def pairs(count, first, wrap):
    route = []
    for low in range(first, count, 2):
        high = low + 1
        if high < count or wrap:
            route += [(low, high % count), (high % count, low)]
    return route


def body(density, velocity, pressure, blade_force, offsets, weights):
    C, T, A = density.shape[1:]
    nc = lax.axis_size("circ")
    ns = lax.axis_size("span")
    area = C * T
    assert area == LANES and nc % 2 == 0 and A == 2 * LANES and C == 8
    rho, v, p, force = density[0], velocity[0], pressure[0], blade_force[0]

    u, force, off, wt, sa, sb, pa, pb = call(
        functools.partial(first_kernel, C, T),
        [(5, C, T, A), (3, C, T, A), offsets, weights, (13, C, A), (13, C, A), (13, T, A), (13, T, A)],
        [pltpu.with_memory_space_constraint(x, pltpu.HBM) for x in (rho, v, p, force, offsets, weights)],
        specs=[hbm()] * 6,
        scratch=[
            pltpu.VMEM((C, T, A), jnp.float32),
            pltpu.VMEM((3, C, T, A), jnp.float32),
            pltpu.VMEM((C, T, A), jnp.float32),
            pltpu.SemaphoreType.DMA((6,)),
        ],
    )
    ha = lax.ppermute(sa, "span", pairs(ns, 0, False))
    hb = lax.ppermute(sb, "span", pairs(ns, 1, False))
    pa = lax.ppermute(pa, "circ", pairs(nc, 0, True))
    pb = lax.ppermute(pb, "circ", pairs(nc, 1, True))

    thin = 2 * 16 * (A // LANES) // 2
    m1, m2 = call(
        functools.partial(thin_kernel, C, T),
        [(ROWS + thin, LANES), (2 * ROWS + thin, LANES)],
        (u, force, ha, hb),
        scratch=[pltpu.VMEM((area, LANES), jnp.float32)],
    )
    planes = m1[:ROWS]
    m1 = lax.ppermute(m1, "circ", pairs(nc, 0, True))
    f32 = jnp.float32
    if nc == 4:
        (m2,) = call(fill_kernel, [m2.shape], (m1, m2), aliases={1: 0})
    (one,) = call(
        functools.partial(bulk_kernel, C, T, ns),
        [(5, C, T, A)],
        (u, force, ha, hb, m2),
        scratch=[pltpu.VMEM((2, 5, C, A), f32)],
        cost=pl.CostEstimate(flops=10_000_000, bytes_accessed=4_000_000, transcendentals=0),
    )
    if nc == 4:
        got = lax.ppermute(m2, "circ", pairs(nc, 1, True))
        (ring,) = call(ring_kernel, [(nc, ROWS, LANES)], (m2, got, one))
    else:
        got = lax.ppermute(m2, "circ", pairs(nc, 1, True))
        whole = lax.all_gather(planes, "circ")
        whole = jnp.concatenate([whole, whole], 0)
        ring = lax.dynamic_slice_in_dim(whole, lax.axis_index("circ"), nc, 0)
    partner = lax.ppermute(ring, "row", [(0, 1), (1, 0)])
    copies = max(1, 8 // nc)
    rows = nc * ROWS
    near, halo_rows, beside, far = call(
        functools.partial(far_kernel, C, T, ns),
        [(5, C + 2, T, LANES), (2, 5, C, LANES), (5, C, T, LANES), (5, C, T, LANES)],
        (u, force, ha, hb, pa, pb, m1, got, one, ring),
        scratch=[
            pltpu.VMEM((2, 5, 2 * C, A), f32),
            pltpu.VMEM((5, 4, T, A), f32),
            pltpu.VMEM((2, 5, C, A), f32),
            pltpu.VMEM((2, 5, C, LANES), f32),
        ],
        cost=pl.CostEstimate(flops=10_000_000, bytes_accessed=4_000_000, transcendentals=0),
    )
    state, plane_flux = call(
        functools.partial(last_kernel, C, T, nc, ns),
        [(5, C, T, A), (2, 5, C, T)],
        (off, wt, force, ring.reshape(rows, LANES), partner.reshape(rows, LANES), near, halo_rows, beside, far),
        specs=[smem(), smem()] + [vmem()] * 7,
        outs=[hbm(), hbm()],
        scratch=[
            pltpu.VMEM((copies * rows, LANES), f32),
            pltpu.VMEM((copies * rows, LANES), f32),
            pltpu.VMEM((LANES, LANES), f32),
            pltpu.VMEM((5, C + 2, T, LANES), f32),
            pltpu.VMEM((2, 5, C, LANES), f32),
            pltpu.VMEM((5, C, T, LANES), f32),
            pltpu.VMEM((2, 5, C, T), f32),
            pltpu.SemaphoreType.DMA((C + 2,)),
        ],
        limit=16,
    )
    return state[None], plane_flux[None]


def solution(mesh):
    placed = (
        P("row", "circ", "span", None),
        P("row", None, "circ", "span", None),
        P("row", "circ", "span", None),
        P("row", None, "circ", "span", None),
        P(),
        P(),
    )
    return jax.shard_map(
        body,
        mesh=mesh,
        in_specs=placed,
        out_specs=(P("row", None, "circ", "span", None), P("row", None, None, "circ", "span")),
        check_vma=False,
    )
```

```python
import functools

import jax
import jax.numpy as jnp
from jax import lax
from jax.experimental import pallas as pl
from jax.experimental.pallas import tpu as pltpu
from jax.sharding import PartitionSpec as P

GAMMA = 1.4
STEP = 0.04
INLET = (1.0, 0.5, 0.0, 0.0, 2.625)
LANES = 128
ROWS = 24


def vmem():
    return pl.BlockSpec(memory_space=pltpu.VMEM)


def hbm():
    return pl.BlockSpec(memory_space=pltpu.HBM)


def call(kernel, shapes, args, specs=None, scratch=(), aliases=None, cost=None, limit=6, outs=None):
    return pl.pallas_call(
        kernel,
        out_shape=[jax.ShapeDtypeStruct(s.shape, s.dtype) if hasattr(s, "dtype") else jax.ShapeDtypeStruct(s, jnp.float32) for s in shapes],
        in_specs=specs or [vmem()] * len(args),
        out_specs=outs or [vmem()] * len(shapes),
        scratch_shapes=list(scratch),
        input_output_aliases=aliases or {},
        cost_estimate=cost,
        compiler_params=pltpu.CompilerParams(vmem_limit_bytes=limit << 20),
    )(*args)


class Cell:
    def __init__(self, u):
        self.u = u
        rho, m0, m1, m2, en = u
        self.inv = 1.0 / rho
        kin = 0.5 * (m0 * m0 + m1 * m1 + m2 * m2) * self.inv
        self.p = (GAMMA - 1.0) * (en - kin)
        self.sound = jnp.sqrt(GAMMA * self.p * self.inv)

    def flux(self, d):
        m = self.u[1:4]
        vel = m[d] * self.inv
        f = [m[d], m[0] * vel, m[1] * vel, m[2] * vel, (self.u[4] + self.p) * vel]
        f[1 + d] = f[1 + d] + self.p
        return f, jnp.abs(vel) + self.sound


def face(ul, fl, sl, ur, fr, sr):
    top = jnp.maximum(sl, sr)
    return [a + b - top * (y - x) for x, a, y, b in zip(ul, fl, ur, fr)]


def updated(u, force, *spans):
    src = [None, u[0] * force[0], u[0] * force[1], u[0] * force[2]]
    src.append(u[1] * force[0] + u[2] * force[1] + u[3] * force[2])
    out = []
    for k in range(5):
        div = spans[0][0][k] - spans[0][1][k]
        for hi, lo in spans[1:]:
            div = div + (hi[k] - lo[k])
        new = u[k] - (0.5 * STEP) * div
        out.append(new if src[k] is None else new + STEP * src[k])
    return out


def conserved(rho, v, p):
    m = [rho * x for x in v]
    en = p / (GAMMA - 1.0) + 0.5 * rho * (v[0] * v[0] + v[1] * v[1] + v[2] * v[2])
    return [rho] + m + [en]


def inlet_flux():
    rho, m0, m1, m2, en = INLET
    p = (GAMMA - 1.0) * (en - 0.5 * (m0 * m0 + m1 * m1 + m2 * m2) / rho)
    vel = m0 / rho
    f = [m0, m0 * vel + p, m1 * vel, m2 * vel, (en + p) * vel]
    return f, abs(vel) + (GAMMA * p / rho) ** 0.5


def axial_faces(cell, slide, rotor):
    u = cell.u
    f, s = cell.flux(0)
    shape = u[0].shape
    lane = lax.broadcasted_iota(jnp.int32, shape, 1)
    last = shape[1] - 1
    first_lane = lane == 0
    last_lane = lane == last
    inf, ins = inlet_flux()

    def back(x, v):
        return jnp.where(first_lane, v, pltpu.roll(x, 1, 1))

    pu = [back(x, v) for x, v in zip(u, INLET)]
    pf = [pu[1]] + [back(x, v) for x, v in zip(f[1:], inf[1:])]
    lo = face(pu, pf, back(s, ins), u, f, s)
    stator_first = jnp.logical_and(first_lane, jnp.logical_not(rotor))
    lo = [jnp.where(stator_first, h, x) for h, x in zip(slide, lo)]
    hi = [
        jnp.where(last_lane, jnp.where(rotor, h, 2.0 * g), pltpu.roll(x, last, 1))
        for h, g, x in zip(slide, f, lo)
    ]
    return hi, lo


def wall_face(f, s, m, sign):
    zero = jnp.zeros_like(s)
    return [zero, zero, zero, 2.0 * (f[3] + sign * s * m), zero]


def place():
    row = lax.axis_index("row")
    circ = lax.axis_index("circ")
    span = lax.axis_index("span")
    return row, lax.rem(circ, 2) == 0, lax.rem(span, 2) == 0, span


def first_kernel(
    C, T,
    rho_hbm, v_hbm, p_hbm, f_hbm, off_hbm, wt_hbm,
    u_ref, f_ref, off_ref, wt_ref, sa_ref, sb_ref, pa_ref, pb_ref,
    rho_ref, v_ref, p_ref, sem,
):
    copies = [
        pltpu.make_async_copy(src, dst, sem.at[i])
        for i, (src, dst) in enumerate(
            [(rho_hbm, rho_ref), (v_hbm, v_ref), (p_hbm, p_ref), (f_hbm, f_ref), (off_hbm, off_ref), (wt_hbm, wt_ref)]
        )
    ]
    for copy in copies:
        copy.start()
    _, even_c, even_s, _ = place()
    for copy in copies:
        copy.wait()
    for c in range(C):
        u = conserved(rho_ref[c], [v_ref[k, c] for k in range(3)], p_ref[c])
        for k in range(5):
            u_ref[k, c] = u[k]

    def row(k, s):
        ref = u_ref.at[k] if k < 5 else f_ref.at[k - 5]
        return ref[:, s, :]

    def send(slot, k, low, high):
        a, b = row(k, low), row(k, high)
        sa_ref[slot] = jnp.where(even_s, b, a)
        sb_ref[slot] = jnp.where(even_s, a, b)

    for k in range(5):
        send(k, k, 0, T - 1)
        send(5 + k, k, 1, T - 2)
    for k in range(3):
        send(10 + k, 5 + k, 0, T - 1)
    near = jnp.where(even_c, C - 1, 0)
    far = jnp.where(even_c, C - 2, 1)
    for ref, n, m in ((pa_ref, near, far), (pb_ref, C - 1 - near, C - 1 - far)):
        for k in range(5):
            ref[k] = u_ref[k, n]
            ref[5 + k] = u_ref[k, m]
        for k in range(3):
            ref[10 + k] = f_ref[k, n]


def thin_kernel(C, T, u_ref, f_ref, ha_ref, hb_ref, m1_ref, m2_ref, t_ref):
    row, even_c, even_s, _ = place()
    rotor = row == 0
    width = u_ref.shape[3]
    half = pl.ds(pl.multiple_of(jnp.where(rotor, width - LANES, 0), LANES), LANES)
    end = jnp.where(rotor, LANES - 1, 0)
    second = jnp.where(rotor, LANES - 2, 1)
    lane = lax.broadcasted_iota(jnp.int32, (C * T, LANES), 1)
    t = jnp.zeros((C * T, LANES), jnp.float32)

    def put(x, j, e):
        return pltpu.roll(x, lax.rem(j - e + LANES, LANES), 1)

    for k in range(5):
        x = u_ref[k, :, :, half].reshape(C * T, LANES)
        t = jnp.where(lane == k, put(x, k, end), t)
        t = jnp.where(lane == 5 + k, put(x, 5 + k, second), t)
    for k in range(3):
        t = jnp.where(lane == 10 + k, put(f_ref[k, :, :, half].reshape(C * T, LANES), 10 + k, end), t)
    t_ref[...] = t
    small = lax.broadcasted_iota(jnp.int32, (C, LANES), 1)
    for start, is_low in ((0, True), (T - 1, False)):
        where_a = even_s if not is_low else jnp.logical_not(even_s)
        rows = pl.ds(start, C, stride=T)
        x = t_ref[rows, :]
        for k in range(5):
            h = jnp.where(where_a, ha_ref[k, :, half], hb_ref[k, :, half])
            x = jnp.where(small == 13 + k, put(h, 13 + k, end), x)
        t_ref[rows, :] = x
    planes = t_ref[...].T[:ROWS]
    m1_ref[0:ROWS, :] = planes
    m2_ref[0:ROWS, :] = planes
    m2_ref[ROWS : 2 * ROWS, :] = jnp.zeros((ROWS, LANES), jnp.float32)

    def corner(ref, base, c):
        for k in range(5):
            for side in range(2):
                where_a = even_s if side == 1 else jnp.logical_not(even_s)
                x = jnp.where(where_a, ha_ref[k, pl.ds(c, 1), :], hb_ref[k, pl.ds(c, 1), :])
                for part in range(width // LANES):
                    r = base + 16 * part + 2 * k + side
                    ref[r : r + 1, :] = x[:, part * LANES : (part + 1) * LANES]
        for part in range(width // LANES):
            r = base + 16 * part
            ref[r + 10 : r + 16, :] = jnp.zeros((6, LANES), jnp.float32)

    near = jnp.where(even_c, C - 1, 0)
    corner(m1_ref, ROWS, near)
    corner(m2_ref, 2 * ROWS, C - 1 - near)


def fill_kernel(m1_ref, m2_ref, out_ref):
    out_ref[...] = m2_ref[...]
    out_ref[ROWS : 2 * ROWS, :] = m1_ref[0:ROWS, :]


def ring_kernel(m2_ref, got_ref, after_ref, ring_ref):
    _, even, _, _ = place()
    mate = m2_ref[ROWS : 2 * ROWS, :]
    next_ = got_ref[0:ROWS, :]
    ring_ref[0] = m2_ref[0:ROWS, :]
    ring_ref[1] = jnp.where(even, mate, next_)
    ring_ref[2] = got_ref[ROWS : 2 * ROWS, :]
    ring_ref[3] = jnp.where(even, next_, mate)


class Halo:
    def __init__(self, C, ha, hb, pa, pb):
        _, self.even_c, self.even_s, _ = place()
        self.C, self.ha, self.hb, self.pa, self.pb = C, ha, hb, pa, pb

    def left(self, slot, rows=slice(None)):
        return jnp.where(self.even_c, self.pb[slot, rows, :], self.pa[slot, rows, :])

    def right(self, slot, rows=slice(None)):
        return jnp.where(self.even_c, self.pa[slot, rows, :], self.pb[slot, rows, :])

    def beyond(self, side, slot):
        where_a = self.even_s if side == 1 else jnp.logical_not(self.even_s)
        return jnp.where(where_a, self.ha[slot], self.hb[slot])


def edge_faces(side, outer, inner, at_wall):
    fo, so = outer.flux(2)
    fi, si = inner.flux(2)
    if side == 0:
        near = face(outer.u, fo, so, inner.u, fi, si)
        wall = wall_face(fi, si, inner.u[3], -1.0)
    else:
        near = face(inner.u, fi, si, outer.u, fo, so)
        wall = wall_face(fi, si, inner.u[3], 1.0)
    return [jnp.where(at_wall, w, x) for w, x in zip(wall, near)], near


def column_update(cell, circ_lo, circ_hi, axial, low_row, top_row, force):
    column = cell.u[0].shape
    T = column[0]
    srow = lax.broadcasted_iota(jnp.int32, column, 0)
    f, s = cell.flux(2)
    back = lambda x: pltpu.roll(x, 1, 0)
    lo2 = face([back(x) for x in cell.u], [back(x) for x in f], back(s), cell.u, f, s)
    lo2 = [jnp.where(srow == 0, jnp.broadcast_to(e, column), x) for e, x in zip(low_row, lo2)]
    hi2 = [
        jnp.where(srow == T - 1, jnp.broadcast_to(e, column), pltpu.roll(x, T - 1, 0))
        for e, x in zip(top_row, lo2)
    ]
    return updated(cell.u, force, axial, (circ_hi, circ_lo), (hi2, lo2))


def sweep(load, lo, hi, axial_of, edges_of, force_of, store):
    prev = Cell(load(lo - 1))
    pf, ps = prev.flux(1)
    cell = Cell(load(lo))
    cf, cs = cell.flux(1)
    h_lo = face(prev.u, pf, ps, cell.u, cf, cs)
    for c in range(lo, hi):
        nxt = Cell(load(c + 1))
        nf, ns_ = nxt.flux(1)
        h_hi = face(cell.u, cf, cs, nxt.u, nf, ns_)
        store(c, column_update(cell, h_lo, h_hi, axial_of(c, cell), *edges_of(c), force_of(c)))
        cell, cf, cs, h_lo = nxt, nf, ns_, h_hi


def walls(ns):
    span = lax.axis_index("span")
    return span == 0, span == ns - 1


def bulk_kernel(C, T, ns, u_ref, f_ref, ha_ref, hb_ref, after_ref, one_ref, edge_s):
    rotor = lax.axis_index("row") == 0
    halo = Halo(C, ha_ref, hb_ref, None, None)
    for side, wall in enumerate(walls(ns)):
        inner = Cell([u_ref[k, :, 0 if side == 0 else T - 1, :] for k in range(5)])
        outer = Cell([halo.beyond(side, k) for k in range(5)])
        edge, _ = edge_faces(side, outer, inner, wall)
        for k in range(5):
            edge_s[side, k] = edge[k]

    def axial(c, cell):
        return axial_faces(cell, [0.0] * 5, rotor)

    def edges(c):
        return [[edge_s[side, k, c : c + 1, :] for k in range(5)] for side in range(2)]

    def store(c, u):
        for k in range(5):
            one_ref[k, c] = u[k]

    sweep(lambda c: [u_ref[k, c] for k in range(5)], 1, C - 1, axial, edges, lambda c: [f_ref[k, c] for k in range(3)], store)


def half_faces(cell, beside, rotor, near, slide=None):
    f, s = cell.flux(0)
    lane = lax.broadcasted_iota(jnp.int32, s.shape, 1)
    first = lane == 0
    last = lane == LANES - 1
    inf, ins = inlet_flux()

    def back(x, v):
        return jnp.where(first, v, pltpu.roll(x, 1, 1))

    pu = [back(x, v) for x, v in zip(cell.u, INLET)]
    pf = [pu[1]] + [back(x, v) for x, v in zip(f[1:], inf[1:])]
    lo = face(pu, pf, back(s, ins), cell.u, f, s)
    fb, sb = beside.flux(0)
    sign = jnp.where(rotor, 1.0, -1.0) * (-1.0 if near else 1.0)
    top = jnp.maximum(s, sb) * sign
    mid = [a + b - top * (y - x) for x, a, y, b in zip(cell.u, f, beside.u, fb)]
    if near:
        lo = [jnp.where(first, jnp.where(rotor, m, h), x) for m, h, x in zip(mid, slide, lo)]
        hi = [jnp.where(last, jnp.where(rotor, h, m), pltpu.roll(x, LANES - 1, 1)) for m, h, x in zip(mid, slide, lo)]
    else:
        lo = [jnp.where(jnp.logical_and(first, jnp.logical_not(rotor)), m, x) for m, x in zip(mid, lo)]
        hi = [
            jnp.where(last, jnp.where(rotor, m, 2.0 * g), pltpu.roll(x, LANES - 1, 1))
            for m, g, x in zip(mid, f, lo)
        ]
    return hi, lo


def halves(width, rotor):
    near = pl.multiple_of(jnp.where(rotor, width - LANES, 0), LANES)
    return near, pl.multiple_of(width - LANES - near, LANES)


class Ring:
    def __init__(self, C, T, nc, ns, off_ref, wt_ref):
        self.C, self.T, self.nc = C, T, nc
        self.off, self.wt = off_ref, wt_ref
        self.periods = max(1, 8 // nc)
        self.depth = nc * self.periods
        self.cycle = nc * C
        self.hub, self.casing = walls(ns)
        self.lane = lax.broadcasted_iota(jnp.int32, (self.depth, LANES), 1)

    def unpack(self, scratch, message):
        rows = self.nc * ROWS
        for copy in range(self.periods):
            scratch[copy * rows : (copy + 1) * rows, :] = message[...]

    def get(self, ref, j):
        return ref[pl.ds(j, self.depth, stride=ROWS), :]

    def ahead(self, x, k):
        if k == 0:
            return x
        a = pltpu.roll(x, (LANES - self.T * k) % LANES, 1)
        b = pltpu.roll(a, self.depth - 1, 0)
        return jnp.where(self.lane < LANES - self.T * k, a, b)

    def behind(self, x):
        a = pltpu.roll(x, self.T, 1)
        b = pltpu.roll(a, 1, 0)
        return jnp.where(self.lane >= self.T, a, b)

    def turned(self, x, cells):
        q = lax.div(cells, self.C)
        r = lax.rem(cells, self.C)
        y = pltpu.roll(x, lax.rem(self.depth - q, self.depth), 0)
        a = pltpu.roll(y, lax.rem(LANES - self.T * r, LANES), 1)
        b = pltpu.roll(a, self.depth - 1, 0)
        return jnp.where(self.lane < LANES - self.T * r, a, b)

    def ghosts(self, xs, t, sign):
        w = [jnp.full((1, LANES), self.wt[t, k], jnp.float32) for k in range(4)]
        total = w[0] + w[1] + w[2] + w[3]
        w = [x / total for x in w]
        start = lax.rem(sign * self.off[t] - 1 + 2 * self.cycle, self.cycle)
        out = []
        for x in xs:
            x = self.turned(x, start)
            g = w[0] * x
            for k in range(1, 4):
                g = g + w[k] * self.ahead(x, k)
            out.append(g)
        return out

    def partial_step(self, ref, cell, sign):
        inner = Cell([self.get(ref, 5 + k) for k in range(5)])
        fi, si = inner.flux(0)
        f, s = cell.flux(0)
        top = jnp.maximum(s, si) * sign
        h1 = [sign * (a + b - top * (x - y)) for x, a, y, b in zip(cell.u, f, inner.u, fi)]
        zero = jnp.zeros_like(s)
        f, s = cell.flux(1)
        behind = self.behind
        lo = face([behind(x) for x in cell.u], [behind(x) for x in f], behind(s), cell.u, f, s)
        hi = [self.ahead(x, 1) for x in lo]
        f, s = cell.flux(2)
        edge = Cell([self.get(ref, 13 + k) for k in range(5)])
        fe, se = edge.flux(2)
        in_span = lax.rem(self.lane, self.T)
        first = in_span == 0
        last = in_span == self.T - 1

        def prev(x, e):
            return jnp.where(first, e, pltpu.roll(x, 1, 1))

        slo = face([prev(x, e) for x, e in zip(cell.u, edge.u)], [prev(x, e) for x, e in zip(f, fe)], prev(s, se), cell.u, f, s)
        wall = wall_face(f, s, cell.u[3], -1.0)
        slo = [jnp.where(jnp.logical_and(first, self.hub), a, b) for a, b in zip(wall, slo)]
        top_face = face(cell.u, f, s, edge.u, fe, se)
        wall = wall_face(f, s, cell.u[3], 1.0)
        top_face = [jnp.where(self.casing, a, b) for a, b in zip(wall, top_face)]
        shi = [jnp.where(last, a, pltpu.roll(b, LANES - 1, 1)) for a, b in zip(top_face, slo)]
        force = [self.get(ref, 10 + k) for k in range(3)]
        return updated(cell.u, force, ([zero] * 5, h1), (hi, lo), (shi, slo))


def slide(cell, ghost, sign):
    f, s = cell.flux(0)
    g = Cell(ghost)
    fg, s_g = g.flux(0)
    top = jnp.maximum(s, s_g) * sign
    return [a + b - top * (y - x) for x, a, y, b in zip(cell.u, f, ghost, fg)]


def scalar_copies(off_ref, wt_ref, off_s, wt_s, sem):
    copies = [pltpu.make_async_copy(off_ref, off_s, sem.at[0]), pltpu.make_async_copy(wt_ref, wt_s, sem.at[1])]
    for copy in copies:
        copy.start()
    return copies


def far_kernel(
    C, T, nc, ns,
    off_ref, wt_ref, u_ref, f_ref, ha_ref, hb_ref, pa_ref, pb_ref, m1_ref, m2_ref, one_ref, own_ref,
    near_ref, rows_ref, beside_ref, far_ref, pre_ref,
    edge_s, col_s, row_s, fedge_s, own_s, off_s, wt_s, small_sem,
):
    rotor = lax.axis_index("row") == 0
    width = u_ref.shape[3]
    near, far = halves(width, rotor)
    halo = Halo(C, ha_ref, hb_ref, pa_ref, pb_ref)
    scalars = scalar_copies(off_ref, wt_ref, off_s, wt_s, small_sem)

    def corner(ref, base, k, side):
        parts = [ref[pl.ds(base + 16 * q + 2 * k + side, 1), :] for q in range(width // LANES)]
        return jnp.concatenate(parts, 1)

    def corners(k, side):
        a = corner(m1_ref, ROWS, k, side)
        b = corner(m2_ref, 2 * ROWS, k, side)
        return jnp.where(halo.even_c, b, a), jnp.where(halo.even_c, a, b)

    top_rows = lax.broadcasted_iota(jnp.int32, (C, width), 0)

    def extend(mid, lf, rt):
        shape = (C, width)
        tail = jnp.where(top_rows == 0, jnp.broadcast_to(rt, shape), jnp.broadcast_to(lf, shape))
        return jnp.concatenate([mid, tail], 0)

    cut = lambda xs: [x[:C] for x in xs]
    for side, wall in enumerate(walls(ns)):
        s0 = 0 if side == 0 else T - 1
        row = pl.ds(s0, 1)
        inner = Cell([extend(u_ref[k, :, s0, :], halo.left(k, row), halo.right(k, row)) for k in range(5)])
        cell = Cell([extend(halo.beyond(side, k), *corners(k, side)) for k in range(5)])
        outer = Cell([halo.beyond(side, 5 + k) for k in range(5)])
        edge, adjoining = edge_faces(side, cell, inner, wall)
        for k in range(5):
            edge_s[side, k] = edge[k]
        f, s = cell.flux(2)
        fo, so = outer.flux(2)
        if side == 0:
            span = cut(adjoining), face(outer.u, fo, so, cut(cell.u), cut(f), s[:C])
        else:
            span = face(cut(cell.u), cut(f), s[:C], outer.u, fo, so), cut(adjoining)
        f, s = cell.flux(1)
        back = lambda x: pltpu.roll(x, 1, 0)
        lo1 = face([back(x) for x in cell.u], [back(x) for x in f], back(s), cell.u, f, s)
        hi1 = [pltpu.roll(x, 2 * C - 1, 0) for x in lo1]
        mid = Cell(cut(cell.u))
        axial = axial_faces(mid, [0.0] * 5, rotor)
        force = [halo.beyond(side, 10 + k) for k in range(3)]
        new = updated(mid.u, force, axial, (cut(hi1), cut(lo1)), span)
        for k in range(5):
            row_s[side, k] = new[k]
            rows_ref[side, k] = row_s[side, k, :, pl.ds(near, LANES)]

    def load(c):
        if c < 0:
            return [halo.left(k + (5 if c == -2 else 0)) for k in range(5)]
        if c >= C:
            return [halo.right(k + (5 if c == C + 1 else 0)) for k in range(5)]
        return [u_ref[k, c] for k in range(5)]

    def edges(c):
        r = c if c >= 0 else 2 * C - 1
        return [[edge_s[side, k, r : r + 1, :] for k in range(5)] for side in range(2)]

    def force_of(c):
        if 0 <= c < C:
            return [f_ref[k, c] for k in range(3)]
        return [(halo.left if c < 0 else halo.right)(10 + k) for k in range(3)]

    slots = {-1: 0, 0: 1, C - 1: 2, C: 3}

    def store(c, u):
        for k in range(5):
            col_s[k, slots[c]] = u[k]

    axial = lambda c, cell: axial_faces(cell, [0.0] * 5, rotor)
    sweep(load, -1, 1, axial, edges, force_of, store)
    sweep(load, C - 1, C + 1, axial, edges, force_of, store)

    def half(k, c, start):
        lanes = pl.ds(start, LANES)
        if c in slots:
            return col_s[k, slots[c], :, lanes]
        return one_ref[k, c, :, lanes]

    def across(k, s0):
        lanes = pl.ds(far, LANES)
        mid = one_ref[k, :, s0, lanes]
        c = lax.broadcasted_iota(jnp.int32, mid.shape, 0)
        ends = [jnp.broadcast_to(col_s[k, slots[e], s0 : s0 + 1, lanes], mid.shape) for e in (0, C - 1)]
        return jnp.where(c == 0, ends[0], jnp.where(c == C - 1, ends[1], mid))

    for k in range(5):
        for c in range(-1, C + 1):
            near_ref[k, c + 1] = half(k, c, near)

    for side, wall in enumerate(walls(ns)):
        s0 = 0 if side == 0 else T - 1
        inner = Cell([across(k, s0) for k in range(5)])
        outer = Cell([row_s[side, k, :, pl.ds(far, LANES)] for k in range(5)])
        edge, _ = edge_faces(side, outer, inner, wall)
        for k in range(5):
            fedge_s[side, k] = edge[k]

    down = jnp.where(rotor, LANES - 1, 1)
    up = jnp.where(rotor, 1, LANES - 1)

    def far_axial(c, cell):
        for k in range(5):
            beside_ref[k, c] = pltpu.roll(cell.u[k], up, 1)
        beside = Cell([pltpu.roll(near_ref[k, c + 1], down, 1) for k in range(5)])
        return half_faces(cell, beside, rotor, False)

    def far_edges(c):
        return [[fedge_s[side, k, c : c + 1, :] for k in range(5)] for side in range(2)]

    def far_store(c, u):
        for k in range(5):
            far_ref[k, c] = u[k]

    sweep(
        lambda c: [half(k, c, far) for k in range(5)], 0, C, far_axial, far_edges,
        lambda c: [f_ref[k, c, :, pl.ds(far, LANES)] for k in range(3)], far_store,
    )
    for copy in scalars:
        copy.wait()
    ring = Ring(C, T, nc, ns, off_s, wt_s)
    ring.unpack(own_s, own_ref)
    own = Cell([ring.get(own_s, k) for k in range(5)])
    part = ring.partial_step(own_s, own, jnp.where(rotor, 1.0, -1.0))
    ghost = ring.ghosts(own.u, 0, jnp.where(rotor, -1, 1))
    for k in range(5):
        pre_ref[k] = part[k]
        pre_ref[5 + k] = ghost[k]


def last_kernel(
    C, T, nc, ns,
    off_ref, wt_ref, f_ref, own_ref, par_ref, near_ref, rows_ref, beside_ref, pre_ref, far_ref,
    out_hbm, pf_hbm,
    own_s, par_s, ht_s, one_s, edge_s, new_s, pf_ref, off_s, wt_s, sem, small_sem,
):
    row = lax.axis_index("row")
    rotor = row == 0
    hub, casing = walls(ns)
    width = f_ref.shape[3]
    near, far = halves(width, rotor)
    scalars = scalar_copies(off_ref, wt_ref, off_s, wt_s, small_sem)
    ring = Ring(C, T, nc, ns, off_s, wt_s)
    get = ring.get
    sg = jnp.where(rotor, 1, -1)
    sgf = jnp.where(rotor, 1.0, -1.0)
    weight = (0.5 * STEP) * sgf
    ring.unpack(own_s, own_ref)
    ring.unpack(par_s, par_ref)
    own = Cell([get(own_s, k) for k in range(5)])
    par = Cell([get(par_s, k) for k in range(5)])
    h_par = slide(par, [pre_ref[5 + k] for k in range(5)], -sgf)
    par_new = ring.partial_step(par_s, par, -sgf)
    par_new = [x + weight * h for x, h in zip(par_new, h_par)]
    for copy in scalars:
        copy.wait()
    h_own = slide(own, ring.ghosts(par.u, 0, sg), sgf)
    g_edge = ring.ghosts([get(par_s, 13 + k) for k in range(5)], 0, sg)
    h_edge = slide(Cell([get(own_s, 13 + k) for k in range(5)]), g_edge, sgf)
    own_new = [pre_ref[k] - weight * h_own[k] for k in range(5)]
    h_next = slide(Cell(own_new), ring.ghosts(par_new, 1, sg), sgf)
    depth = ring.depth

    def eight(x):
        if depth == 8:
            return x
        return jnp.concatenate([x[0:7], x[depth - 1 : depth]], 0)

    tile = [eight(x) for x in h_own + h_edge + h_next]
    tile.append(jnp.zeros((8, LANES), jnp.float32))
    ht_s[...] = jnp.concatenate(tile, 0).T
    for t, h in ((0, h_own), (1, h_next)):
        for k in range(5):
            x = 0.5 * h[k][0:1, :]
            for c in range(C):
                pf_ref[t, k, c : c + 1, :] = x[:, c * T : (c + 1) * T]

    pf_copy = pltpu.make_async_copy(pf_ref, pf_hbm, small_sem.at[2])
    pf_copy.start()

    lane = lax.broadcasted_iota(jnp.int32, (T, LANES), 1)
    end = lane == jnp.where(rotor, LANES - 1, 0)

    def at_end(x, column):
        return pltpu.roll(x, jnp.where(rotor, LANES - 1 - column, (LANES - column) % LANES), 1)

    for c in range(-1, C + 1):
        sector = 0 if 0 <= c < C else (1 if c >= C else 7)
        r = (c % C) * T
        for k in range(5):
            h = at_end(ht_s[r : r + T, :], 8 * k + sector)
            one_s[k, c + 1] = near_ref[k, c + 1] - jnp.where(end, weight * h, 0.0)
    for side, wall in enumerate((hub, casing)):
        s0 = 0 if side == 0 else T - 1
        strip = ht_s[pl.ds(s0, C, stride=T), :]
        inner = Cell([one_s[k, 1 : C + 1, s0, :] for k in range(5)])
        outer = Cell([
            rows_ref[side, k] - jnp.where(end[:C], weight * at_end(strip, 40 + 8 * k), 0.0)
            for k in range(5)
        ])
        edge, _ = edge_faces(side, outer, inner, wall)
        for k in range(5):
            edge_s[side, k] = edge[k]

    def axial(c, cell):
        beside = Cell([beside_ref[k, c] for k in range(5)])
        h = [at_end(ht_s[c * T : (c + 1) * T, :], 80 + 8 * k) for k in range(5)]
        return half_faces(cell, beside, rotor, True, h)

    def edges(c):
        return [[edge_s[side, k, c : c + 1, :] for k in range(5)] for side in range(2)]

    def out_copy(k, c):
        return pltpu.make_async_copy(new_s.at[k, c], out_hbm.at[k, c], sem.at[c, k])

    def store(c, u):
        for k in range(5):
            new_s[k, c, :, pl.ds(near, LANES)] = u[k]
            new_s[k, c, :, pl.ds(far, LANES)] = far_ref[k, c]
            out_copy(k, c).start()

    sweep(
        lambda c: [one_s[k, c + 1] for k in range(5)], 0, C, axial, edges,
        lambda c: [f_ref[k, c, :, pl.ds(near, LANES)] for k in range(3)], store,
    )
    pf_copy.wait()
    for c in range(C):
        for k in range(5):
            out_copy(k, c).wait()


def pairs(count, first, wrap):
    route = []
    for low in range(first, count, 2):
        high = low + 1
        if high < count or wrap:
            route += [(low, high % count), (high % count, low)]
    return route


def body(density, velocity, pressure, blade_force, offsets, weights):
    C, T, A = density.shape[1:]
    nc = lax.axis_size("circ")
    ns = lax.axis_size("span")
    area = C * T
    assert area == LANES and nc % 2 == 0 and A == 2 * LANES and C == 8
    rho, v, p, force = density[0], velocity[0], pressure[0], blade_force[0]

    u, force, off, wt, sa, sb, pa, pb = call(
        functools.partial(first_kernel, C, T),
        [(5, C, T, A), (3, C, T, A), offsets, weights, (13, C, A), (13, C, A), (13, T, A), (13, T, A)],
        [pltpu.with_memory_space_constraint(x, pltpu.HBM) for x in (rho, v, p, force, offsets, weights)],
        specs=[hbm()] * 6,
        scratch=[
            pltpu.VMEM((C, T, A), jnp.float32),
            pltpu.VMEM((3, C, T, A), jnp.float32),
            pltpu.VMEM((C, T, A), jnp.float32),
            pltpu.SemaphoreType.DMA((6,)),
        ],
    )
    ha = lax.ppermute(sa, "span", pairs(ns, 0, False))
    hb = lax.ppermute(sb, "span", pairs(ns, 1, False))
    pa = lax.ppermute(pa, "circ", pairs(nc, 0, True))
    pb = lax.ppermute(pb, "circ", pairs(nc, 1, True))

    thin = 2 * 16 * (A // LANES) // 2
    m1, m2 = call(
        functools.partial(thin_kernel, C, T),
        [(ROWS + thin, LANES), (2 * ROWS + thin, LANES)],
        (u, force, ha, hb),
        scratch=[pltpu.VMEM((area, LANES), jnp.float32)],
    )
    planes = m1[:ROWS]
    m1 = lax.ppermute(m1, "circ", pairs(nc, 0, True))
    f32 = jnp.float32
    if nc == 4:
        (m2,) = call(fill_kernel, [m2.shape], (m1, m2), aliases={1: 0})
    (one,) = call(
        functools.partial(bulk_kernel, C, T, ns),
        [(5, C, T, A)],
        (u, force, ha, hb, m2),
        scratch=[pltpu.VMEM((2, 5, C, A), f32)],
        cost=pl.CostEstimate(flops=10_000_000, bytes_accessed=4_000_000, transcendentals=0),
    )
    if nc == 4:
        got = lax.ppermute(m2, "circ", pairs(nc, 1, True))
        (ring,) = call(ring_kernel, [(nc, ROWS, LANES)], (m2, got, one))
    else:
        got = lax.ppermute(m2, "circ", pairs(nc, 1, True))
        whole = lax.all_gather(planes, "circ")
        whole = jnp.concatenate([whole, whole], 0)
        ring = lax.dynamic_slice_in_dim(whole, lax.axis_index("circ"), nc, 0)
    partner = lax.ppermute(ring, "row", [(0, 1), (1, 0)])
    copies = max(1, 8 // nc)
    rows = nc * ROWS
    ring = ring.reshape(rows, LANES)
    near, halo_rows, beside, far, pre = call(
        functools.partial(far_kernel, C, T, nc, ns),
        [(5, C + 2, T, LANES), (2, 5, C, LANES), (5, C, T, LANES), (5, C, T, LANES), (10, copies * nc, LANES)],
        (off, wt, u, force, ha, hb, pa, pb, m1, got, one, ring),
        scratch=[
            pltpu.VMEM((2, 5, 2 * C, A), f32),
            pltpu.VMEM((5, 4, T, A), f32),
            pltpu.VMEM((2, 5, C, A), f32),
            pltpu.VMEM((2, 5, C, LANES), f32),
            pltpu.VMEM((copies * rows, LANES), f32),
            pltpu.SMEM(offsets.shape, jnp.int32),
            pltpu.SMEM(weights.shape, f32),
            pltpu.SemaphoreType.DMA((2,)),
        ],
        cost=pl.CostEstimate(flops=10_000_000, bytes_accessed=4_000_000, transcendentals=0),
    )
    state, plane_flux = call(
        functools.partial(last_kernel, C, T, nc, ns),
        [(5, C, T, A), (2, 5, C, T)],
        (off, wt, force, ring, partner.reshape(rows, LANES), near, halo_rows, beside, pre, far),
        outs=[hbm(), hbm()],
        scratch=[
            pltpu.VMEM((copies * rows, LANES), f32),
            pltpu.VMEM((copies * rows, LANES), f32),
            pltpu.VMEM((LANES, LANES), f32),
            pltpu.VMEM((5, C + 2, T, LANES), f32),
            pltpu.VMEM((2, 5, C, LANES), f32),
            pltpu.VMEM((5, C, T, A), f32),
            pltpu.VMEM((2, 5, C, T), f32),
            pltpu.SMEM(offsets.shape, jnp.int32),
            pltpu.SMEM(weights.shape, f32),
            pltpu.SemaphoreType.DMA((C, 5)),
            pltpu.SemaphoreType.DMA((3,)),
        ],
        limit=16,
    )
    return state[None], plane_flux[None]


def solution(mesh):
    placed = (
        P("row", "circ", "span", None),
        P("row", None, "circ", "span", None),
        P("row", "circ", "span", None),
        P("row", None, "circ", "span", None),
        P(),
        P(),
    )
    return jax.shard_map(
        body,
        mesh=mesh,
        in_specs=placed,
        out_specs=(P("row", None, "circ", "span", None), P("row", None, None, "circ", "span")),
        check_vma=False,
    )
```

```python
import functools

import jax
import jax.numpy as jnp
from jax import lax
from jax.experimental import pallas as pl
from jax.experimental.pallas import tpu as pltpu
from jax.sharding import PartitionSpec as P

GAMMA = 1.4
STEP = 0.04
INLET = (1.0, 0.5, 0.0, 0.0, 2.625)
LANES = 128
ROWS = 24


def vmem():
    return pl.BlockSpec(memory_space=pltpu.VMEM)


def hbm():
    return pl.BlockSpec(memory_space=pltpu.HBM)


def call(kernel, shapes, args, specs=None, scratch=(), aliases=None, cost=None, limit=6, outs=None):
    return pl.pallas_call(
        kernel,
        out_shape=[jax.ShapeDtypeStruct(s.shape, s.dtype) if hasattr(s, "dtype") else jax.ShapeDtypeStruct(s, jnp.float32) for s in shapes],
        in_specs=specs or [vmem()] * len(args),
        out_specs=outs or [vmem()] * len(shapes),
        scratch_shapes=list(scratch),
        input_output_aliases=aliases or {},
        cost_estimate=cost,
        compiler_params=pltpu.CompilerParams(vmem_limit_bytes=limit << 20),
    )(*args)


class Cell:
    def __init__(self, u):
        self.u = u
        rho, m0, m1, m2, en = u
        self.inv = 1.0 / rho
        kin = 0.5 * (m0 * m0 + m1 * m1 + m2 * m2) * self.inv
        self.p = (GAMMA - 1.0) * (en - kin)
        self.sound = jnp.sqrt(GAMMA * self.p * self.inv)

    def flux(self, d):
        m = self.u[1:4]
        vel = m[d] * self.inv
        f = [m[d], m[0] * vel, m[1] * vel, m[2] * vel, (self.u[4] + self.p) * vel]
        f[1 + d] = f[1 + d] + self.p
        return f, jnp.abs(vel) + self.sound


def face(ul, fl, sl, ur, fr, sr):
    top = jnp.maximum(sl, sr)
    return [a + b - top * (y - x) for x, a, y, b in zip(ul, fl, ur, fr)]


def updated(u, force, *spans):
    src = [None, u[0] * force[0], u[0] * force[1], u[0] * force[2]]
    src.append(u[1] * force[0] + u[2] * force[1] + u[3] * force[2])
    out = []
    for k in range(5):
        div = spans[0][0][k] - spans[0][1][k]
        for hi, lo in spans[1:]:
            div = div + (hi[k] - lo[k])
        new = u[k] - (0.5 * STEP) * div
        out.append(new if src[k] is None else new + STEP * src[k])
    return out


def conserved(rho, v, p):
    m = [rho * x for x in v]
    en = p / (GAMMA - 1.0) + 0.5 * rho * (v[0] * v[0] + v[1] * v[1] + v[2] * v[2])
    return [rho] + m + [en]


def inlet_flux():
    rho, m0, m1, m2, en = INLET
    p = (GAMMA - 1.0) * (en - 0.5 * (m0 * m0 + m1 * m1 + m2 * m2) / rho)
    vel = m0 / rho
    f = [m0, m0 * vel + p, m1 * vel, m2 * vel, (en + p) * vel]
    return f, abs(vel) + (GAMMA * p / rho) ** 0.5


def axial_faces(cell, slide, rotor):
    u = cell.u
    f, s = cell.flux(0)
    shape = u[0].shape
    lane = lax.broadcasted_iota(jnp.int32, shape, 1)
    last = shape[1] - 1
    first_lane = lane == 0
    last_lane = lane == last
    inf, ins = inlet_flux()

    def back(x, v):
        return jnp.where(first_lane, v, pltpu.roll(x, 1, 1))

    pu = [back(x, v) for x, v in zip(u, INLET)]
    pf = [pu[1]] + [back(x, v) for x, v in zip(f[1:], inf[1:])]
    lo = face(pu, pf, back(s, ins), u, f, s)
    stator_first = jnp.logical_and(first_lane, jnp.logical_not(rotor))
    lo = [jnp.where(stator_first, h, x) for h, x in zip(slide, lo)]
    hi = [
        jnp.where(last_lane, jnp.where(rotor, h, 2.0 * g), pltpu.roll(x, last, 1))
        for h, g, x in zip(slide, f, lo)
    ]
    return hi, lo


def wall_face(f, s, m, sign):
    zero = jnp.zeros_like(s)
    return [zero, zero, zero, 2.0 * (f[3] + sign * s * m), zero]


def place():
    row = lax.axis_index("row")
    circ = lax.axis_index("circ")
    span = lax.axis_index("span")
    return row, lax.rem(circ, 2) == 0, row == 0, span


def first_kernel(
    C, T,
    rho_hbm, v_hbm, p_hbm, f_hbm, off_hbm, wt_hbm,
    u_ref, f_ref, off_ref, wt_ref, sa_ref, sb_ref, pa_ref, pb_ref,
    rho_ref, v_ref, p_ref, sem,
):
    copies = [
        pltpu.make_async_copy(src, dst, sem.at[i])
        for i, (src, dst) in enumerate(
            [(rho_hbm, rho_ref), (v_hbm, v_ref), (p_hbm, p_ref), (f_hbm, f_ref), (off_hbm, off_ref), (wt_hbm, wt_ref)]
        )
    ]
    for copy in copies:
        copy.start()
    _, even_c, even_s, _ = place()
    for copy in copies:
        copy.wait()
    for c in range(C):
        u = conserved(rho_ref[c], [v_ref[k, c] for k in range(3)], p_ref[c])
        for k in range(5):
            u_ref[k, c] = u[k]

    def row(k, s):
        ref = u_ref.at[k] if k < 5 else f_ref.at[k - 5]
        return ref[:, s, :]

    def send(slot, k, low, high):
        a, b = row(k, low), row(k, high)
        sa_ref[slot] = jnp.where(even_s, b, a)
        sb_ref[slot] = jnp.where(even_s, a, b)

    for k in range(5):
        send(k, k, 0, T - 1)
        send(5 + k, k, 1, T - 2)
    for k in range(3):
        send(10 + k, 5 + k, 0, T - 1)
    near = jnp.where(even_c, C - 1, 0)
    far = jnp.where(even_c, C - 2, 1)
    for ref, n, m in ((pa_ref, near, far), (pb_ref, C - 1 - near, C - 1 - far)):
        for k in range(5):
            ref[k] = u_ref[k, n]
            ref[5 + k] = u_ref[k, m]
        for k in range(3):
            ref[10 + k] = f_ref[k, n]


def thin_kernel(C, T, u_ref, f_ref, ha_ref, hb_ref, m1_ref, m2_ref, t_ref):
    row, even_c, even_s, _ = place()
    even_s = jnp.logical_not(even_s)
    rotor = row == 0
    width = u_ref.shape[3]
    half = pl.ds(pl.multiple_of(jnp.where(rotor, width - LANES, 0), LANES), LANES)
    end = jnp.where(rotor, LANES - 1, 0)
    second = jnp.where(rotor, LANES - 2, 1)
    lane = lax.broadcasted_iota(jnp.int32, (C * T, LANES), 1)
    t = jnp.zeros((C * T, LANES), jnp.float32)

    def put(x, j, e):
        return pltpu.roll(x, lax.rem(j - e + LANES, LANES), 1)

    for k in range(5):
        x = u_ref[k, :, :, half].reshape(C * T, LANES)
        t = jnp.where(lane == k, put(x, k, end), t)
        t = jnp.where(lane == 5 + k, put(x, 5 + k, second), t)
    for k in range(3):
        t = jnp.where(lane == 10 + k, put(f_ref[k, :, :, half].reshape(C * T, LANES), 10 + k, end), t)
    t_ref[...] = t
    small = lax.broadcasted_iota(jnp.int32, (C, LANES), 1)
    for start, is_low in ((0, True), (T - 1, False)):
        where_a = even_s if not is_low else jnp.logical_not(even_s)
        rows = pl.ds(start, C, stride=T)
        x = t_ref[rows, :]
        for k in range(5):
            h = jnp.where(where_a, ha_ref[k, :, half], hb_ref[k, :, half])
            x = jnp.where(small == 13 + k, put(h, 13 + k, end), x)
        t_ref[rows, :] = x
    planes = t_ref[...].T[:ROWS]
    m1_ref[0:ROWS, :] = planes
    m2_ref[0:ROWS, :] = planes
    m2_ref[ROWS : 2 * ROWS, :] = jnp.zeros((ROWS, LANES), jnp.float32)

    def corner(ref, base, c):
        for k in range(5):
            for side in range(2):
                where_a = even_s if side == 1 else jnp.logical_not(even_s)
                x = jnp.where(where_a, ha_ref[k, pl.ds(c, 1), :], hb_ref[k, pl.ds(c, 1), :])
                for part in range(width // LANES):
                    r = base + 16 * part + 2 * k + side
                    ref[r : r + 1, :] = x[:, part * LANES : (part + 1) * LANES]
        for part in range(width // LANES):
            r = base + 16 * part
            ref[r + 10 : r + 16, :] = jnp.zeros((6, LANES), jnp.float32)

    near = jnp.where(even_c, C - 1, 0)
    corner(m1_ref, ROWS, near)
    corner(m2_ref, 2 * ROWS, C - 1 - near)


def fill_kernel(m1_ref, m2_ref, out_ref):
    out_ref[...] = m2_ref[...]
    out_ref[ROWS : 2 * ROWS, :] = m1_ref[0:ROWS, :]


def ring_kernel(m2_ref, got_ref, after_ref, ring_ref):
    _, even, _, _ = place()
    mate = m2_ref[ROWS : 2 * ROWS, :]
    next_ = got_ref[0:ROWS, :]
    ring_ref[0] = m2_ref[0:ROWS, :]
    ring_ref[1] = jnp.where(even, mate, next_)
    ring_ref[2] = got_ref[ROWS : 2 * ROWS, :]
    ring_ref[3] = jnp.where(even, next_, mate)


class Halo:
    def __init__(self, C, ha, hb, pa, pb):
        _, self.even_c, even_s, _ = place()
        self.even_s = jnp.logical_not(even_s)
        self.C, self.ha, self.hb, self.pa, self.pb = C, ha, hb, pa, pb

    def left(self, slot, rows=slice(None)):
        return jnp.where(self.even_c, self.pb[slot, rows, :], self.pa[slot, rows, :])

    def right(self, slot, rows=slice(None)):
        return jnp.where(self.even_c, self.pa[slot, rows, :], self.pb[slot, rows, :])

    def beyond(self, side, slot):
        where_a = self.even_s if side == 1 else jnp.logical_not(self.even_s)
        return jnp.where(where_a, self.ha[slot], self.hb[slot])


def edge_faces(side, outer, inner, at_wall):
    fo, so = outer.flux(2)
    fi, si = inner.flux(2)
    if side == 0:
        near = face(outer.u, fo, so, inner.u, fi, si)
        wall = wall_face(fi, si, inner.u[3], -1.0)
    else:
        near = face(inner.u, fi, si, outer.u, fo, so)
        wall = wall_face(fi, si, inner.u[3], 1.0)
    return [jnp.where(at_wall, w, x) for w, x in zip(wall, near)], near


def column_update(cell, circ_lo, circ_hi, axial, low_row, top_row, force):
    column = cell.u[0].shape
    T = column[0]
    srow = lax.broadcasted_iota(jnp.int32, column, 0)
    f, s = cell.flux(2)
    back = lambda x: pltpu.roll(x, 1, 0)
    lo2 = face([back(x) for x in cell.u], [back(x) for x in f], back(s), cell.u, f, s)
    lo2 = [jnp.where(srow == 0, jnp.broadcast_to(e, column), x) for e, x in zip(low_row, lo2)]
    hi2 = [
        jnp.where(srow == T - 1, jnp.broadcast_to(e, column), pltpu.roll(x, T - 1, 0))
        for e, x in zip(top_row, lo2)
    ]
    return updated(cell.u, force, axial, (circ_hi, circ_lo), (hi2, lo2))


def sweep(load, lo, hi, axial_of, edges_of, force_of, store):
    prev = Cell(load(lo - 1))
    pf, ps = prev.flux(1)
    cell = Cell(load(lo))
    cf, cs = cell.flux(1)
    h_lo = face(prev.u, pf, ps, cell.u, cf, cs)
    for c in range(lo, hi):
        nxt = Cell(load(c + 1))
        nf, ns_ = nxt.flux(1)
        h_hi = face(cell.u, cf, cs, nxt.u, nf, ns_)
        store(c, column_update(cell, h_lo, h_hi, axial_of(c, cell), *edges_of(c), force_of(c)))
        cell, cf, cs, h_lo = nxt, nf, ns_, h_hi


def walls(ns):
    span = lax.axis_index("span")
    return span == 0, span == ns - 1


def bulk_kernel(C, T, ns, u_ref, f_ref, ha_ref, hb_ref, after_ref, one_ref, edge_s):
    rotor = lax.axis_index("row") == 0
    halo = Halo(C, ha_ref, hb_ref, None, None)
    for side, wall in enumerate(walls(ns)):
        inner = Cell([u_ref[k, :, 0 if side == 0 else T - 1, :] for k in range(5)])
        outer = Cell([halo.beyond(side, k) for k in range(5)])
        edge, _ = edge_faces(side, outer, inner, wall)
        for k in range(5):
            edge_s[side, k] = edge[k]

    def axial(c, cell):
        return axial_faces(cell, [0.0] * 5, rotor)

    def edges(c):
        return [[edge_s[side, k, c : c + 1, :] for k in range(5)] for side in range(2)]

    def store(c, u):
        for k in range(5):
            one_ref[k, c] = u[k]

    sweep(lambda c: [u_ref[k, c] for k in range(5)], 1, C - 1, axial, edges, lambda c: [f_ref[k, c] for k in range(3)], store)


def half_faces(cell, beside, rotor, near, slide=None):
    f, s = cell.flux(0)
    lane = lax.broadcasted_iota(jnp.int32, s.shape, 1)
    first = lane == 0
    last = lane == LANES - 1
    inf, ins = inlet_flux()

    def back(x, v):
        return jnp.where(first, v, pltpu.roll(x, 1, 1))

    pu = [back(x, v) for x, v in zip(cell.u, INLET)]
    pf = [pu[1]] + [back(x, v) for x, v in zip(f[1:], inf[1:])]
    lo = face(pu, pf, back(s, ins), cell.u, f, s)
    fb, sb = beside.flux(0)
    sign = jnp.where(rotor, 1.0, -1.0) * (-1.0 if near else 1.0)
    top = jnp.maximum(s, sb) * sign
    mid = [a + b - top * (y - x) for x, a, y, b in zip(cell.u, f, beside.u, fb)]
    if near:
        lo = [jnp.where(first, jnp.where(rotor, m, h), x) for m, h, x in zip(mid, slide, lo)]
        hi = [jnp.where(last, jnp.where(rotor, h, m), pltpu.roll(x, LANES - 1, 1)) for m, h, x in zip(mid, slide, lo)]
    else:
        lo = [jnp.where(jnp.logical_and(first, jnp.logical_not(rotor)), m, x) for m, x in zip(mid, lo)]
        hi = [
            jnp.where(last, jnp.where(rotor, m, 2.0 * g), pltpu.roll(x, LANES - 1, 1))
            for m, g, x in zip(mid, f, lo)
        ]
    return hi, lo


def halves(width, rotor):
    near = pl.multiple_of(jnp.where(rotor, width - LANES, 0), LANES)
    return near, pl.multiple_of(width - LANES - near, LANES)


class Ring:
    def __init__(self, C, T, nc, ns, off_ref, wt_ref):
        self.C, self.T, self.nc = C, T, nc
        self.off, self.wt = off_ref, wt_ref
        self.periods = max(1, 8 // nc)
        self.depth = nc * self.periods
        self.cycle = nc * C
        self.hub, self.casing = walls(ns)
        self.lane = lax.broadcasted_iota(jnp.int32, (self.depth, LANES), 1)

    def unpack(self, scratch, message):
        rows = self.nc * ROWS
        for copy in range(self.periods):
            scratch[copy * rows : (copy + 1) * rows, :] = message[...]

    def get(self, ref, j):
        return ref[pl.ds(j, self.depth, stride=ROWS), :]

    def ahead(self, x, k):
        if k == 0:
            return x
        a = pltpu.roll(x, (LANES - self.T * k) % LANES, 1)
        b = pltpu.roll(a, self.depth - 1, 0)
        return jnp.where(self.lane < LANES - self.T * k, a, b)

    def behind(self, x):
        a = pltpu.roll(x, self.T, 1)
        b = pltpu.roll(a, 1, 0)
        return jnp.where(self.lane >= self.T, a, b)

    def turned(self, x, cells):
        q = lax.div(cells, self.C)
        r = lax.rem(cells, self.C)
        y = pltpu.roll(x, lax.rem(self.depth - q, self.depth), 0)
        a = pltpu.roll(y, lax.rem(LANES - self.T * r, LANES), 1)
        b = pltpu.roll(a, self.depth - 1, 0)
        return jnp.where(self.lane < LANES - self.T * r, a, b)

    def ghosts(self, xs, t, sign):
        w = [jnp.full((1, LANES), self.wt[t, k], jnp.float32) for k in range(4)]
        total = w[0] + w[1] + w[2] + w[3]
        w = [x / total for x in w]
        start = lax.rem(sign * self.off[t] - 1 + 2 * self.cycle, self.cycle)
        out = []
        for x in xs:
            x = self.turned(x, start)
            g = w[0] * x
            for k in range(1, 4):
                g = g + w[k] * self.ahead(x, k)
            out.append(g)
        return out

    def partial_step(self, ref, cell, sign):
        inner = Cell([self.get(ref, 5 + k) for k in range(5)])
        fi, si = inner.flux(0)
        f, s = cell.flux(0)
        top = jnp.maximum(s, si) * sign
        h1 = [sign * (a + b - top * (x - y)) for x, a, y, b in zip(cell.u, f, inner.u, fi)]
        zero = jnp.zeros_like(s)
        f, s = cell.flux(1)
        behind = self.behind
        lo = face([behind(x) for x in cell.u], [behind(x) for x in f], behind(s), cell.u, f, s)
        hi = [self.ahead(x, 1) for x in lo]
        f, s = cell.flux(2)
        edge = Cell([self.get(ref, 13 + k) for k in range(5)])
        fe, se = edge.flux(2)
        in_span = lax.rem(self.lane, self.T)
        first = in_span == 0
        last = in_span == self.T - 1

        def prev(x, e):
            return jnp.where(first, e, pltpu.roll(x, 1, 1))

        slo = face([prev(x, e) for x, e in zip(cell.u, edge.u)], [prev(x, e) for x, e in zip(f, fe)], prev(s, se), cell.u, f, s)
        wall = wall_face(f, s, cell.u[3], -1.0)
        slo = [jnp.where(jnp.logical_and(first, self.hub), a, b) for a, b in zip(wall, slo)]
        top_face = face(cell.u, f, s, edge.u, fe, se)
        wall = wall_face(f, s, cell.u[3], 1.0)
        top_face = [jnp.where(self.casing, a, b) for a, b in zip(wall, top_face)]
        shi = [jnp.where(last, a, pltpu.roll(b, LANES - 1, 1)) for a, b in zip(top_face, slo)]
        force = [self.get(ref, 10 + k) for k in range(3)]
        return updated(cell.u, force, ([zero] * 5, h1), (hi, lo), (shi, slo))


def slide(cell, ghost, sign):
    f, s = cell.flux(0)
    g = Cell(ghost)
    fg, s_g = g.flux(0)
    top = jnp.maximum(s, s_g) * sign
    return [a + b - top * (y - x) for x, a, y, b in zip(cell.u, f, ghost, fg)]


def scalar_copies(off_ref, wt_ref, off_s, wt_s, sem):
    copies = [pltpu.make_async_copy(off_ref, off_s, sem.at[0]), pltpu.make_async_copy(wt_ref, wt_s, sem.at[1])]
    for copy in copies:
        copy.start()
    return copies


def far_kernel(
    C, T, nc, ns,
    off_ref, wt_ref, u_ref, f_ref, ha_ref, hb_ref, pa_ref, pb_ref, m1_ref, m2_ref, one_ref, own_ref,
    near_ref, rows_ref, beside_ref, far_ref, pre_ref,
    edge_s, col_s, row_s, fedge_s, own_s, off_s, wt_s, small_sem,
):
    rotor = lax.axis_index("row") == 0
    width = u_ref.shape[3]
    near, far = halves(width, rotor)
    halo = Halo(C, ha_ref, hb_ref, pa_ref, pb_ref)
    scalars = scalar_copies(off_ref, wt_ref, off_s, wt_s, small_sem)

    def corner(ref, base, k, side):
        parts = [ref[pl.ds(base + 16 * q + 2 * k + side, 1), :] for q in range(width // LANES)]
        return jnp.concatenate(parts, 1)

    def corners(k, side):
        a = corner(m1_ref, ROWS, k, side)
        b = corner(m2_ref, 2 * ROWS, k, side)
        return jnp.where(halo.even_c, b, a), jnp.where(halo.even_c, a, b)

    top_rows = lax.broadcasted_iota(jnp.int32, (C, width), 0)

    def extend(mid, lf, rt):
        shape = (C, width)
        tail = jnp.where(top_rows == 0, jnp.broadcast_to(rt, shape), jnp.broadcast_to(lf, shape))
        return jnp.concatenate([mid, tail], 0)

    cut = lambda xs: [x[:C] for x in xs]
    for side, wall in enumerate(walls(ns)):
        s0 = 0 if side == 0 else T - 1
        row = pl.ds(s0, 1)
        inner = Cell([extend(u_ref[k, :, s0, :], halo.left(k, row), halo.right(k, row)) for k in range(5)])
        cell = Cell([extend(halo.beyond(side, k), *corners(k, side)) for k in range(5)])
        outer = Cell([halo.beyond(side, 5 + k) for k in range(5)])
        edge, adjoining = edge_faces(side, cell, inner, wall)
        for k in range(5):
            edge_s[side, k] = edge[k]
        f, s = cell.flux(2)
        fo, so = outer.flux(2)
        if side == 0:
            span = cut(adjoining), face(outer.u, fo, so, cut(cell.u), cut(f), s[:C])
        else:
            span = face(cut(cell.u), cut(f), s[:C], outer.u, fo, so), cut(adjoining)
        f, s = cell.flux(1)
        back = lambda x: pltpu.roll(x, 1, 0)
        lo1 = face([back(x) for x in cell.u], [back(x) for x in f], back(s), cell.u, f, s)
        hi1 = [pltpu.roll(x, 2 * C - 1, 0) for x in lo1]
        mid = Cell(cut(cell.u))
        axial = axial_faces(mid, [0.0] * 5, rotor)
        force = [halo.beyond(side, 10 + k) for k in range(3)]
        new = updated(mid.u, force, axial, (cut(hi1), cut(lo1)), span)
        for k in range(5):
            row_s[side, k] = new[k]
            rows_ref[side, k] = row_s[side, k, :, pl.ds(near, LANES)]

    def load(c):
        if c < 0:
            return [halo.left(k + (5 if c == -2 else 0)) for k in range(5)]
        if c >= C:
            return [halo.right(k + (5 if c == C + 1 else 0)) for k in range(5)]
        return [u_ref[k, c] for k in range(5)]

    def edges(c):
        r = c if c >= 0 else 2 * C - 1
        return [[edge_s[side, k, r : r + 1, :] for k in range(5)] for side in range(2)]

    def force_of(c):
        if 0 <= c < C:
            return [f_ref[k, c] for k in range(3)]
        return [(halo.left if c < 0 else halo.right)(10 + k) for k in range(3)]

    slots = {-1: 0, 0: 1, C - 1: 2, C: 3}

    def store(c, u):
        for k in range(5):
            col_s[k, slots[c]] = u[k]

    axial = lambda c, cell: axial_faces(cell, [0.0] * 5, rotor)
    sweep(load, -1, 1, axial, edges, force_of, store)
    sweep(load, C - 1, C + 1, axial, edges, force_of, store)

    def half(k, c, start):
        lanes = pl.ds(start, LANES)
        if c in slots:
            return col_s[k, slots[c], :, lanes]
        return one_ref[k, c, :, lanes]

    def across(k, s0):
        lanes = pl.ds(far, LANES)
        mid = one_ref[k, :, s0, lanes]
        c = lax.broadcasted_iota(jnp.int32, mid.shape, 0)
        ends = [jnp.broadcast_to(col_s[k, slots[e], s0 : s0 + 1, lanes], mid.shape) for e in (0, C - 1)]
        return jnp.where(c == 0, ends[0], jnp.where(c == C - 1, ends[1], mid))

    for k in range(5):
        for c in range(-1, C + 1):
            near_ref[k, c + 1] = half(k, c, near)

    for side, wall in enumerate(walls(ns)):
        s0 = 0 if side == 0 else T - 1
        inner = Cell([across(k, s0) for k in range(5)])
        outer = Cell([row_s[side, k, :, pl.ds(far, LANES)] for k in range(5)])
        edge, _ = edge_faces(side, outer, inner, wall)
        for k in range(5):
            fedge_s[side, k] = edge[k]

    down = jnp.where(rotor, LANES - 1, 1)
    up = jnp.where(rotor, 1, LANES - 1)

    def far_axial(c, cell):
        for k in range(5):
            beside_ref[k, c] = pltpu.roll(cell.u[k], up, 1)
        beside = Cell([pltpu.roll(near_ref[k, c + 1], down, 1) for k in range(5)])
        return half_faces(cell, beside, rotor, False)

    def far_edges(c):
        return [[fedge_s[side, k, c : c + 1, :] for k in range(5)] for side in range(2)]

    def far_store(c, u):
        for k in range(5):
            far_ref[k, c] = u[k]

    sweep(
        lambda c: [half(k, c, far) for k in range(5)], 0, C, far_axial, far_edges,
        lambda c: [f_ref[k, c, :, pl.ds(far, LANES)] for k in range(3)], far_store,
    )
    for copy in scalars:
        copy.wait()
    ring = Ring(C, T, nc, ns, off_s, wt_s)
    ring.unpack(own_s, own_ref)
    own = Cell([ring.get(own_s, k) for k in range(5)])
    part = ring.partial_step(own_s, own, jnp.where(rotor, 1.0, -1.0))
    ghost = ring.ghosts(own.u, 0, jnp.where(rotor, -1, 1))
    for k in range(5):
        pre_ref[k] = part[k]
        pre_ref[5 + k] = ghost[k]


def last_kernel(
    C, T, nc, ns,
    off_ref, wt_ref, f_ref, own_ref, par_ref, near_ref, rows_ref, beside_ref, pre_ref, far_ref,
    out_hbm, pf_hbm,
    own_s, par_s, ht_s, one_s, edge_s, new_s, pf_ref, off_s, wt_s, sem, small_sem,
):
    row = lax.axis_index("row")
    rotor = row == 0
    hub, casing = walls(ns)
    width = f_ref.shape[3]
    near, far = halves(width, rotor)
    scalars = scalar_copies(off_ref, wt_ref, off_s, wt_s, small_sem)
    ring = Ring(C, T, nc, ns, off_s, wt_s)
    get = ring.get
    sg = jnp.where(rotor, 1, -1)
    sgf = jnp.where(rotor, 1.0, -1.0)
    weight = (0.5 * STEP) * sgf
    ring.unpack(own_s, own_ref)
    ring.unpack(par_s, par_ref)
    own = Cell([get(own_s, k) for k in range(5)])
    par = Cell([get(par_s, k) for k in range(5)])
    h_par = slide(par, [pre_ref[5 + k] for k in range(5)], -sgf)
    par_new = ring.partial_step(par_s, par, -sgf)
    par_new = [x + weight * h for x, h in zip(par_new, h_par)]
    for copy in scalars:
        copy.wait()
    h_own = slide(own, ring.ghosts(par.u, 0, sg), sgf)
    g_edge = ring.ghosts([get(par_s, 13 + k) for k in range(5)], 0, sg)
    h_edge = slide(Cell([get(own_s, 13 + k) for k in range(5)]), g_edge, sgf)
    own_new = [pre_ref[k] - weight * h_own[k] for k in range(5)]
    h_next = slide(Cell(own_new), ring.ghosts(par_new, 1, sg), sgf)
    depth = ring.depth

    def eight(x):
        if depth == 8:
            return x
        return jnp.concatenate([x[0:7], x[depth - 1 : depth]], 0)

    tile = [eight(x) for x in h_own + h_edge + h_next]
    tile.append(jnp.zeros((8, LANES), jnp.float32))
    ht_s[...] = jnp.concatenate(tile, 0).T
    for t, h in ((0, h_own), (1, h_next)):
        for k in range(5):
            x = 0.5 * h[k][0:1, :]
            for c in range(C):
                pf_ref[t, k, c : c + 1, :] = x[:, c * T : (c + 1) * T]

    pf_copy = pltpu.make_async_copy(pf_ref, pf_hbm, small_sem.at[2])
    pf_copy.start()

    lane = lax.broadcasted_iota(jnp.int32, (T, LANES), 1)
    end = lane == jnp.where(rotor, LANES - 1, 0)

    def at_end(x, column):
        return pltpu.roll(x, jnp.where(rotor, LANES - 1 - column, (LANES - column) % LANES), 1)

    for c in range(-1, C + 1):
        sector = 0 if 0 <= c < C else (1 if c >= C else 7)
        r = (c % C) * T
        for k in range(5):
            h = at_end(ht_s[r : r + T, :], 8 * k + sector)
            one_s[k, c + 1] = near_ref[k, c + 1] - jnp.where(end, weight * h, 0.0)
    for side, wall in enumerate((hub, casing)):
        s0 = 0 if side == 0 else T - 1
        strip = ht_s[pl.ds(s0, C, stride=T), :]
        inner = Cell([one_s[k, 1 : C + 1, s0, :] for k in range(5)])
        outer = Cell([
            rows_ref[side, k] - jnp.where(end[:C], weight * at_end(strip, 40 + 8 * k), 0.0)
            for k in range(5)
        ])
        edge, _ = edge_faces(side, outer, inner, wall)
        for k in range(5):
            edge_s[side, k] = edge[k]

    def axial(c, cell):
        beside = Cell([beside_ref[k, c] for k in range(5)])
        h = [at_end(ht_s[c * T : (c + 1) * T, :], 80 + 8 * k) for k in range(5)]
        return half_faces(cell, beside, rotor, True, h)

    def edges(c):
        return [[edge_s[side, k, c : c + 1, :] for k in range(5)] for side in range(2)]

    def out_copy(k, c):
        return pltpu.make_async_copy(new_s.at[k, c], out_hbm.at[k, c], sem.at[c, k])

    def store(c, u):
        for k in range(5):
            new_s[k, c, :, pl.ds(near, LANES)] = u[k]
            new_s[k, c, :, pl.ds(far, LANES)] = far_ref[k, c]
            out_copy(k, c).start()

    sweep(
        lambda c: [one_s[k, c + 1] for k in range(5)], 0, C, axial, edges,
        lambda c: [f_ref[k, c, :, pl.ds(near, LANES)] for k in range(3)], store,
    )
    pf_copy.wait()
    for c in range(C):
        for k in range(5):
            out_copy(k, c).wait()


def pairs(count, first, wrap):
    route = []
    for low in range(first, count, 2):
        high = low + 1
        if high < count or wrap:
            route += [(low, high % count), (high % count, low)]
    return route


def snake(count, turn):
    order = [span for span in range(count)] + [2 * count - 1 - span for span in range(count)]
    n = len(order)
    return [(order[i], order[(i + turn) % n]) for i in range(n)]


def body(density, velocity, pressure, blade_force, offsets, weights):
    C, T, A = density.shape[1:]
    nc = lax.axis_size("circ")
    ns = lax.axis_size("span")
    area = C * T
    assert area == LANES and nc % 2 == 0 and A == 2 * LANES and C == 8
    rho, v, p, force = density[0], velocity[0], pressure[0], blade_force[0]

    u, force, off, wt, sa, sb, pa, pb = call(
        functools.partial(first_kernel, C, T),
        [(5, C, T, A), (3, C, T, A), offsets, weights, (13, C, A), (13, C, A), (13, T, A), (13, T, A)],
        [pltpu.with_memory_space_constraint(x, pltpu.HBM) for x in (rho, v, p, force, offsets, weights)],
        specs=[hbm()] * 6,
        scratch=[
            pltpu.VMEM((C, T, A), jnp.float32),
            pltpu.VMEM((3, C, T, A), jnp.float32),
            pltpu.VMEM((C, T, A), jnp.float32),
            pltpu.SemaphoreType.DMA((6,)),
        ],
    )
    ha = lax.ppermute(sa, ("row", "span"), snake(ns, 1))
    hb = lax.ppermute(sb, ("row", "span"), snake(ns, -1))
    pa = lax.ppermute(pa, "circ", pairs(nc, 0, True))
    pb = lax.ppermute(pb, "circ", pairs(nc, 1, True))

    thin = 2 * 16 * (A // LANES) // 2
    m1, m2 = call(
        functools.partial(thin_kernel, C, T),
        [(ROWS + thin, LANES), (2 * ROWS + thin, LANES)],
        (u, force, ha, hb),
        scratch=[pltpu.VMEM((area, LANES), jnp.float32)],
    )
    planes = m1[:ROWS]
    m1 = lax.ppermute(m1, "circ", pairs(nc, 0, True))
    f32 = jnp.float32
    if nc == 4:
        (m2,) = call(fill_kernel, [m2.shape], (m1, m2), aliases={1: 0})
    (one,) = call(
        functools.partial(bulk_kernel, C, T, ns),
        [(5, C, T, A)],
        (u, force, ha, hb, m2),
        scratch=[pltpu.VMEM((2, 5, C, A), f32)],
        cost=pl.CostEstimate(flops=10_000_000, bytes_accessed=4_000_000, transcendentals=0),
    )
    if nc == 4:
        got = lax.ppermute(m2, "circ", pairs(nc, 1, True))
        (ring,) = call(ring_kernel, [(nc, ROWS, LANES)], (m2, got, one))
    else:
        got = lax.ppermute(m2, "circ", pairs(nc, 1, True))
        whole = lax.all_gather(planes, "circ")
        whole = jnp.concatenate([whole, whole], 0)
        ring = lax.dynamic_slice_in_dim(whole, lax.axis_index("circ"), nc, 0)
    partner = lax.ppermute(ring, "row", [(0, 1), (1, 0)])
    copies = max(1, 8 // nc)
    rows = nc * ROWS
    ring = ring.reshape(rows, LANES)
    near, halo_rows, beside, far, pre = call(
        functools.partial(far_kernel, C, T, nc, ns),
        [(5, C + 2, T, LANES), (2, 5, C, LANES), (5, C, T, LANES), (5, C, T, LANES), (10, copies * nc, LANES)],
        (off, wt, u, force, ha, hb, pa, pb, m1, got, one, ring),
        scratch=[
            pltpu.VMEM((2, 5, 2 * C, A), f32),
            pltpu.VMEM((5, 4, T, A), f32),
            pltpu.VMEM((2, 5, C, A), f32),
            pltpu.VMEM((2, 5, C, LANES), f32),
            pltpu.VMEM((copies * rows, LANES), f32),
            pltpu.SMEM(offsets.shape, jnp.int32),
            pltpu.SMEM(weights.shape, f32),
            pltpu.SemaphoreType.DMA((2,)),
        ],
        cost=pl.CostEstimate(flops=10_000_000, bytes_accessed=4_000_000, transcendentals=0),
    )
    state, plane_flux = call(
        functools.partial(last_kernel, C, T, nc, ns),
        [(5, C, T, A), (2, 5, C, T)],
        (off, wt, force, ring, partner.reshape(rows, LANES), near, halo_rows, beside, pre, far),
        outs=[hbm(), hbm()],
        scratch=[
            pltpu.VMEM((copies * rows, LANES), f32),
            pltpu.VMEM((copies * rows, LANES), f32),
            pltpu.VMEM((LANES, LANES), f32),
            pltpu.VMEM((5, C + 2, T, LANES), f32),
            pltpu.VMEM((2, 5, C, LANES), f32),
            pltpu.VMEM((5, C, T, A), f32),
            pltpu.VMEM((2, 5, C, T), f32),
            pltpu.SMEM(offsets.shape, jnp.int32),
            pltpu.SMEM(weights.shape, f32),
            pltpu.SemaphoreType.DMA((C, 5)),
            pltpu.SemaphoreType.DMA((3,)),
        ],
        limit=16,
    )
    return state[None], plane_flux[None]


def solution(mesh):
    placed = (
        P("row", "circ", "span", None),
        P("row", None, "circ", "span", None),
        P("row", "circ", "span", None),
        P("row", None, "circ", "span", None),
        P(),
        P(),
    )
    return jax.shard_map(
        body,
        mesh=mesh,
        in_specs=placed,
        out_specs=(P("row", None, "circ", "span", None), P("row", None, None, "circ", "span")),
        check_vma=False,
    )
```

```python
import functools

import jax
import jax.numpy as jnp
from jax import lax
from jax.experimental import pallas as pl
from jax.experimental.pallas import tpu as pltpu
from jax.sharding import PartitionSpec as P

GAMMA = 1.4
STEP = 0.04
INLET = (1.0, 0.5, 0.0, 0.0, 2.625)
LANES = 128
ROWS = 24


def vmem():
    return pl.BlockSpec(memory_space=pltpu.VMEM)


def hbm():
    return pl.BlockSpec(memory_space=pltpu.HBM)


def call(kernel, shapes, args, specs=None, scratch=(), aliases=None, cost=None, limit=6, outs=None):
    return pl.pallas_call(
        kernel,
        out_shape=[jax.ShapeDtypeStruct(s.shape, s.dtype) if hasattr(s, "dtype") else jax.ShapeDtypeStruct(s, jnp.float32) for s in shapes],
        in_specs=specs or [vmem()] * len(args),
        out_specs=outs or [vmem()] * len(shapes),
        scratch_shapes=list(scratch),
        input_output_aliases=aliases or {},
        cost_estimate=cost,
        compiler_params=pltpu.CompilerParams(vmem_limit_bytes=limit << 20),
    )(*args)


class Cell:
    def __init__(self, u):
        self.u = u
        rho, m0, m1, m2, en = u
        self.inv = 1.0 / rho
        kin = 0.5 * (m0 * m0 + m1 * m1 + m2 * m2) * self.inv
        self.p = (GAMMA - 1.0) * (en - kin)
        self.sound = jnp.sqrt(GAMMA * self.p * self.inv)

    def flux(self, d):
        m = self.u[1:4]
        vel = m[d] * self.inv
        f = [m[d], m[0] * vel, m[1] * vel, m[2] * vel, (self.u[4] + self.p) * vel]
        f[1 + d] = f[1 + d] + self.p
        return f, jnp.abs(vel) + self.sound


def face(ul, fl, sl, ur, fr, sr):
    top = jnp.maximum(sl, sr)
    return [a + b - top * (y - x) for x, a, y, b in zip(ul, fl, ur, fr)]


def updated(u, force, *spans):
    src = [None, u[0] * force[0], u[0] * force[1], u[0] * force[2]]
    src.append(u[1] * force[0] + u[2] * force[1] + u[3] * force[2])
    out = []
    for k in range(5):
        div = spans[0][0][k] - spans[0][1][k]
        for hi, lo in spans[1:]:
            div = div + (hi[k] - lo[k])
        new = u[k] - (0.5 * STEP) * div
        out.append(new if src[k] is None else new + STEP * src[k])
    return out


def conserved(rho, v, p):
    m = [rho * x for x in v]
    en = p / (GAMMA - 1.0) + 0.5 * rho * (v[0] * v[0] + v[1] * v[1] + v[2] * v[2])
    return [rho] + m + [en]


def inlet_flux():
    rho, m0, m1, m2, en = INLET
    p = (GAMMA - 1.0) * (en - 0.5 * (m0 * m0 + m1 * m1 + m2 * m2) / rho)
    vel = m0 / rho
    f = [m0, m0 * vel + p, m1 * vel, m2 * vel, (en + p) * vel]
    return f, abs(vel) + (GAMMA * p / rho) ** 0.5


def axial_faces(cell, slide, rotor):
    u = cell.u
    f, s = cell.flux(0)
    shape = u[0].shape
    lane = lax.broadcasted_iota(jnp.int32, shape, 1)
    last = shape[1] - 1
    first_lane = lane == 0
    last_lane = lane == last
    inf, ins = inlet_flux()

    def back(x, v):
        return jnp.where(first_lane, v, pltpu.roll(x, 1, 1))

    pu = [back(x, v) for x, v in zip(u, INLET)]
    pf = [pu[1]] + [back(x, v) for x, v in zip(f[1:], inf[1:])]
    lo = face(pu, pf, back(s, ins), u, f, s)
    stator_first = jnp.logical_and(first_lane, jnp.logical_not(rotor))
    lo = [jnp.where(stator_first, h, x) for h, x in zip(slide, lo)]
    hi = [
        jnp.where(last_lane, jnp.where(rotor, h, 2.0 * g), pltpu.roll(x, last, 1))
        for h, g, x in zip(slide, f, lo)
    ]
    return hi, lo


def wall_face(f, s, m, sign):
    zero = jnp.zeros_like(s)
    return [zero, zero, zero, 2.0 * (f[3] + sign * s * m), zero]


def place():
    row = lax.axis_index("row")
    circ = lax.axis_index("circ")
    span = lax.axis_index("span")
    return row, lax.rem(circ, 2) == 0, row == 0, span


def first_kernel(
    C, T,
    rho_hbm, v_hbm, p_hbm, f_hbm, off_hbm, wt_hbm,
    u_ref, f_ref, off_ref, wt_ref, ta_ref, tb_ref, sa_ref, sb_ref, pa_ref, pb_ref,
    rho_ref, v_ref, p_ref, sem,
):
    copies = [
        pltpu.make_async_copy(src, dst, sem.at[i])
        for i, (src, dst) in enumerate(
            [(rho_hbm, rho_ref), (v_hbm, v_ref), (p_hbm, p_ref), (f_hbm, f_ref), (off_hbm, off_ref), (wt_hbm, wt_ref)]
        )
    ]
    for copy in copies:
        copy.start()
    _, even_c, even_s, _ = place()
    for copy in copies:
        copy.wait()
    for c in range(C):
        u = conserved(rho_ref[c], [v_ref[k, c] for k in range(3)], p_ref[c])
        for k in range(5):
            u_ref[k, c] = u[k]

    rotor = lax.axis_index("row") == 0
    width = u_ref.shape[3]
    half = pl.ds(pl.multiple_of(jnp.where(rotor, width - LANES, 0), LANES), LANES)
    end = jnp.where(rotor, LANES - 1, 0)
    small = lax.broadcasted_iota(jnp.int32, (C, LANES), 1)

    def pick(ref, rows, low, high):
        ref[0][rows, :] = jnp.where(even_s, high, low)
        ref[1][rows, :] = jnp.where(even_s, low, high)

    thin = ta_ref, tb_ref
    tiles = []
    for s in (0, T - 1):
        tile = jnp.zeros((C, LANES), jnp.float32)
        for k in range(5):
            x = pltpu.roll(u_ref[k, :, s, half], lax.rem(13 + k - end + LANES, LANES), 1)
            tile = jnp.where(small == 13 + k, x, tile)
        tiles.append(tile)
    pick(thin, slice(0, C), *tiles)
    for part in range(width // LANES):
        lanes = slice(part * LANES, (part + 1) * LANES)
        base = C + 16 * part
        for k in range(5):
            for e, c in enumerate((0, C - 1)):
                r = base + 2 * k + e
                pick(thin, slice(r, r + 1), u_ref[k, c, 0:1, lanes], u_ref[k, c, T - 1 : T, lanes])
        zero = jnp.zeros((6, LANES), jnp.float32)
        pick(thin, slice(base + 10, base + 16), zero, zero)

    def row(k, s):
        ref = u_ref.at[k] if k < 5 else f_ref.at[k - 5]
        return ref[:, s, :]

    def send(slot, k, low, high):
        a, b = row(k, low), row(k, high)
        sa_ref[slot] = jnp.where(even_s, b, a)
        sb_ref[slot] = jnp.where(even_s, a, b)

    for k in range(5):
        send(k, k, 0, T - 1)
        send(5 + k, k, 1, T - 2)
    for k in range(3):
        send(10 + k, 5 + k, 0, T - 1)
    near = jnp.where(even_c, C - 1, 0)
    far = jnp.where(even_c, C - 2, 1)
    for ref, n, m in ((pa_ref, near, far), (pb_ref, C - 1 - near, C - 1 - far)):
        for k in range(5):
            ref[k] = u_ref[k, n]
            ref[5 + k] = u_ref[k, m]
        for k in range(3):
            ref[10 + k] = f_ref[k, n]


def thin_kernel(C, T, u_ref, f_ref, ha_ref, hb_ref, m1_ref, m2_ref, t_ref):
    row, even_c, even_s, _ = place()
    even_s = jnp.logical_not(even_s)
    rotor = row == 0
    width = u_ref.shape[3]
    half = pl.ds(pl.multiple_of(jnp.where(rotor, width - LANES, 0), LANES), LANES)
    end = jnp.where(rotor, LANES - 1, 0)
    second = jnp.where(rotor, LANES - 2, 1)
    lane = lax.broadcasted_iota(jnp.int32, (C * T, LANES), 1)
    t = jnp.zeros((C * T, LANES), jnp.float32)

    def put(x, j, e):
        return pltpu.roll(x, lax.rem(j - e + LANES, LANES), 1)

    for k in range(5):
        x = u_ref[k, :, :, half].reshape(C * T, LANES)
        t = jnp.where(lane == k, put(x, k, end), t)
        t = jnp.where(lane == 5 + k, put(x, 5 + k, second), t)
    for k in range(3):
        t = jnp.where(lane == 10 + k, put(f_ref[k, :, :, half].reshape(C * T, LANES), 10 + k, end), t)
    t_ref[...] = t
    small = lax.broadcasted_iota(jnp.int32, (C, LANES), 1)
    for start, is_low in ((0, True), (T - 1, False)):
        where_a = even_s if not is_low else jnp.logical_not(even_s)
        rows = pl.ds(start, C, stride=T)
        x = jnp.where(where_a, ha_ref[0:C, :], hb_ref[0:C, :])
        edge_lane = jnp.logical_and(small >= 13, small < 18)
        t_ref[rows, :] = jnp.where(edge_lane, x, t_ref[rows, :])
    planes = t_ref[...].T[:ROWS]
    m1_ref[0:ROWS, :] = planes
    m2_ref[0:ROWS, :] = planes
    m2_ref[ROWS : 2 * ROWS, :] = jnp.zeros((ROWS, LANES), jnp.float32)

    def corner(ref, base, c):
        for k in range(5):
            for side in range(2):
                where_a = even_s if side == 1 else jnp.logical_not(even_s)
                for part in range(width // LANES):
                    r = base + 16 * part + 2 * k + side
                    q = pl.ds(C + 16 * part + 2 * k + jnp.where(c == 0, 0, 1), 1)
                    ref[r : r + 1, :] = jnp.where(where_a, ha_ref[q, :], hb_ref[q, :])
        for part in range(width // LANES):
            r = base + 16 * part
            ref[r + 10 : r + 16, :] = jnp.zeros((6, LANES), jnp.float32)

    near = jnp.where(even_c, C - 1, 0)
    corner(m1_ref, ROWS, near)
    corner(m2_ref, 2 * ROWS, C - 1 - near)


def fill_kernel(m1_ref, m2_ref, out_ref):
    out_ref[...] = m2_ref[...]
    out_ref[ROWS : 2 * ROWS, :] = m1_ref[0:ROWS, :]


def ring_kernel(m2_ref, got_ref, after_ref, ring_ref):
    _, even, _, _ = place()
    mate = m2_ref[ROWS : 2 * ROWS, :]
    next_ = got_ref[0:ROWS, :]
    ring_ref[0] = m2_ref[0:ROWS, :]
    ring_ref[1] = jnp.where(even, mate, next_)
    ring_ref[2] = got_ref[ROWS : 2 * ROWS, :]
    ring_ref[3] = jnp.where(even, next_, mate)


class Halo:
    def __init__(self, C, ha, hb, pa, pb):
        _, self.even_c, even_s, _ = place()
        self.even_s = jnp.logical_not(even_s)
        self.C, self.ha, self.hb, self.pa, self.pb = C, ha, hb, pa, pb

    def left(self, slot, rows=slice(None)):
        return jnp.where(self.even_c, self.pb[slot, rows, :], self.pa[slot, rows, :])

    def right(self, slot, rows=slice(None)):
        return jnp.where(self.even_c, self.pa[slot, rows, :], self.pb[slot, rows, :])

    def beyond(self, side, slot):
        where_a = self.even_s if side == 1 else jnp.logical_not(self.even_s)
        return jnp.where(where_a, self.ha[slot], self.hb[slot])


def edge_faces(side, outer, inner, at_wall):
    fo, so = outer.flux(2)
    fi, si = inner.flux(2)
    if side == 0:
        near = face(outer.u, fo, so, inner.u, fi, si)
        wall = wall_face(fi, si, inner.u[3], -1.0)
    else:
        near = face(inner.u, fi, si, outer.u, fo, so)
        wall = wall_face(fi, si, inner.u[3], 1.0)
    return [jnp.where(at_wall, w, x) for w, x in zip(wall, near)], near


def column_update(cell, circ_lo, circ_hi, axial, low_row, top_row, force):
    column = cell.u[0].shape
    T = column[0]
    srow = lax.broadcasted_iota(jnp.int32, column, 0)
    f, s = cell.flux(2)
    back = lambda x: pltpu.roll(x, 1, 0)
    lo2 = face([back(x) for x in cell.u], [back(x) for x in f], back(s), cell.u, f, s)
    lo2 = [jnp.where(srow == 0, jnp.broadcast_to(e, column), x) for e, x in zip(low_row, lo2)]
    hi2 = [
        jnp.where(srow == T - 1, jnp.broadcast_to(e, column), pltpu.roll(x, T - 1, 0))
        for e, x in zip(top_row, lo2)
    ]
    return updated(cell.u, force, axial, (circ_hi, circ_lo), (hi2, lo2))


def sweep(load, lo, hi, axial_of, edges_of, force_of, store):
    prev = Cell(load(lo - 1))
    pf, ps = prev.flux(1)
    cell = Cell(load(lo))
    cf, cs = cell.flux(1)
    h_lo = face(prev.u, pf, ps, cell.u, cf, cs)
    for c in range(lo, hi):
        nxt = Cell(load(c + 1))
        nf, ns_ = nxt.flux(1)
        h_hi = face(cell.u, cf, cs, nxt.u, nf, ns_)
        store(c, column_update(cell, h_lo, h_hi, axial_of(c, cell), *edges_of(c), force_of(c)))
        cell, cf, cs, h_lo = nxt, nf, ns_, h_hi


def walls(ns):
    span = lax.axis_index("span")
    return span == 0, span == ns - 1


def bulk_kernel(C, u_ref, f_ref, after_ref, one_ref):
    rotor = lax.axis_index("row") == 0

    def axial(c, cell):
        return axial_faces(cell, [0.0] * 5, rotor)

    def edges(c):
        return [[jnp.zeros((1, u_ref.shape[3]), jnp.float32)] * 5] * 2

    def store(c, u):
        for k in range(5):
            one_ref[k, c] = u[k]

    sweep(lambda c: [u_ref[k, c] for k in range(5)], 1, C - 1, axial, edges, lambda c: [f_ref[k, c] for k in range(3)], store)


def half_faces(cell, beside, rotor, near, slide=None):
    f, s = cell.flux(0)
    lane = lax.broadcasted_iota(jnp.int32, s.shape, 1)
    first = lane == 0
    last = lane == LANES - 1
    inf, ins = inlet_flux()

    def back(x, v):
        return jnp.where(first, v, pltpu.roll(x, 1, 1))

    pu = [back(x, v) for x, v in zip(cell.u, INLET)]
    pf = [pu[1]] + [back(x, v) for x, v in zip(f[1:], inf[1:])]
    lo = face(pu, pf, back(s, ins), cell.u, f, s)
    fb, sb = beside.flux(0)
    sign = jnp.where(rotor, 1.0, -1.0) * (-1.0 if near else 1.0)
    top = jnp.maximum(s, sb) * sign
    mid = [a + b - top * (y - x) for x, a, y, b in zip(cell.u, f, beside.u, fb)]
    if near:
        lo = [jnp.where(first, jnp.where(rotor, m, h), x) for m, h, x in zip(mid, slide, lo)]
        hi = [jnp.where(last, jnp.where(rotor, h, m), pltpu.roll(x, LANES - 1, 1)) for m, h, x in zip(mid, slide, lo)]
    else:
        lo = [jnp.where(jnp.logical_and(first, jnp.logical_not(rotor)), m, x) for m, x in zip(mid, lo)]
        hi = [
            jnp.where(last, jnp.where(rotor, m, 2.0 * g), pltpu.roll(x, LANES - 1, 1))
            for m, g, x in zip(mid, f, lo)
        ]
    return hi, lo


def halves(width, rotor):
    near = pl.multiple_of(jnp.where(rotor, width - LANES, 0), LANES)
    return near, pl.multiple_of(width - LANES - near, LANES)


class Ring:
    def __init__(self, C, T, nc, ns, off_ref, wt_ref):
        self.C, self.T, self.nc = C, T, nc
        self.off, self.wt = off_ref, wt_ref
        self.periods = max(1, 8 // nc)
        self.depth = nc * self.periods
        self.cycle = nc * C
        self.hub, self.casing = walls(ns)
        self.lane = lax.broadcasted_iota(jnp.int32, (self.depth, LANES), 1)

    def unpack(self, scratch, message):
        rows = self.nc * ROWS
        for copy in range(self.periods):
            scratch[copy * rows : (copy + 1) * rows, :] = message[...]

    def get(self, ref, j):
        return ref[pl.ds(j, self.depth, stride=ROWS), :]

    def ahead(self, x, k):
        if k == 0:
            return x
        a = pltpu.roll(x, (LANES - self.T * k) % LANES, 1)
        b = pltpu.roll(a, self.depth - 1, 0)
        return jnp.where(self.lane < LANES - self.T * k, a, b)

    def behind(self, x):
        a = pltpu.roll(x, self.T, 1)
        b = pltpu.roll(a, 1, 0)
        return jnp.where(self.lane >= self.T, a, b)

    def turned(self, x, cells):
        q = lax.div(cells, self.C)
        r = lax.rem(cells, self.C)
        y = pltpu.roll(x, lax.rem(self.depth - q, self.depth), 0)
        a = pltpu.roll(y, lax.rem(LANES - self.T * r, LANES), 1)
        b = pltpu.roll(a, self.depth - 1, 0)
        return jnp.where(self.lane < LANES - self.T * r, a, b)

    def ghosts(self, xs, t, sign):
        w = [jnp.full((1, LANES), self.wt[t, k], jnp.float32) for k in range(4)]
        total = w[0] + w[1] + w[2] + w[3]
        w = [x / total for x in w]
        start = lax.rem(sign * self.off[t] - 1 + 2 * self.cycle, self.cycle)
        out = []
        for x in xs:
            x = self.turned(x, start)
            g = w[0] * x
            for k in range(1, 4):
                g = g + w[k] * self.ahead(x, k)
            out.append(g)
        return out

    def partial_step(self, ref, cell, sign):
        inner = Cell([self.get(ref, 5 + k) for k in range(5)])
        fi, si = inner.flux(0)
        f, s = cell.flux(0)
        top = jnp.maximum(s, si) * sign
        h1 = [sign * (a + b - top * (x - y)) for x, a, y, b in zip(cell.u, f, inner.u, fi)]
        zero = jnp.zeros_like(s)
        f, s = cell.flux(1)
        behind = self.behind
        lo = face([behind(x) for x in cell.u], [behind(x) for x in f], behind(s), cell.u, f, s)
        hi = [self.ahead(x, 1) for x in lo]
        f, s = cell.flux(2)
        edge = Cell([self.get(ref, 13 + k) for k in range(5)])
        fe, se = edge.flux(2)
        in_span = lax.rem(self.lane, self.T)
        first = in_span == 0
        last = in_span == self.T - 1

        def prev(x, e):
            return jnp.where(first, e, pltpu.roll(x, 1, 1))

        slo = face([prev(x, e) for x, e in zip(cell.u, edge.u)], [prev(x, e) for x, e in zip(f, fe)], prev(s, se), cell.u, f, s)
        wall = wall_face(f, s, cell.u[3], -1.0)
        slo = [jnp.where(jnp.logical_and(first, self.hub), a, b) for a, b in zip(wall, slo)]
        top_face = face(cell.u, f, s, edge.u, fe, se)
        wall = wall_face(f, s, cell.u[3], 1.0)
        top_face = [jnp.where(self.casing, a, b) for a, b in zip(wall, top_face)]
        shi = [jnp.where(last, a, pltpu.roll(b, LANES - 1, 1)) for a, b in zip(top_face, slo)]
        force = [self.get(ref, 10 + k) for k in range(3)]
        return updated(cell.u, force, ([zero] * 5, h1), (hi, lo), (shi, slo))


def slide(cell, ghost, sign):
    f, s = cell.flux(0)
    g = Cell(ghost)
    fg, s_g = g.flux(0)
    top = jnp.maximum(s, s_g) * sign
    return [a + b - top * (y - x) for x, a, y, b in zip(cell.u, f, ghost, fg)]


def scalar_copies(off_ref, wt_ref, off_s, wt_s, sem):
    copies = [pltpu.make_async_copy(off_ref, off_s, sem.at[0]), pltpu.make_async_copy(wt_ref, wt_s, sem.at[1])]
    for copy in copies:
        copy.start()
    return copies


def far_kernel(
    C, T, nc, ns,
    off_ref, wt_ref, u_ref, f_ref, ha_ref, hb_ref, pa_ref, pb_ref, m1_ref, m2_ref, one_ref, own_ref,
    near_ref, rows_ref, beside_ref, far_ref, pre_ref,
    edge_s, col_s, row_s, fedge_s, own_s, off_s, wt_s, small_sem,
):
    rotor = lax.axis_index("row") == 0
    width = u_ref.shape[3]
    near, far = halves(width, rotor)
    halo = Halo(C, ha_ref, hb_ref, pa_ref, pb_ref)
    scalars = scalar_copies(off_ref, wt_ref, off_s, wt_s, small_sem)

    def corner(ref, base, k, side):
        parts = [ref[pl.ds(base + 16 * q + 2 * k + side, 1), :] for q in range(width // LANES)]
        return jnp.concatenate(parts, 1)

    def corners(k, side):
        a = corner(m1_ref, ROWS, k, side)
        b = corner(m2_ref, 2 * ROWS, k, side)
        return jnp.where(halo.even_c, b, a), jnp.where(halo.even_c, a, b)

    top_rows = lax.broadcasted_iota(jnp.int32, (C, width), 0)

    def extend(mid, lf, rt):
        shape = (C, width)
        tail = jnp.where(top_rows == 0, jnp.broadcast_to(rt, shape), jnp.broadcast_to(lf, shape))
        return jnp.concatenate([mid, tail], 0)

    cut = lambda xs: [x[:C] for x in xs]
    for side, wall in enumerate(walls(ns)):
        s0 = 0 if side == 0 else T - 1
        row = pl.ds(s0, 1)
        inner = Cell([extend(u_ref[k, :, s0, :], halo.left(k, row), halo.right(k, row)) for k in range(5)])
        cell = Cell([extend(halo.beyond(side, k), *corners(k, side)) for k in range(5)])
        outer = Cell([halo.beyond(side, 5 + k) for k in range(5)])
        edge, adjoining = edge_faces(side, cell, inner, wall)
        for k in range(5):
            edge_s[side, k] = edge[k]
        f, s = cell.flux(2)
        fo, so = outer.flux(2)
        if side == 0:
            span = cut(adjoining), face(outer.u, fo, so, cut(cell.u), cut(f), s[:C])
        else:
            span = face(cut(cell.u), cut(f), s[:C], outer.u, fo, so), cut(adjoining)
        f, s = cell.flux(1)
        back = lambda x: pltpu.roll(x, 1, 0)
        lo1 = face([back(x) for x in cell.u], [back(x) for x in f], back(s), cell.u, f, s)
        hi1 = [pltpu.roll(x, 2 * C - 1, 0) for x in lo1]
        mid = Cell(cut(cell.u))
        axial = axial_faces(mid, [0.0] * 5, rotor)
        force = [halo.beyond(side, 10 + k) for k in range(3)]
        new = updated(mid.u, force, axial, (cut(hi1), cut(lo1)), span)
        for k in range(5):
            row_s[side, k] = new[k]
            rows_ref[side, k] = row_s[side, k, :, pl.ds(near, LANES)]

    def load(c):
        if c < 0:
            return [halo.left(k + (5 if c == -2 else 0)) for k in range(5)]
        if c >= C:
            return [halo.right(k + (5 if c == C + 1 else 0)) for k in range(5)]
        return [u_ref[k, c] for k in range(5)]

    def edges(c):
        r = c if c >= 0 else 2 * C - 1
        return [[edge_s[side, k, r : r + 1, :] for k in range(5)] for side in range(2)]

    def force_of(c):
        if 0 <= c < C:
            return [f_ref[k, c] for k in range(3)]
        return [(halo.left if c < 0 else halo.right)(10 + k) for k in range(3)]

    slots = {-1: 0, 0: 1, C - 1: 2, C: 3}

    def store(c, u):
        for k in range(5):
            col_s[k, slots[c]] = u[k]

    axial = lambda c, cell: axial_faces(cell, [0.0] * 5, rotor)
    sweep(load, -1, 1, axial, edges, force_of, store)
    sweep(load, C - 1, C + 1, axial, edges, force_of, store)

    span_row = lax.broadcasted_iota(jnp.int32, (T, LANES), 0)

    def half(k, c, start):
        lanes = pl.ds(start, LANES)
        if c in slots:
            return col_s[k, slots[c], :, lanes]
        low_face = jnp.broadcast_to(edge_s[0, k, c : c + 1, lanes], (T, LANES))
        top_face = jnp.broadcast_to(edge_s[1, k, c : c + 1, lanes], (T, LANES))
        gain = jnp.where(span_row == 0, low_face, jnp.where(span_row == T - 1, -top_face, 0.0))
        return one_ref[k, c, :, lanes] + (0.5 * STEP) * gain

    def across(k, s0):
        lanes = pl.ds(far, LANES)
        gain = edge_s[0, k, 0:C, lanes] if s0 == 0 else -edge_s[1, k, 0:C, lanes]
        mid = one_ref[k, :, s0, lanes] + (0.5 * STEP) * gain
        c = lax.broadcasted_iota(jnp.int32, mid.shape, 0)
        ends = [jnp.broadcast_to(col_s[k, slots[e], s0 : s0 + 1, lanes], mid.shape) for e in (0, C - 1)]
        return jnp.where(c == 0, ends[0], jnp.where(c == C - 1, ends[1], mid))

    for k in range(5):
        for c in range(-1, C + 1):
            near_ref[k, c + 1] = half(k, c, near)

    for side, wall in enumerate(walls(ns)):
        s0 = 0 if side == 0 else T - 1
        inner = Cell([across(k, s0) for k in range(5)])
        outer = Cell([row_s[side, k, :, pl.ds(far, LANES)] for k in range(5)])
        edge, _ = edge_faces(side, outer, inner, wall)
        for k in range(5):
            fedge_s[side, k] = edge[k]

    down = jnp.where(rotor, LANES - 1, 1)
    up = jnp.where(rotor, 1, LANES - 1)

    def far_axial(c, cell):
        for k in range(5):
            beside_ref[k, c] = pltpu.roll(cell.u[k], up, 1)
        beside = Cell([pltpu.roll(near_ref[k, c + 1], down, 1) for k in range(5)])
        return half_faces(cell, beside, rotor, False)

    def far_edges(c):
        return [[fedge_s[side, k, c : c + 1, :] for k in range(5)] for side in range(2)]

    def far_store(c, u):
        for k in range(5):
            far_ref[k, c] = u[k]

    sweep(
        lambda c: [half(k, c, far) for k in range(5)], 0, C, far_axial, far_edges,
        lambda c: [f_ref[k, c, :, pl.ds(far, LANES)] for k in range(3)], far_store,
    )
    for copy in scalars:
        copy.wait()
    ring = Ring(C, T, nc, ns, off_s, wt_s)
    ring.unpack(own_s, own_ref)
    own = Cell([ring.get(own_s, k) for k in range(5)])
    part = ring.partial_step(own_s, own, jnp.where(rotor, 1.0, -1.0))
    ghost = ring.ghosts(own.u, 0, jnp.where(rotor, -1, 1))
    for k in range(5):
        pre_ref[k] = part[k]
        pre_ref[5 + k] = ghost[k]


def last_kernel(
    C, T, nc, ns,
    off_ref, wt_ref, f_ref, own_ref, par_ref, near_ref, rows_ref, beside_ref, pre_ref, far_ref,
    out_hbm, pf_hbm,
    own_s, par_s, ht_s, one_s, edge_s, new_s, pf_ref, off_s, wt_s, sem, small_sem,
):
    row = lax.axis_index("row")
    rotor = row == 0
    hub, casing = walls(ns)
    width = f_ref.shape[3]
    near, far = halves(width, rotor)
    scalars = scalar_copies(off_ref, wt_ref, off_s, wt_s, small_sem)
    ring = Ring(C, T, nc, ns, off_s, wt_s)
    get = ring.get
    sg = jnp.where(rotor, 1, -1)
    sgf = jnp.where(rotor, 1.0, -1.0)
    weight = (0.5 * STEP) * sgf
    ring.unpack(own_s, own_ref)
    ring.unpack(par_s, par_ref)
    own = Cell([get(own_s, k) for k in range(5)])
    par = Cell([get(par_s, k) for k in range(5)])
    h_par = slide(par, [pre_ref[5 + k] for k in range(5)], -sgf)
    par_new = ring.partial_step(par_s, par, -sgf)
    par_new = [x + weight * h for x, h in zip(par_new, h_par)]
    for copy in scalars:
        copy.wait()
    h_own = slide(own, ring.ghosts(par.u, 0, sg), sgf)
    g_edge = ring.ghosts([get(par_s, 13 + k) for k in range(5)], 0, sg)
    h_edge = slide(Cell([get(own_s, 13 + k) for k in range(5)]), g_edge, sgf)
    own_new = [pre_ref[k] - weight * h_own[k] for k in range(5)]
    h_next = slide(Cell(own_new), ring.ghosts(par_new, 1, sg), sgf)
    depth = ring.depth

    def eight(x):
        if depth == 8:
            return x
        return jnp.concatenate([x[0:7], x[depth - 1 : depth]], 0)

    tile = [eight(x) for x in h_own + h_edge + h_next]
    tile.append(jnp.zeros((8, LANES), jnp.float32))
    ht_s[...] = jnp.concatenate(tile, 0).T
    for t, h in ((0, h_own), (1, h_next)):
        for k in range(5):
            x = 0.5 * h[k][0:1, :]
            for c in range(C):
                pf_ref[t, k, c : c + 1, :] = x[:, c * T : (c + 1) * T]

    pf_copy = pltpu.make_async_copy(pf_ref, pf_hbm, small_sem.at[2])
    pf_copy.start()

    lane = lax.broadcasted_iota(jnp.int32, (T, LANES), 1)
    end = lane == jnp.where(rotor, LANES - 1, 0)

    def at_end(x, column):
        return pltpu.roll(x, jnp.where(rotor, LANES - 1 - column, (LANES - column) % LANES), 1)

    for c in range(-1, C + 1):
        sector = 0 if 0 <= c < C else (1 if c >= C else 7)
        r = (c % C) * T
        for k in range(5):
            h = at_end(ht_s[r : r + T, :], 8 * k + sector)
            one_s[k, c + 1] = near_ref[k, c + 1] - jnp.where(end, weight * h, 0.0)
    for side, wall in enumerate((hub, casing)):
        s0 = 0 if side == 0 else T - 1
        strip = ht_s[pl.ds(s0, C, stride=T), :]
        inner = Cell([one_s[k, 1 : C + 1, s0, :] for k in range(5)])
        outer = Cell([
            rows_ref[side, k] - jnp.where(end[:C], weight * at_end(strip, 40 + 8 * k), 0.0)
            for k in range(5)
        ])
        edge, _ = edge_faces(side, outer, inner, wall)
        for k in range(5):
            edge_s[side, k] = edge[k]

    def axial(c, cell):
        beside = Cell([beside_ref[k, c] for k in range(5)])
        h = [at_end(ht_s[c * T : (c + 1) * T, :], 80 + 8 * k) for k in range(5)]
        return half_faces(cell, beside, rotor, True, h)

    def edges(c):
        return [[edge_s[side, k, c : c + 1, :] for k in range(5)] for side in range(2)]

    def out_copy(k, c):
        return pltpu.make_async_copy(new_s.at[k, c], out_hbm.at[k, c], sem.at[c, k])

    def store(c, u):
        for k in range(5):
            new_s[k, c, :, pl.ds(near, LANES)] = u[k]
            new_s[k, c, :, pl.ds(far, LANES)] = far_ref[k, c]
            out_copy(k, c).start()

    sweep(
        lambda c: [one_s[k, c + 1] for k in range(5)], 0, C, axial, edges,
        lambda c: [f_ref[k, c, :, pl.ds(near, LANES)] for k in range(3)], store,
    )
    pf_copy.wait()
    for c in range(C):
        for k in range(5):
            out_copy(k, c).wait()


def pairs(count, first, wrap):
    route = []
    for low in range(first, count, 2):
        high = low + 1
        if high < count or wrap:
            route += [(low, high % count), (high % count, low)]
    return route


def snake(count, turn):
    order = [span for span in range(count)] + [2 * count - 1 - span for span in range(count)]
    n = len(order)
    return [(order[i], order[(i + turn) % n]) for i in range(n)]


def body(density, velocity, pressure, blade_force, offsets, weights):
    C, T, A = density.shape[1:]
    nc = lax.axis_size("circ")
    ns = lax.axis_size("span")
    area = C * T
    assert area == LANES and nc % 2 == 0 and A == 2 * LANES and C == 8
    rho, v, p, force = density[0], velocity[0], pressure[0], blade_force[0]

    thin = 16 * (A // LANES)
    u, force, off, wt, ta, tb, sa, sb, pa, pb = call(
        functools.partial(first_kernel, C, T),
        [(5, C, T, A), (3, C, T, A), offsets, weights, (C + thin, LANES), (C + thin, LANES), (13, C, A), (13, C, A), (13, T, A), (13, T, A)],
        [pltpu.with_memory_space_constraint(x, pltpu.HBM) for x in (rho, v, p, force, offsets, weights)],
        specs=[hbm()] * 6,
        scratch=[
            pltpu.VMEM((C, T, A), jnp.float32),
            pltpu.VMEM((3, C, T, A), jnp.float32),
            pltpu.VMEM((C, T, A), jnp.float32),
            pltpu.SemaphoreType.DMA((6,)),
        ],
    )
    ta = lax.ppermute(ta, ("row", "span"), snake(ns, 1))
    tb = lax.ppermute(tb, ("row", "span"), snake(ns, -1))
    ha = lax.ppermute(sa, ("row", "span"), snake(ns, 1))
    hb = lax.ppermute(sb, ("row", "span"), snake(ns, -1))
    pa = lax.ppermute(pa, "circ", pairs(nc, 0, True))
    pb = lax.ppermute(pb, "circ", pairs(nc, 1, True))

    m1, m2 = call(
        functools.partial(thin_kernel, C, T),
        [(ROWS + thin, LANES), (2 * ROWS + thin, LANES)],
        (u, force, ta, tb),
        scratch=[pltpu.VMEM((area, LANES), jnp.float32)],
    )
    planes = m1[:ROWS]
    m1 = lax.ppermute(m1, "circ", pairs(nc, 0, True))
    f32 = jnp.float32
    if nc == 4:
        (m2,) = call(fill_kernel, [m2.shape], (m1, m2), aliases={1: 0})
    (one,) = call(
        functools.partial(bulk_kernel, C),
        [(5, C, T, A)],
        (u, force, m2),
        cost=pl.CostEstimate(flops=10_000_000, bytes_accessed=4_000_000, transcendentals=0),
    )
    if nc == 4:
        got = lax.ppermute(m2, "circ", pairs(nc, 1, True))
        (ring,) = call(ring_kernel, [(nc, ROWS, LANES)], (m2, got, one))
    else:
        got = lax.ppermute(m2, "circ", pairs(nc, 1, True))
        whole = lax.all_gather(planes, "circ")
        whole = jnp.concatenate([whole, whole], 0)
        ring = lax.dynamic_slice_in_dim(whole, lax.axis_index("circ"), nc, 0)
    partner = lax.ppermute(ring, "row", [(0, 1), (1, 0)])
    copies = max(1, 8 // nc)
    rows = nc * ROWS
    ring = ring.reshape(rows, LANES)
    near, halo_rows, beside, far, pre = call(
        functools.partial(far_kernel, C, T, nc, ns),
        [(5, C + 2, T, LANES), (2, 5, C, LANES), (5, C, T, LANES), (5, C, T, LANES), (10, copies * nc, LANES)],
        (off, wt, u, force, ha, hb, pa, pb, m1, got, one, ring),
        scratch=[
            pltpu.VMEM((2, 5, 2 * C, A), f32),
            pltpu.VMEM((5, 4, T, A), f32),
            pltpu.VMEM((2, 5, C, A), f32),
            pltpu.VMEM((2, 5, C, LANES), f32),
            pltpu.VMEM((copies * rows, LANES), f32),
            pltpu.SMEM(offsets.shape, jnp.int32),
            pltpu.SMEM(weights.shape, f32),
            pltpu.SemaphoreType.DMA((2,)),
        ],
        cost=pl.CostEstimate(flops=10_000_000, bytes_accessed=4_000_000, transcendentals=0),
    )
    state, plane_flux = call(
        functools.partial(last_kernel, C, T, nc, ns),
        [(5, C, T, A), (2, 5, C, T)],
        (off, wt, force, ring, partner.reshape(rows, LANES), near, halo_rows, beside, pre, far),
        outs=[hbm(), hbm()],
        scratch=[
            pltpu.VMEM((copies * rows, LANES), f32),
            pltpu.VMEM((copies * rows, LANES), f32),
            pltpu.VMEM((LANES, LANES), f32),
            pltpu.VMEM((5, C + 2, T, LANES), f32),
            pltpu.VMEM((2, 5, C, LANES), f32),
            pltpu.VMEM((5, C, T, A), f32),
            pltpu.VMEM((2, 5, C, T), f32),
            pltpu.SMEM(offsets.shape, jnp.int32),
            pltpu.SMEM(weights.shape, f32),
            pltpu.SemaphoreType.DMA((C, 5)),
            pltpu.SemaphoreType.DMA((3,)),
        ],
        limit=16,
    )
    return state[None], plane_flux[None]


def solution(mesh):
    placed = (
        P("row", "circ", "span", None),
        P("row", None, "circ", "span", None),
        P("row", "circ", "span", None),
        P("row", None, "circ", "span", None),
        P(),
        P(),
    )
    return jax.shard_map(
        body,
        mesh=mesh,
        in_specs=placed,
        out_specs=(P("row", None, "circ", "span", None), P("row", None, None, "circ", "span")),
        check_vma=False,
    )
```

```python
import functools

import jax
import jax.numpy as jnp
from jax import lax
from jax.experimental import pallas as pl
from jax.experimental.pallas import tpu as pltpu
from jax.sharding import PartitionSpec as P

GAMMA = 1.4
STEP = 0.04
INLET = (1.0, 0.5, 0.0, 0.0, 2.625)
LANES = 128
ROWS = 24


def vmem():
    return pl.BlockSpec(memory_space=pltpu.VMEM)


def hbm():
    return pl.BlockSpec(memory_space=pltpu.HBM)


def call(kernel, shapes, args, specs=None, scratch=(), aliases=None, cost=None, limit=6, outs=None):
    return pl.pallas_call(
        kernel,
        out_shape=[jax.ShapeDtypeStruct(s.shape, s.dtype) if hasattr(s, "dtype") else jax.ShapeDtypeStruct(s, jnp.float32) for s in shapes],
        in_specs=specs or [vmem()] * len(args),
        out_specs=outs or [vmem()] * len(shapes),
        scratch_shapes=list(scratch),
        input_output_aliases=aliases or {},
        cost_estimate=cost,
        compiler_params=pltpu.CompilerParams(vmem_limit_bytes=limit << 20),
    )(*args)


class Cell:
    def __init__(self, u):
        self.u = u
        rho, m0, m1, m2, en = u
        self.inv = 1.0 / rho
        kin = 0.5 * (m0 * m0 + m1 * m1 + m2 * m2) * self.inv
        self.p = (GAMMA - 1.0) * (en - kin)
        self.sound = jnp.sqrt(GAMMA * self.p * self.inv)

    def flux(self, d):
        m = self.u[1:4]
        vel = m[d] * self.inv
        f = [m[d], m[0] * vel, m[1] * vel, m[2] * vel, (self.u[4] + self.p) * vel]
        f[1 + d] = f[1 + d] + self.p
        return f, jnp.abs(vel) + self.sound


def face(ul, fl, sl, ur, fr, sr):
    top = jnp.maximum(sl, sr)
    return [a + b - top * (y - x) for x, a, y, b in zip(ul, fl, ur, fr)]


def updated(u, force, *spans):
    src = [None, u[0] * force[0], u[0] * force[1], u[0] * force[2]]
    src.append(u[1] * force[0] + u[2] * force[1] + u[3] * force[2])
    out = []
    for k in range(5):
        div = spans[0][0][k] - spans[0][1][k]
        for hi, lo in spans[1:]:
            div = div + (hi[k] - lo[k])
        new = u[k] - (0.5 * STEP) * div
        out.append(new if src[k] is None else new + STEP * src[k])
    return out


def conserved(rho, v, p):
    m = [rho * x for x in v]
    en = p / (GAMMA - 1.0) + 0.5 * rho * (v[0] * v[0] + v[1] * v[1] + v[2] * v[2])
    return [rho] + m + [en]


def inlet_flux():
    rho, m0, m1, m2, en = INLET
    p = (GAMMA - 1.0) * (en - 0.5 * (m0 * m0 + m1 * m1 + m2 * m2) / rho)
    vel = m0 / rho
    f = [m0, m0 * vel + p, m1 * vel, m2 * vel, (en + p) * vel]
    return f, abs(vel) + (GAMMA * p / rho) ** 0.5


def axial_faces(cell, slide, rotor):
    u = cell.u
    f, s = cell.flux(0)
    shape = u[0].shape
    lane = lax.broadcasted_iota(jnp.int32, shape, 1)
    last = shape[1] - 1
    first_lane = lane == 0
    last_lane = lane == last
    inf, ins = inlet_flux()

    def back(x, v):
        return jnp.where(first_lane, v, pltpu.roll(x, 1, 1))

    pu = [back(x, v) for x, v in zip(u, INLET)]
    pf = [pu[1]] + [back(x, v) for x, v in zip(f[1:], inf[1:])]
    lo = face(pu, pf, back(s, ins), u, f, s)
    stator_first = jnp.logical_and(first_lane, jnp.logical_not(rotor))
    lo = [jnp.where(stator_first, h, x) for h, x in zip(slide, lo)]
    hi = [
        jnp.where(last_lane, jnp.where(rotor, h, 2.0 * g), pltpu.roll(x, last, 1))
        for h, g, x in zip(slide, f, lo)
    ]
    return hi, lo


def wall_face(f, s, m, sign):
    zero = jnp.zeros_like(s)
    return [zero, zero, zero, 2.0 * (f[3] + sign * s * m), zero]


def place():
    row = lax.axis_index("row")
    circ = lax.axis_index("circ")
    span = lax.axis_index("span")
    return row, lax.rem(circ, 2) == 0, row == 0, span


def first_kernel(
    C, T,
    rho_hbm, v_hbm, p_hbm, f_hbm, off_hbm, wt_hbm,
    u_ref, f_ref, off_ref, wt_ref, ta_ref, tb_ref,
    rho_ref, v_ref, p_ref, sem,
):
    copies = [
        pltpu.make_async_copy(src, dst, sem.at[i])
        for i, (src, dst) in enumerate(
            [(rho_hbm, rho_ref), (v_hbm, v_ref), (p_hbm, p_ref), (f_hbm, f_ref), (off_hbm, off_ref), (wt_hbm, wt_ref)]
        )
    ]
    for copy in copies:
        copy.start()
    _, _, even_s, _ = place()
    for copy in copies:
        copy.wait()
    for c in range(C):
        u = conserved(rho_ref[c], [v_ref[k, c] for k in range(3)], p_ref[c])
        for k in range(5):
            u_ref[k, c] = u[k]

    rotor = lax.axis_index("row") == 0
    width = u_ref.shape[3]
    half = pl.ds(pl.multiple_of(jnp.where(rotor, width - LANES, 0), LANES), LANES)
    end = jnp.where(rotor, LANES - 1, 0)
    small = lax.broadcasted_iota(jnp.int32, (C, LANES), 1)

    def pick(ref, rows, low, high):
        ref[0][rows, :] = jnp.where(even_s, high, low)
        ref[1][rows, :] = jnp.where(even_s, low, high)

    thin = ta_ref, tb_ref
    tiles = []
    for s in (0, T - 1):
        tile = jnp.zeros((C, LANES), jnp.float32)
        for k in range(5):
            x = pltpu.roll(u_ref[k, :, s, half], lax.rem(13 + k - end + LANES, LANES), 1)
            tile = jnp.where(small == 13 + k, x, tile)
        tiles.append(tile)
    pick(thin, slice(0, C), *tiles)
    for part in range(width // LANES):
        lanes = slice(part * LANES, (part + 1) * LANES)
        base = C + 16 * part
        for k in range(5):
            for e, c in enumerate((0, C - 1)):
                r = base + 2 * k + e
                pick(thin, slice(r, r + 1), u_ref[k, c, 0:1, lanes], u_ref[k, c, T - 1 : T, lanes])
        zero = jnp.zeros((6, LANES), jnp.float32)
        pick(thin, slice(base + 10, base + 16), zero, zero)


def pack_kernel(C, T, u_ref, f_ref, after_ref, sa_ref, sb_ref, pa_ref, pb_ref):
    _, even_c, even_s, _ = place()

    def row(k, s):
        ref = u_ref.at[k] if k < 5 else f_ref.at[k - 5]
        return ref[:, s, :]

    def send(slot, k, low, high):
        a, b = row(k, low), row(k, high)
        sa_ref[slot] = jnp.where(even_s, b, a)
        sb_ref[slot] = jnp.where(even_s, a, b)

    for k in range(5):
        send(k, k, 0, T - 1)
        send(5 + k, k, 1, T - 2)
    for k in range(3):
        send(10 + k, 5 + k, 0, T - 1)
    near = jnp.where(even_c, C - 1, 0)
    far = jnp.where(even_c, C - 2, 1)
    for ref, n, m in ((pa_ref, near, far), (pb_ref, C - 1 - near, C - 1 - far)):
        for k in range(5):
            ref[k] = u_ref[k, n]
            ref[5 + k] = u_ref[k, m]
        for k in range(3):
            ref[10 + k] = f_ref[k, n]


def thin_kernel(C, T, u_ref, f_ref, ha_ref, hb_ref, m1_ref, m2_ref, t_ref):
    row, even_c, even_s, _ = place()
    even_s = jnp.logical_not(even_s)
    rotor = row == 0
    width = u_ref.shape[3]
    half = pl.ds(pl.multiple_of(jnp.where(rotor, width - LANES, 0), LANES), LANES)
    end = jnp.where(rotor, LANES - 1, 0)
    second = jnp.where(rotor, LANES - 2, 1)
    lane = lax.broadcasted_iota(jnp.int32, (C * T, LANES), 1)
    t = jnp.zeros((C * T, LANES), jnp.float32)

    def put(x, j, e):
        return pltpu.roll(x, lax.rem(j - e + LANES, LANES), 1)

    for k in range(5):
        x = u_ref[k, :, :, half].reshape(C * T, LANES)
        t = jnp.where(lane == k, put(x, k, end), t)
        t = jnp.where(lane == 5 + k, put(x, 5 + k, second), t)
    for k in range(3):
        t = jnp.where(lane == 10 + k, put(f_ref[k, :, :, half].reshape(C * T, LANES), 10 + k, end), t)
    t_ref[...] = t
    small = lax.broadcasted_iota(jnp.int32, (C, LANES), 1)
    for start, is_low in ((0, True), (T - 1, False)):
        where_a = even_s if not is_low else jnp.logical_not(even_s)
        rows = pl.ds(start, C, stride=T)
        x = jnp.where(where_a, ha_ref[0:C, :], hb_ref[0:C, :])
        edge_lane = jnp.logical_and(small >= 13, small < 18)
        t_ref[rows, :] = jnp.where(edge_lane, x, t_ref[rows, :])
    planes = t_ref[...].T[:ROWS]
    m1_ref[0:ROWS, :] = planes
    m2_ref[0:ROWS, :] = planes
    m2_ref[ROWS : 2 * ROWS, :] = jnp.zeros((ROWS, LANES), jnp.float32)

    def corner(ref, base, c):
        for k in range(5):
            for side in range(2):
                where_a = even_s if side == 1 else jnp.logical_not(even_s)
                for part in range(width // LANES):
                    r = base + 16 * part + 2 * k + side
                    q = pl.ds(C + 16 * part + 2 * k + jnp.where(c == 0, 0, 1), 1)
                    ref[r : r + 1, :] = jnp.where(where_a, ha_ref[q, :], hb_ref[q, :])
        for part in range(width // LANES):
            r = base + 16 * part
            ref[r + 10 : r + 16, :] = jnp.zeros((6, LANES), jnp.float32)

    near = jnp.where(even_c, C - 1, 0)
    corner(m1_ref, ROWS, near)
    corner(m2_ref, 2 * ROWS, C - 1 - near)


def fill_kernel(m1_ref, m2_ref, out_ref):
    out_ref[...] = m2_ref[...]
    out_ref[ROWS : 2 * ROWS, :] = m1_ref[0:ROWS, :]


def ring_kernel(m2_ref, got_ref, after_ref, ring_ref):
    _, even, _, _ = place()
    mate = m2_ref[ROWS : 2 * ROWS, :]
    next_ = got_ref[0:ROWS, :]
    ring_ref[0] = m2_ref[0:ROWS, :]
    ring_ref[1] = jnp.where(even, mate, next_)
    ring_ref[2] = got_ref[ROWS : 2 * ROWS, :]
    ring_ref[3] = jnp.where(even, next_, mate)


class Halo:
    def __init__(self, C, ha, hb, pa, pb):
        _, self.even_c, even_s, _ = place()
        self.even_s = jnp.logical_not(even_s)
        self.C, self.ha, self.hb, self.pa, self.pb = C, ha, hb, pa, pb

    def left(self, slot, rows=slice(None)):
        return jnp.where(self.even_c, self.pb[slot, rows, :], self.pa[slot, rows, :])

    def right(self, slot, rows=slice(None)):
        return jnp.where(self.even_c, self.pa[slot, rows, :], self.pb[slot, rows, :])

    def beyond(self, side, slot):
        where_a = self.even_s if side == 1 else jnp.logical_not(self.even_s)
        return jnp.where(where_a, self.ha[slot], self.hb[slot])


def edge_faces(side, outer, inner, at_wall):
    fo, so = outer.flux(2)
    fi, si = inner.flux(2)
    if side == 0:
        near = face(outer.u, fo, so, inner.u, fi, si)
        wall = wall_face(fi, si, inner.u[3], -1.0)
    else:
        near = face(inner.u, fi, si, outer.u, fo, so)
        wall = wall_face(fi, si, inner.u[3], 1.0)
    return [jnp.where(at_wall, w, x) for w, x in zip(wall, near)], near


def column_update(cell, circ_lo, circ_hi, axial, low_row, top_row, force):
    column = cell.u[0].shape
    T = column[0]
    srow = lax.broadcasted_iota(jnp.int32, column, 0)
    f, s = cell.flux(2)
    back = lambda x: pltpu.roll(x, 1, 0)
    lo2 = face([back(x) for x in cell.u], [back(x) for x in f], back(s), cell.u, f, s)
    lo2 = [jnp.where(srow == 0, jnp.broadcast_to(e, column), x) for e, x in zip(low_row, lo2)]
    hi2 = [
        jnp.where(srow == T - 1, jnp.broadcast_to(e, column), pltpu.roll(x, T - 1, 0))
        for e, x in zip(top_row, lo2)
    ]
    return updated(cell.u, force, axial, (circ_hi, circ_lo), (hi2, lo2))


def sweep(load, lo, hi, axial_of, edges_of, force_of, store):
    prev = Cell(load(lo - 1))
    pf, ps = prev.flux(1)
    cell = Cell(load(lo))
    cf, cs = cell.flux(1)
    h_lo = face(prev.u, pf, ps, cell.u, cf, cs)
    for c in range(lo, hi):
        nxt = Cell(load(c + 1))
        nf, ns_ = nxt.flux(1)
        h_hi = face(cell.u, cf, cs, nxt.u, nf, ns_)
        store(c, column_update(cell, h_lo, h_hi, axial_of(c, cell), *edges_of(c), force_of(c)))
        cell, cf, cs, h_lo = nxt, nf, ns_, h_hi


def walls(ns):
    span = lax.axis_index("span")
    return span == 0, span == ns - 1


def bulk_kernel(C, u_ref, f_ref, after_ref, one_ref):
    rotor = lax.axis_index("row") == 0

    def axial(c, cell):
        return axial_faces(cell, [0.0] * 5, rotor)

    def edges(c):
        return [[jnp.zeros((1, u_ref.shape[3]), jnp.float32)] * 5] * 2

    def store(c, u):
        for k in range(5):
            one_ref[k, c] = u[k]

    sweep(lambda c: [u_ref[k, c] for k in range(5)], 1, C - 1, axial, edges, lambda c: [f_ref[k, c] for k in range(3)], store)


def half_faces(cell, beside, rotor, near, slide=None):
    f, s = cell.flux(0)
    lane = lax.broadcasted_iota(jnp.int32, s.shape, 1)
    first = lane == 0
    last = lane == LANES - 1
    inf, ins = inlet_flux()

    def back(x, v):
        return jnp.where(first, v, pltpu.roll(x, 1, 1))

    pu = [back(x, v) for x, v in zip(cell.u, INLET)]
    pf = [pu[1]] + [back(x, v) for x, v in zip(f[1:], inf[1:])]
    lo = face(pu, pf, back(s, ins), cell.u, f, s)
    fb, sb = beside.flux(0)
    sign = jnp.where(rotor, 1.0, -1.0) * (-1.0 if near else 1.0)
    top = jnp.maximum(s, sb) * sign
    mid = [a + b - top * (y - x) for x, a, y, b in zip(cell.u, f, beside.u, fb)]
    if near:
        lo = [jnp.where(first, jnp.where(rotor, m, h), x) for m, h, x in zip(mid, slide, lo)]
        hi = [jnp.where(last, jnp.where(rotor, h, m), pltpu.roll(x, LANES - 1, 1)) for m, h, x in zip(mid, slide, lo)]
    else:
        lo = [jnp.where(jnp.logical_and(first, jnp.logical_not(rotor)), m, x) for m, x in zip(mid, lo)]
        hi = [
            jnp.where(last, jnp.where(rotor, m, 2.0 * g), pltpu.roll(x, LANES - 1, 1))
            for m, g, x in zip(mid, f, lo)
        ]
    return hi, lo


def halves(width, rotor):
    near = pl.multiple_of(jnp.where(rotor, width - LANES, 0), LANES)
    return near, pl.multiple_of(width - LANES - near, LANES)


class Ring:
    def __init__(self, C, T, nc, ns, off_ref, wt_ref):
        self.C, self.T, self.nc = C, T, nc
        self.off, self.wt = off_ref, wt_ref
        self.periods = max(1, 8 // nc)
        self.depth = nc * self.periods
        self.cycle = nc * C
        self.hub, self.casing = walls(ns)
        self.lane = lax.broadcasted_iota(jnp.int32, (self.depth, LANES), 1)

    def unpack(self, scratch, message):
        rows = self.nc * ROWS
        for copy in range(self.periods):
            scratch[copy * rows : (copy + 1) * rows, :] = message[...]

    def get(self, ref, j):
        return ref[pl.ds(j, self.depth, stride=ROWS), :]

    def ahead(self, x, k):
        if k == 0:
            return x
        a = pltpu.roll(x, (LANES - self.T * k) % LANES, 1)
        b = pltpu.roll(a, self.depth - 1, 0)
        return jnp.where(self.lane < LANES - self.T * k, a, b)

    def behind(self, x):
        a = pltpu.roll(x, self.T, 1)
        b = pltpu.roll(a, 1, 0)
        return jnp.where(self.lane >= self.T, a, b)

    def turned(self, x, cells):
        q = lax.div(cells, self.C)
        r = lax.rem(cells, self.C)
        y = pltpu.roll(x, lax.rem(self.depth - q, self.depth), 0)
        a = pltpu.roll(y, lax.rem(LANES - self.T * r, LANES), 1)
        b = pltpu.roll(a, self.depth - 1, 0)
        return jnp.where(self.lane < LANES - self.T * r, a, b)

    def ghosts(self, xs, t, sign):
        w = [jnp.full((1, LANES), self.wt[t, k], jnp.float32) for k in range(4)]
        total = w[0] + w[1] + w[2] + w[3]
        w = [x / total for x in w]
        start = lax.rem(sign * self.off[t] - 1 + 2 * self.cycle, self.cycle)
        out = []
        for x in xs:
            x = self.turned(x, start)
            g = w[0] * x
            for k in range(1, 4):
                g = g + w[k] * self.ahead(x, k)
            out.append(g)
        return out

    def partial_step(self, ref, cell, sign):
        inner = Cell([self.get(ref, 5 + k) for k in range(5)])
        fi, si = inner.flux(0)
        f, s = cell.flux(0)
        top = jnp.maximum(s, si) * sign
        h1 = [sign * (a + b - top * (x - y)) for x, a, y, b in zip(cell.u, f, inner.u, fi)]
        zero = jnp.zeros_like(s)
        f, s = cell.flux(1)
        behind = self.behind
        lo = face([behind(x) for x in cell.u], [behind(x) for x in f], behind(s), cell.u, f, s)
        hi = [self.ahead(x, 1) for x in lo]
        f, s = cell.flux(2)
        edge = Cell([self.get(ref, 13 + k) for k in range(5)])
        fe, se = edge.flux(2)
        in_span = lax.rem(self.lane, self.T)
        first = in_span == 0
        last = in_span == self.T - 1

        def prev(x, e):
            return jnp.where(first, e, pltpu.roll(x, 1, 1))

        slo = face([prev(x, e) for x, e in zip(cell.u, edge.u)], [prev(x, e) for x, e in zip(f, fe)], prev(s, se), cell.u, f, s)
        wall = wall_face(f, s, cell.u[3], -1.0)
        slo = [jnp.where(jnp.logical_and(first, self.hub), a, b) for a, b in zip(wall, slo)]
        top_face = face(cell.u, f, s, edge.u, fe, se)
        wall = wall_face(f, s, cell.u[3], 1.0)
        top_face = [jnp.where(self.casing, a, b) for a, b in zip(wall, top_face)]
        shi = [jnp.where(last, a, pltpu.roll(b, LANES - 1, 1)) for a, b in zip(top_face, slo)]
        force = [self.get(ref, 10 + k) for k in range(3)]
        return updated(cell.u, force, ([zero] * 5, h1), (hi, lo), (shi, slo))


def slide(cell, ghost, sign):
    f, s = cell.flux(0)
    g = Cell(ghost)
    fg, s_g = g.flux(0)
    top = jnp.maximum(s, s_g) * sign
    return [a + b - top * (y - x) for x, a, y, b in zip(cell.u, f, ghost, fg)]


def scalar_copies(off_ref, wt_ref, off_s, wt_s, sem):
    copies = [pltpu.make_async_copy(off_ref, off_s, sem.at[0]), pltpu.make_async_copy(wt_ref, wt_s, sem.at[1])]
    for copy in copies:
        copy.start()
    return copies


def far_kernel(
    C, T, nc, ns,
    off_ref, wt_ref, u_ref, f_ref, ha_ref, hb_ref, pa_ref, pb_ref, m1_ref, m2_ref, one_ref, own_ref,
    near_ref, rows_ref, beside_ref, far_ref, pre_ref,
    edge_s, col_s, row_s, fedge_s, own_s, off_s, wt_s, small_sem,
):
    rotor = lax.axis_index("row") == 0
    width = u_ref.shape[3]
    near, far = halves(width, rotor)
    halo = Halo(C, ha_ref, hb_ref, pa_ref, pb_ref)
    scalars = scalar_copies(off_ref, wt_ref, off_s, wt_s, small_sem)

    def corner(ref, base, k, side):
        parts = [ref[pl.ds(base + 16 * q + 2 * k + side, 1), :] for q in range(width // LANES)]
        return jnp.concatenate(parts, 1)

    def corners(k, side):
        a = corner(m1_ref, ROWS, k, side)
        b = corner(m2_ref, 2 * ROWS, k, side)
        return jnp.where(halo.even_c, b, a), jnp.where(halo.even_c, a, b)

    top_rows = lax.broadcasted_iota(jnp.int32, (C, width), 0)

    def extend(mid, lf, rt):
        shape = (C, width)
        tail = jnp.where(top_rows == 0, jnp.broadcast_to(rt, shape), jnp.broadcast_to(lf, shape))
        return jnp.concatenate([mid, tail], 0)

    cut = lambda xs: [x[:C] for x in xs]
    for side, wall in enumerate(walls(ns)):
        s0 = 0 if side == 0 else T - 1
        row = pl.ds(s0, 1)
        inner = Cell([extend(u_ref[k, :, s0, :], halo.left(k, row), halo.right(k, row)) for k in range(5)])
        cell = Cell([extend(halo.beyond(side, k), *corners(k, side)) for k in range(5)])
        outer = Cell([halo.beyond(side, 5 + k) for k in range(5)])
        edge, adjoining = edge_faces(side, cell, inner, wall)
        for k in range(5):
            edge_s[side, k] = edge[k]
        f, s = cell.flux(2)
        fo, so = outer.flux(2)
        if side == 0:
            span = cut(adjoining), face(outer.u, fo, so, cut(cell.u), cut(f), s[:C])
        else:
            span = face(cut(cell.u), cut(f), s[:C], outer.u, fo, so), cut(adjoining)
        f, s = cell.flux(1)
        back = lambda x: pltpu.roll(x, 1, 0)
        lo1 = face([back(x) for x in cell.u], [back(x) for x in f], back(s), cell.u, f, s)
        hi1 = [pltpu.roll(x, 2 * C - 1, 0) for x in lo1]
        mid = Cell(cut(cell.u))
        axial = axial_faces(mid, [0.0] * 5, rotor)
        force = [halo.beyond(side, 10 + k) for k in range(3)]
        new = updated(mid.u, force, axial, (cut(hi1), cut(lo1)), span)
        for k in range(5):
            row_s[side, k] = new[k]
            rows_ref[side, k] = row_s[side, k, :, pl.ds(near, LANES)]

    def load(c):
        if c < 0:
            return [halo.left(k + (5 if c == -2 else 0)) for k in range(5)]
        if c >= C:
            return [halo.right(k + (5 if c == C + 1 else 0)) for k in range(5)]
        return [u_ref[k, c] for k in range(5)]

    def edges(c):
        r = c if c >= 0 else 2 * C - 1
        return [[edge_s[side, k, r : r + 1, :] for k in range(5)] for side in range(2)]

    def force_of(c):
        if 0 <= c < C:
            return [f_ref[k, c] for k in range(3)]
        return [(halo.left if c < 0 else halo.right)(10 + k) for k in range(3)]

    slots = {-1: 0, 0: 1, C - 1: 2, C: 3}

    def store(c, u):
        for k in range(5):
            col_s[k, slots[c]] = u[k]

    axial = lambda c, cell: axial_faces(cell, [0.0] * 5, rotor)
    sweep(load, -1, 1, axial, edges, force_of, store)
    sweep(load, C - 1, C + 1, axial, edges, force_of, store)

    span_row = lax.broadcasted_iota(jnp.int32, (T, LANES), 0)

    def half(k, c, start):
        lanes = pl.ds(start, LANES)
        if c in slots:
            return col_s[k, slots[c], :, lanes]
        low_face = jnp.broadcast_to(edge_s[0, k, c : c + 1, lanes], (T, LANES))
        top_face = jnp.broadcast_to(edge_s[1, k, c : c + 1, lanes], (T, LANES))
        gain = jnp.where(span_row == 0, low_face, jnp.where(span_row == T - 1, -top_face, 0.0))
        return one_ref[k, c, :, lanes] + (0.5 * STEP) * gain

    def across(k, s0):
        lanes = pl.ds(far, LANES)
        gain = edge_s[0, k, 0:C, lanes] if s0 == 0 else -edge_s[1, k, 0:C, lanes]
        mid = one_ref[k, :, s0, lanes] + (0.5 * STEP) * gain
        c = lax.broadcasted_iota(jnp.int32, mid.shape, 0)
        ends = [jnp.broadcast_to(col_s[k, slots[e], s0 : s0 + 1, lanes], mid.shape) for e in (0, C - 1)]
        return jnp.where(c == 0, ends[0], jnp.where(c == C - 1, ends[1], mid))

    for k in range(5):
        for c in range(-1, C + 1):
            near_ref[k, c + 1] = half(k, c, near)

    for side, wall in enumerate(walls(ns)):
        s0 = 0 if side == 0 else T - 1
        inner = Cell([across(k, s0) for k in range(5)])
        outer = Cell([row_s[side, k, :, pl.ds(far, LANES)] for k in range(5)])
        edge, _ = edge_faces(side, outer, inner, wall)
        for k in range(5):
            fedge_s[side, k] = edge[k]

    down = jnp.where(rotor, LANES - 1, 1)
    up = jnp.where(rotor, 1, LANES - 1)

    def far_axial(c, cell):
        for k in range(5):
            beside_ref[k, c] = pltpu.roll(cell.u[k], up, 1)
        beside = Cell([pltpu.roll(near_ref[k, c + 1], down, 1) for k in range(5)])
        return half_faces(cell, beside, rotor, False)

    def far_edges(c):
        return [[fedge_s[side, k, c : c + 1, :] for k in range(5)] for side in range(2)]

    def far_store(c, u):
        for k in range(5):
            far_ref[k, c] = u[k]

    sweep(
        lambda c: [half(k, c, far) for k in range(5)], 0, C, far_axial, far_edges,
        lambda c: [f_ref[k, c, :, pl.ds(far, LANES)] for k in range(3)], far_store,
    )
    for copy in scalars:
        copy.wait()
    ring = Ring(C, T, nc, ns, off_s, wt_s)
    ring.unpack(own_s, own_ref)
    own = Cell([ring.get(own_s, k) for k in range(5)])
    part = ring.partial_step(own_s, own, jnp.where(rotor, 1.0, -1.0))
    ghost = ring.ghosts(own.u, 0, jnp.where(rotor, -1, 1))
    for k in range(5):
        pre_ref[k] = part[k]
        pre_ref[5 + k] = ghost[k]


def last_kernel(
    C, T, nc, ns,
    off_ref, wt_ref, f_ref, own_ref, par_ref, near_ref, rows_ref, beside_ref, pre_ref, far_ref,
    out_hbm, pf_hbm,
    own_s, par_s, ht_s, one_s, edge_s, new_s, pf_ref, off_s, wt_s, sem, small_sem,
):
    row = lax.axis_index("row")
    rotor = row == 0
    hub, casing = walls(ns)
    width = f_ref.shape[3]
    near, far = halves(width, rotor)
    scalars = scalar_copies(off_ref, wt_ref, off_s, wt_s, small_sem)
    ring = Ring(C, T, nc, ns, off_s, wt_s)
    get = ring.get
    sg = jnp.where(rotor, 1, -1)
    sgf = jnp.where(rotor, 1.0, -1.0)
    weight = (0.5 * STEP) * sgf
    ring.unpack(own_s, own_ref)
    ring.unpack(par_s, par_ref)
    own = Cell([get(own_s, k) for k in range(5)])
    par = Cell([get(par_s, k) for k in range(5)])
    h_par = slide(par, [pre_ref[5 + k] for k in range(5)], -sgf)
    par_new = ring.partial_step(par_s, par, -sgf)
    par_new = [x + weight * h for x, h in zip(par_new, h_par)]
    for copy in scalars:
        copy.wait()
    h_own = slide(own, ring.ghosts(par.u, 0, sg), sgf)
    g_edge = ring.ghosts([get(par_s, 13 + k) for k in range(5)], 0, sg)
    h_edge = slide(Cell([get(own_s, 13 + k) for k in range(5)]), g_edge, sgf)
    own_new = [pre_ref[k] - weight * h_own[k] for k in range(5)]
    h_next = slide(Cell(own_new), ring.ghosts(par_new, 1, sg), sgf)
    depth = ring.depth

    def eight(x):
        if depth == 8:
            return x
        return jnp.concatenate([x[0:7], x[depth - 1 : depth]], 0)

    tile = [eight(x) for x in h_own + h_edge + h_next]
    tile.append(jnp.zeros((8, LANES), jnp.float32))
    ht_s[...] = jnp.concatenate(tile, 0).T
    for t, h in ((0, h_own), (1, h_next)):
        for k in range(5):
            x = 0.5 * h[k][0:1, :]
            for c in range(C):
                pf_ref[t, k, c : c + 1, :] = x[:, c * T : (c + 1) * T]

    pf_copy = pltpu.make_async_copy(pf_ref, pf_hbm, small_sem.at[2])
    pf_copy.start()

    lane = lax.broadcasted_iota(jnp.int32, (T, LANES), 1)
    end = lane == jnp.where(rotor, LANES - 1, 0)

    def at_end(x, column):
        return pltpu.roll(x, jnp.where(rotor, LANES - 1 - column, (LANES - column) % LANES), 1)

    for c in range(-1, C + 1):
        sector = 0 if 0 <= c < C else (1 if c >= C else 7)
        r = (c % C) * T
        for k in range(5):
            h = at_end(ht_s[r : r + T, :], 8 * k + sector)
            one_s[k, c + 1] = near_ref[k, c + 1] - jnp.where(end, weight * h, 0.0)
    for side, wall in enumerate((hub, casing)):
        s0 = 0 if side == 0 else T - 1
        strip = ht_s[pl.ds(s0, C, stride=T), :]
        inner = Cell([one_s[k, 1 : C + 1, s0, :] for k in range(5)])
        outer = Cell([
            rows_ref[side, k] - jnp.where(end[:C], weight * at_end(strip, 40 + 8 * k), 0.0)
            for k in range(5)
        ])
        edge, _ = edge_faces(side, outer, inner, wall)
        for k in range(5):
            edge_s[side, k] = edge[k]

    def axial(c, cell):
        beside = Cell([beside_ref[k, c] for k in range(5)])
        h = [at_end(ht_s[c * T : (c + 1) * T, :], 80 + 8 * k) for k in range(5)]
        return half_faces(cell, beside, rotor, True, h)

    def edges(c):
        return [[edge_s[side, k, c : c + 1, :] for k in range(5)] for side in range(2)]

    def out_copy(k, c):
        return pltpu.make_async_copy(new_s.at[k, c], out_hbm.at[k, c], sem.at[c, k])

    def store(c, u):
        for k in range(5):
            new_s[k, c, :, pl.ds(near, LANES)] = u[k]
            new_s[k, c, :, pl.ds(far, LANES)] = far_ref[k, c]
            out_copy(k, c).start()

    sweep(
        lambda c: [one_s[k, c + 1] for k in range(5)], 0, C, axial, edges,
        lambda c: [f_ref[k, c, :, pl.ds(near, LANES)] for k in range(3)], store,
    )
    pf_copy.wait()
    for c in range(C):
        for k in range(5):
            out_copy(k, c).wait()


def pairs(count, first, wrap):
    route = []
    for low in range(first, count, 2):
        high = low + 1
        if high < count or wrap:
            route += [(low, high % count), (high % count, low)]
    return route


def snake(count, turn):
    order = [span for span in range(count)] + [2 * count - 1 - span for span in range(count)]
    n = len(order)
    return [(order[i], order[(i + turn) % n]) for i in range(n)]


def body(density, velocity, pressure, blade_force, offsets, weights):
    C, T, A = density.shape[1:]
    nc = lax.axis_size("circ")
    ns = lax.axis_size("span")
    area = C * T
    assert area == LANES and nc % 2 == 0 and A == 2 * LANES and C == 8
    rho, v, p, force = density[0], velocity[0], pressure[0], blade_force[0]

    thin = 16 * (A // LANES)
    u, force, off, wt, ta, tb = call(
        functools.partial(first_kernel, C, T),
        [(5, C, T, A), (3, C, T, A), offsets, weights, (C + thin, LANES), (C + thin, LANES)],
        [pltpu.with_memory_space_constraint(x, pltpu.HBM) for x in (rho, v, p, force, offsets, weights)],
        specs=[hbm()] * 6,
        scratch=[
            pltpu.VMEM((C, T, A), jnp.float32),
            pltpu.VMEM((3, C, T, A), jnp.float32),
            pltpu.VMEM((C, T, A), jnp.float32),
            pltpu.SemaphoreType.DMA((6,)),
        ],
    )
    sa, sb, pa, pb = call(
        functools.partial(pack_kernel, C, T),
        [(13, C, A), (13, C, A), (13, T, A), (13, T, A)],
        (u, force, ta),
        cost=pl.CostEstimate(flops=1_000_000, bytes_accessed=1_000_000, transcendentals=0),
    )
    ta = lax.ppermute(ta, ("row", "span"), snake(ns, 1))
    tb = lax.ppermute(tb, ("row", "span"), snake(ns, -1))
    ha = lax.ppermute(sa, ("row", "span"), snake(ns, 1))
    hb = lax.ppermute(sb, ("row", "span"), snake(ns, -1))
    pa = lax.ppermute(pa, "circ", pairs(nc, 0, True))
    pb = lax.ppermute(pb, "circ", pairs(nc, 1, True))

    m1, m2 = call(
        functools.partial(thin_kernel, C, T),
        [(ROWS + thin, LANES), (2 * ROWS + thin, LANES)],
        (u, force, ta, tb),
        scratch=[pltpu.VMEM((area, LANES), jnp.float32)],
    )
    planes = m1[:ROWS]
    m1 = lax.ppermute(m1, "circ", pairs(nc, 0, True))
    f32 = jnp.float32
    if nc == 4:
        (m2,) = call(fill_kernel, [m2.shape], (m1, m2), aliases={1: 0})
    (one,) = call(
        functools.partial(bulk_kernel, C),
        [(5, C, T, A)],
        (u, force, m2),
        cost=pl.CostEstimate(flops=10_000_000, bytes_accessed=4_000_000, transcendentals=0),
    )
    if nc == 4:
        got = lax.ppermute(m2, "circ", pairs(nc, 1, True))
        (ring,) = call(ring_kernel, [(nc, ROWS, LANES)], (m2, got, one))
    else:
        got = lax.ppermute(m2, "circ", pairs(nc, 1, True))
        whole = lax.all_gather(planes, "circ")
        whole = jnp.concatenate([whole, whole], 0)
        ring = lax.dynamic_slice_in_dim(whole, lax.axis_index("circ"), nc, 0)
    partner = lax.ppermute(ring, "row", [(0, 1), (1, 0)])
    copies = max(1, 8 // nc)
    rows = nc * ROWS
    ring = ring.reshape(rows, LANES)
    near, halo_rows, beside, far, pre = call(
        functools.partial(far_kernel, C, T, nc, ns),
        [(5, C + 2, T, LANES), (2, 5, C, LANES), (5, C, T, LANES), (5, C, T, LANES), (10, copies * nc, LANES)],
        (off, wt, u, force, ha, hb, pa, pb, m1, got, one, ring),
        scratch=[
            pltpu.VMEM((2, 5, 2 * C, A), f32),
            pltpu.VMEM((5, 4, T, A), f32),
            pltpu.VMEM((2, 5, C, A), f32),
            pltpu.VMEM((2, 5, C, LANES), f32),
            pltpu.VMEM((copies * rows, LANES), f32),
            pltpu.SMEM(offsets.shape, jnp.int32),
            pltpu.SMEM(weights.shape, f32),
            pltpu.SemaphoreType.DMA((2,)),
        ],
        cost=pl.CostEstimate(flops=10_000_000, bytes_accessed=4_000_000, transcendentals=0),
    )
    state, plane_flux = call(
        functools.partial(last_kernel, C, T, nc, ns),
        [(5, C, T, A), (2, 5, C, T)],
        (off, wt, force, ring, partner.reshape(rows, LANES), near, halo_rows, beside, pre, far),
        outs=[hbm(), hbm()],
        scratch=[
            pltpu.VMEM((copies * rows, LANES), f32),
            pltpu.VMEM((copies * rows, LANES), f32),
            pltpu.VMEM((LANES, LANES), f32),
            pltpu.VMEM((5, C + 2, T, LANES), f32),
            pltpu.VMEM((2, 5, C, LANES), f32),
            pltpu.VMEM((5, C, T, A), f32),
            pltpu.VMEM((2, 5, C, T), f32),
            pltpu.SMEM(offsets.shape, jnp.int32),
            pltpu.SMEM(weights.shape, f32),
            pltpu.SemaphoreType.DMA((C, 5)),
            pltpu.SemaphoreType.DMA((3,)),
        ],
        limit=16,
    )
    return state[None], plane_flux[None]


def solution(mesh):
    placed = (
        P("row", "circ", "span", None),
        P("row", None, "circ", "span", None),
        P("row", "circ", "span", None),
        P("row", None, "circ", "span", None),
        P(),
        P(),
    )
    return jax.shard_map(
        body,
        mesh=mesh,
        in_specs=placed,
        out_specs=(P("row", None, "circ", "span", None), P("row", None, None, "circ", "span")),
        check_vma=False,
    )
```
